128 devices in a mesh: space: 8 (over z, x_hi), ens: 16 (over y, x_lo, core).
Axes of the slice: x: 4 (x_hi: 2, x_lo: 2; x = x_hi * 2 + x_lo), y: 4, z: 4, core: 2. Of those that a mesh axis runs over, the one named last changes fastest.
Arguments:
- log_perm: float32 [128, 16, 64, 512], P('ens', 'space'), may hold values from -4 to 4
- storage: float32 [16, 64, 512], P('space'), may hold values from 0.5 to 2
- head_init: float32 [16, 64, 512], P('space'), may hold values from -6 to 6
- well_cells: int32 [16], replicated, may hold values from 0 to 524287
- well_rates: float32 [16], replicated, may hold values from -12 to 12
- obs_cells: int32 [32], replicated, may hold values from 0 to 524287
- obs_values: float32 [32], replicated, may hold values from -6 to 6
- noise_var: float32 [32], replicated, may hold values from 0.05 to 0.5
- step_size: float32 [1], replicated, may hold values from 0.5 to 2
- perturb: float32 [128, 32], P('ens'), may hold values from -2 to 2
Outputs:
- head_field: float32 [128, 16, 64, 512], P('ens', 'space')
- updated: float32 [128, 16, 64, 512], P('ens', 'space')
The draws below stay inside these ranges and needn't reach their ends.
All inputs are finite; a program needn't handle non-finite values.
Results may differ from the reference program's by a relative error of at most 0.00025.
Values sent between devices are 32-bit elements; how exact they have to be, the bound alone decides.
A program may use at most 192 MiB of HBM per device.

```python
import math
import jax
import jax.numpy as jnp
from jax import lax

NZ = 64
NY = 512
SWEEPS = 3
NOBS = 32
NWELL = 16
NX = 16
PARTICLES = 128
NCELLS = 524288


def plant(entries, rng, low, high):
    longest = entries.shape.index(max(entries.shape))
    spots = []
    for shift in (0, 1):
        where = [jax.random.randint(jax.random.fold_in(rng, axis), (), 0, length) for axis, length in enumerate(entries.shape)]
        where[longest] = (where[longest] + shift) % entries.shape[longest]
        spots.append(tuple(where))
    return entries.at[spots[0]].set(low).at[spots[1]].set(high)


def steps_of(rng, dims, shards, least, high):
    gain, own = 1.0, jax.random.fold_in(rng, 6)
    for position, blocks in shards:
        draws = jnp.exp(jax.random.uniform(jax.random.fold_in(own, position), (blocks,), jnp.float32, least / len(shards), high / len(shards)))
        gain = gain * jnp.repeat(draws, dims[position] // blocks).reshape([-1 if axis == position else 1 for axis in range(len(dims))])
    return gain


def normal_values(rng, dims, spread, most, pieces=(), kind=jnp.bfloat16):
    values = spread * jax.random.normal(rng, dims, jnp.float32)
    if pieces:
        values = values * steps_of(rng, dims, pieces, -0.22, 0.18)
    return jnp.clip(values, -most, most).astype(kind)


def setup_inputs(seed: int = 0) -> dict:
    splits = jax.random.split(jax.random.key(seed), 11)
    return {
        "log_perm": normal_values(splits[0], (PARTICLES, NX, NZ, NY), 1.0, 4.0, ((0, 16), (1, 8)), jnp.float32),
        "storage": jnp.clip(jnp.exp(math.log(2.0) - 1.3862944 * jax.random.uniform(splits[1], (NX, NZ, NY), jnp.float32) ** steps_of(splits[1], (NX, NZ, NY), ((0, 8),), -0.2, 0.2)), 0.5, 2.0),
        "head_init": normal_values(splits[2], (NX, NZ, NY), 1.0, 6.0, ((0, 8),), jnp.float32),
        "well_cells": plant(jax.random.randint(splits[3], (NWELL,), 0, NCELLS), jax.random.fold_in(splits[3], 1), 0, NCELLS - 1).astype(jnp.int32),
        "well_rates": normal_values(splits[4], (NWELL,), 3.0, 12.0, (), jnp.float32),
        "obs_cells": plant(jax.random.randint(splits[5], (NOBS,), 0, NCELLS), jax.random.fold_in(splits[5], 1), 0, NCELLS - 1).astype(jnp.int32),
        "obs_values": normal_values(splits[6], (NOBS,), 1.0, 6.0, (), jnp.float32),
        "noise_var": jnp.clip(jnp.exp(jax.random.uniform(splits[7], (NOBS,), jnp.float32, math.log(0.05), math.log(0.5))), 0.05, 0.5),
        "step_size": jnp.clip(jax.random.uniform(splits[8], (1,), jnp.float32, 0.5, 2.0), 0.5, 2.0),
        "perturb": normal_values(splits[9], (PARTICLES, NOBS), 0.3, 2.0, ((0, 16),), jnp.float32),
    }


OMEGA = 0.8
HIGHEST = lax.Precision.HIGHEST
DIRECTIONS = [(a, b, c) for a in (-1, 0, 1) for b in (-1, 0, 1) for c in (-1, 0, 1) if (a, b, c) != (0, 0, 0)]

def shifted(padded, a, b, c, planes, depth, across):
    return padded[..., 1 + a:1 + a + planes, 1 + b:1 + b + depth, 1 + c:1 + c + across]

def forward(log_row, storage, head_init, source):
    planes, depth, across = log_row.shape
    permeability = jnp.exp(log_row)
    padded = jnp.pad(permeability, 1)
    transmit = []
    for a, b, c in DIRECTIONS:
        factor = 2.0 ** (1 - abs(a) - abs(b) - abs(c))
        neighbour = shifted(padded, a, b, c, planes, depth, across)
        transmit.append(factor * 2.0 * permeability * neighbour / (permeability + neighbour))
    diagonal = storage + sum(transmit)
    forcing = storage * head_init + source
    head_field = head_init
    for sweep_index in range(SWEEPS):
        padded_head = jnp.pad(head_field, 1)
        gathered = sum((transmit[i] * shifted(padded_head, a, b, c, planes, depth, across) for i, (a, b, c) in enumerate(DIRECTIONS)))
        head_field = (1.0 - OMEGA) * head_field + OMEGA * (forcing + gathered) / diagonal
    return head_field

def solve_pair(factor, residual):
    first = lax.linalg.triangular_solve(factor, residual.T, left_side=True, lower=True)
    second = lax.linalg.triangular_solve(factor, first, left_side=True, lower=True, transpose_a=True)
    return second.T

def reference(log_perm, storage, head_init, well_cells, well_rates, obs_cells, obs_values, noise_var, step_size, perturb):
    source = jnp.zeros((NX * NZ * NY,), jnp.float32).at[well_cells].add(well_rates).reshape(NX, NZ, NY)

    def member(log_row):
        field = forward(log_row, storage, head_init, source)
        return (field, field.reshape(-1)[obs_cells])
    head_field, observed = lax.map(member, log_perm)
    members = log_perm.shape[0]
    deviation = observed - jnp.mean(observed, axis=0)
    covariance = jnp.dot(deviation.T, deviation, precision=HIGHEST) / (members - 1)
    system = covariance + jnp.diag(noise_var / step_size[0])
    factor = jnp.linalg.cholesky(system)
    gain_rows = solve_pair(factor, obs_values[None, :] + perturb - observed)
    flat = log_perm.reshape(members, -1)
    centred = flat - jnp.mean(flat, axis=0)
    cross = jnp.dot(deviation.T, centred, precision=HIGHEST)
    change = jnp.dot(gain_rows, cross, precision=HIGHEST) / (members - 1)
    updated = (flat + change).reshape(log_perm.shape)
    return (head_field, updated)
```

```python
import jax
import jax.numpy as jnp
from jax import lax
from jax.sharding import PartitionSpec as P

SWEEPS = 3


OMEGA = 0.8
HIGHEST = lax.Precision.HIGHEST
DIRECTIONS = [
    (a, b, c) for a in (-1, 0, 1) for b in (-1, 0, 1) for c in (-1, 0, 1) if (a, b, c) != (0, 0, 0)
]


def shifted(padded, a, b, c, planes, depth, across):
    return padded[..., 1 + a : 1 + a + planes, 1 + b : 1 + b + depth, 1 + c : 1 + c + across]


def solve_pair(factor, residual):
    first = lax.linalg.triangular_solve(factor, residual.T, left_side=True, lower=True)
    second = lax.linalg.triangular_solve(
        factor, first, left_side=True, lower=True, transpose_a=True
    )
    return second.T


def forward(log_row, storage, head_init, source):
    planes, depth, across = log_row.shape
    permeability = jnp.exp(log_row)
    padded = jnp.pad(permeability, 1)
    transmit = []
    for a, b, c in DIRECTIONS:
        factor = 2.0 ** (1 - abs(a) - abs(b) - abs(c))
        neighbour = shifted(padded, a, b, c, planes, depth, across)
        transmit.append(factor * 2.0 * permeability * neighbour / (permeability + neighbour))
    diagonal = storage + sum(transmit)
    forcing = storage * head_init + source
    head_field = head_init
    for sweep_index in range(SWEEPS):
        padded_head = jnp.pad(head_field, 1)
        gathered = sum(
            (
                transmit[i] * shifted(padded_head, a, b, c, planes, depth, across)
                for i, (a, b, c) in enumerate(DIRECTIONS)
            )
        )
        head_field = (1.0 - OMEGA) * head_field + OMEGA * (forcing + gathered) / diagonal
    return head_field


def shards(
    log_perm,
    storage,
    head_init,
    well_cells,
    well_rates,
    obs_cells,
    obs_values,
    noise_var,
    step_size,
    perturb,
):
    members, planes, depth, across = log_perm.shape
    n_space = lax.axis_size("space")
    n_ens = lax.axis_size("ens")
    cell_count = planes * depth * across
    total_members = members * n_ens
    grid_planes = planes * n_space

    whole_log = lax.all_to_all(log_perm, "space", 0, 1, tiled=True)
    whole_storage = lax.all_gather(storage, "space", axis=0, tiled=True)
    whole_head = lax.all_gather(head_init, "space", axis=0, tiled=True)
    source = (
        jnp.zeros((grid_planes * depth * across,), jnp.float32)
        .at[well_cells]
        .add(well_rates)
        .reshape(grid_planes, depth, across)
    )
    field = forward(whole_log[0], whole_storage, whole_head, source)
    picked = field.reshape(-1)[obs_cells]
    head_field = lax.all_to_all(field[None], "space", 1, 0, tiled=True)

    every_obs = lax.all_gather(picked[None], ("ens", "space"), axis=0, tiled=True)
    every_perturb = lax.all_gather(perturb, "ens", axis=0, tiled=True)
    mean_obs = jnp.mean(every_obs, axis=0)
    spread = every_obs - mean_obs
    covariance = jnp.dot(spread.T, spread, precision=HIGHEST) / (total_members - 1)
    system = covariance + jnp.diag(noise_var / step_size[0])
    factor_lower = jnp.linalg.cholesky(system)
    gain_rows = solve_pair(factor_lower, obs_values[None, :] + every_perturb - every_obs)
    mixing = jnp.dot(gain_rows, spread.T, precision=HIGHEST)

    flat = log_perm.reshape(members, cell_count)
    column = lax.all_to_all(flat, "ens", 1, 0, tiled=True)
    change = jnp.dot(mixing, column, precision=HIGHEST)
    new_column = column + change / (total_members - 1)
    updated = lax.all_to_all(new_column, "ens", 0, 1, tiled=True).reshape(log_perm.shape)
    return (head_field, updated)


def solution(mesh):
    return jax.shard_map(
        shards,
        mesh=mesh,
        in_specs=(
            P("ens", "space", None, None),
            P("space", None, None),
            P("space", None, None),
            P(),
            P(),
            P(),
            P(),
            P(),
            P(),
            P("ens", None),
        ),
        out_specs=(P("ens", "space", None, None), P("ens", "space", None, None)),
        check_vma=False,
    )
```

```python
import jax
import jax.numpy as jnp
from jax import lax
from jax.sharding import PartitionSpec as P

SWEEPS = 3


OMEGA = 0.8
HIGHEST = lax.Precision.HIGHEST
DIRECTIONS = [
    (a, b, c) for a in (-1, 0, 1) for b in (-1, 0, 1) for c in (-1, 0, 1) if (a, b, c) != (0, 0, 0)
]


def shifted(padded, a, b, c, planes, depth, across):
    return padded[..., 1 + a : 1 + a + planes, 1 + b : 1 + b + depth, 1 + c : 1 + c + across]


def solve_pair(factor, residual):
    first = lax.linalg.triangular_solve(factor, residual.T, left_side=True, lower=True)
    second = lax.linalg.triangular_solve(
        factor, first, left_side=True, lower=True, transpose_a=True
    )
    return second.T


HALF = [(a, b, c) for a, b, c in DIRECTIONS if (a, b, c) > (0, 0, 0)]


def shift_to(padded, a, b, c, planes, depth, across):
    return padded[1 + a : 1 + a + planes, 1 + b : 1 + b + depth, 1 + c : 1 + c + across]


def forward(log_row, storage, head_init, source):
    planes, depth, across = log_row.shape
    permeability = jnp.exp(log_row)
    padded = jnp.pad(permeability, 1)
    transmit = []
    for a, b, c in HALF:
        factor = 2.0 ** (1 - abs(a) - abs(b) - abs(c))
        neighbour = shift_to(padded, a, b, c, planes, depth, across)
        transmit.append(factor * 2.0 * permeability * neighbour / (permeability + neighbour))
    total = storage
    for i, (a, b, c) in enumerate(HALF):
        back = shift_to(jnp.pad(transmit[i], 1), -a, -b, -c, planes, depth, across)
        total = total + transmit[i] + back
    diagonal = total
    forcing = storage * head_init + source
    head_field = head_init
    for sweep_index in range(SWEEPS):
        padded_head = jnp.pad(head_field, 1)
        gathered = 0.0
        for i, (a, b, c) in enumerate(HALF):
            ahead = transmit[i] * shift_to(padded_head, a, b, c, planes, depth, across)
            flow = jnp.pad(transmit[i] * head_field, 1)
            gathered = gathered + ahead + shift_to(flow, -a, -b, -c, planes, depth, across)
        head_field = (1.0 - OMEGA) * head_field + OMEGA * (forcing + gathered) / diagonal
    return head_field


def shards(
    log_perm,
    storage,
    head_init,
    well_cells,
    well_rates,
    obs_cells,
    obs_values,
    noise_var,
    step_size,
    perturb,
):
    members, planes, depth, across = log_perm.shape
    n_space = lax.axis_size("space")
    n_ens = lax.axis_size("ens")
    cell_count = planes * depth * across
    total_members = members * n_ens
    grid_planes = planes * n_space

    whole_log = lax.all_to_all(log_perm, "space", 0, 1, tiled=True)
    whole_storage = lax.all_gather(storage, "space", axis=0, tiled=True)
    whole_head = lax.all_gather(head_init, "space", axis=0, tiled=True)
    source = (
        jnp.zeros((grid_planes * depth * across,), jnp.float32)
        .at[well_cells]
        .add(well_rates)
        .reshape(grid_planes, depth, across)
    )
    field = forward(whole_log[0], whole_storage, whole_head, source)
    picked = field.reshape(-1)[obs_cells]
    head_field = lax.all_to_all(field[None], "space", 1, 0, tiled=True)

    observed = lax.all_gather(picked[None], "space", axis=0, tiled=True)
    both = lax.all_gather(jnp.concatenate([observed, perturb], axis=1), "ens", axis=0, tiled=True)
    obs_count = observed.shape[1]
    every_obs, every_perturb = both[:, :obs_count], both[:, obs_count:]
    mean_obs = jnp.mean(every_obs, axis=0)
    spread = every_obs - mean_obs
    covariance = jnp.dot(spread.T, spread, precision=HIGHEST) / (total_members - 1)
    system = covariance + jnp.diag(noise_var / step_size[0])
    factor_lower = jnp.linalg.cholesky(system)
    gain_rows = solve_pair(factor_lower, obs_values[None, :] + every_perturb - every_obs)
    mixing = jnp.dot(gain_rows, spread.T, precision=HIGHEST)

    flat = log_perm.reshape(members, cell_count)
    column = lax.all_to_all(flat, "ens", 1, 0, tiled=True)
    change = jnp.dot(mixing, column, precision=HIGHEST)
    new_column = column + change / (total_members - 1)
    updated = lax.all_to_all(new_column, "ens", 0, 1, tiled=True).reshape(log_perm.shape)
    return (head_field, updated)


def solution(mesh):
    return jax.shard_map(
        shards,
        mesh=mesh,
        in_specs=(
            P("ens", "space", None, None),
            P("space", None, None),
            P("space", None, None),
            P(),
            P(),
            P(),
            P(),
            P(),
            P(),
            P("ens", None),
        ),
        out_specs=(P("ens", "space", None, None), P("ens", "space", None, None)),
        check_vma=False,
    )
```

```python
import jax
from jax.experimental import pallas as pl
from jax.experimental.pallas import tpu as pltpu
import jax.numpy as jnp
from jax import lax
from jax.sharding import PartitionSpec as P

SWEEPS = 3


OMEGA = 0.8
HIGHEST = lax.Precision.HIGHEST
DIRECTIONS = [
    (a, b, c) for a in (-1, 0, 1) for b in (-1, 0, 1) for c in (-1, 0, 1) if (a, b, c) != (0, 0, 0)
]


def shifted(padded, a, b, c, planes, depth, across):
    return padded[..., 1 + a : 1 + a + planes, 1 + b : 1 + b + depth, 1 + c : 1 + c + across]


def solve_pair(factor, residual):
    first = lax.linalg.triangular_solve(factor, residual.T, left_side=True, lower=True)
    second = lax.linalg.triangular_solve(
        factor, first, left_side=True, lower=True, transpose_a=True
    )
    return second.T


HALF = [(a, b, c) for a, b, c in DIRECTIONS if (a, b, c) > (0, 0, 0)]


def shift_plane(x, b, c):
    depth, across = x.shape
    valid = None
    if b != 0:
        x = pltpu.roll(x, (-b) % depth, 0)
        rows = lax.broadcasted_iota(jnp.int32, x.shape, 0) + b
        valid = (rows >= 0) & (rows < depth)
    if c != 0:
        x = pltpu.roll(x, (-c) % across, 1)
        cols = lax.broadcasted_iota(jnp.int32, x.shape, 1) + c
        ok = (cols >= 0) & (cols < across)
        valid = ok if valid is None else valid & ok
    if valid is None:
        return x
    return jnp.where(valid, x, 0.0)


def forward_kernel(log_ref, sto_ref, init_ref, forc_ref, out_ref, perm, trans, diag, head_a, head_b):
    planes, depth, across = log_ref.shape
    zero = jnp.zeros((depth, across), jnp.float32)
    for buf in (perm, head_a, head_b):
        buf[0] = zero
        buf[planes + 1] = zero

    def fill(p, carry):
        perm[p + 1] = jnp.exp(log_ref[p])
        head_a[p + 1] = init_ref[p]
        return carry

    lax.fori_loop(0, planes, fill, 0)

    def transmissibility(p, carry):
        own = perm[p + 1]
        for k, (a, b, c) in enumerate(HALF):
            factor = 2.0 ** (1 - abs(a) - abs(b) - abs(c))
            other = shift_plane(perm[p + 1 + a], b, c)
            trans[k, p] = factor * 2.0 * own * other / (own + other)
        return carry

    lax.fori_loop(0, planes, transmissibility, 0)

    def diagonal(p, carry):
        total = sto_ref[p]
        for k, (a, b, c) in enumerate(HALF):
            back = p - a
            inside = (back >= 0) & (back < planes)
            behind = shift_plane(trans[k, jnp.clip(back, 0, planes - 1)], -b, -c)
            total = total + trans[k, p] + jnp.where(inside, behind, 0.0)
        diag[p] = total
        return carry

    lax.fori_loop(0, planes, diagonal, 0)

    def sweep(source, target, padded_target):
        def body(p, carry):
            gathered = None
            for k, (a, b, c) in enumerate(HALF):
                ahead = trans[k, p] * shift_plane(source[p + 1 + a], b, c)
                back = jnp.clip(p - a, 0, planes - 1)
                flow = shift_plane(trans[k, back] * source[p + 1 - a], -b, -c)
                term = ahead + flow
                gathered = term if gathered is None else gathered + term
            value = (1.0 - OMEGA) * source[p + 1] + OMEGA * (forc_ref[p] + gathered) / diag[p]
            if padded_target:
                target[p + 1] = value
            else:
                target[p] = value
            return carry

        lax.fori_loop(0, planes, body, 0)

    sweep(head_a, head_b, True)
    sweep(head_b, head_a, True)
    sweep(head_a, out_ref, False)


def forward_pallas(log_row, storage, head_init, forcing):
    planes, depth, across = log_row.shape
    vmem = pl.BlockSpec(memory_space=pltpu.VMEM)
    return pl.pallas_call(
        forward_kernel,
        out_shape=jax.ShapeDtypeStruct((planes, depth, across), jnp.float32),
        in_specs=[vmem] * 4,
        out_specs=vmem,
        scratch_shapes=[
            pltpu.VMEM((planes + 2, depth, across), jnp.float32),
            pltpu.VMEM((len(HALF), planes, depth, across), jnp.float32),
            pltpu.VMEM((planes, depth, across), jnp.float32),
            pltpu.VMEM((planes + 2, depth, across), jnp.float32),
            pltpu.VMEM((planes + 2, depth, across), jnp.float32),
        ],
        compiler_params=pltpu.CompilerParams(vmem_limit_bytes=66 * 1024 * 1024),
    )(log_row, storage, head_init, forcing)


def shards(
    log_perm,
    storage,
    head_init,
    well_cells,
    well_rates,
    obs_cells,
    obs_values,
    noise_var,
    step_size,
    perturb,
):
    members, planes, depth, across = log_perm.shape
    n_space = lax.axis_size("space")
    n_ens = lax.axis_size("ens")
    cell_count = planes * depth * across
    total_members = members * n_ens
    grid_planes = planes * n_space

    whole_log = lax.all_to_all(log_perm, "space", 0, 1, tiled=True)
    whole_storage = lax.all_gather(storage, "space", axis=0, tiled=True)
    whole_head = lax.all_gather(head_init, "space", axis=0, tiled=True)
    source = (
        jnp.zeros((grid_planes * depth * across,), jnp.float32)
        .at[well_cells]
        .add(well_rates)
        .reshape(grid_planes, depth, across)
    )
    forcing = whole_storage * whole_head + source
    field = forward_pallas(whole_log[0], whole_storage, whole_head, forcing)
    picked = field.reshape(-1)[obs_cells]
    head_field = lax.all_to_all(field[None], "space", 1, 0, tiled=True)

    observed = lax.all_gather(picked[None], "space", axis=0, tiled=True)
    both = lax.all_gather(jnp.concatenate([observed, perturb], axis=1), "ens", axis=0, tiled=True)
    obs_count = observed.shape[1]
    every_obs, every_perturb = both[:, :obs_count], both[:, obs_count:]
    mean_obs = jnp.mean(every_obs, axis=0)
    spread = every_obs - mean_obs
    covariance = jnp.dot(spread.T, spread, precision=HIGHEST) / (total_members - 1)
    system = covariance + jnp.diag(noise_var / step_size[0])
    factor_lower = jnp.linalg.cholesky(system)
    gain_rows = solve_pair(factor_lower, obs_values[None, :] + every_perturb - every_obs)
    mixing = jnp.dot(gain_rows, spread.T, precision=HIGHEST)

    flat = log_perm.reshape(members, cell_count)
    column = lax.all_to_all(flat, "ens", 1, 0, tiled=True)
    change = jnp.dot(mixing, column, precision=HIGHEST)
    new_column = column + change / (total_members - 1)
    updated = lax.all_to_all(new_column, "ens", 0, 1, tiled=True).reshape(log_perm.shape)
    return (head_field, updated)


def solution(mesh):
    return jax.shard_map(
        shards,
        mesh=mesh,
        in_specs=(
            P("ens", "space", None, None),
            P("space", None, None),
            P("space", None, None),
            P(),
            P(),
            P(),
            P(),
            P(),
            P(),
            P("ens", None),
        ),
        out_specs=(P("ens", "space", None, None), P("ens", "space", None, None)),
        check_vma=False,
    )
```

```python
import jax
from jax.experimental import pallas as pl
from jax.experimental.pallas import tpu as pltpu
import jax.numpy as jnp
from jax import lax
from jax.sharding import PartitionSpec as P

SWEEPS = 3


OMEGA = 0.8
HIGHEST = lax.Precision.HIGHEST
DIRECTIONS = [
    (a, b, c) for a in (-1, 0, 1) for b in (-1, 0, 1) for c in (-1, 0, 1) if (a, b, c) != (0, 0, 0)
]


def shifted(padded, a, b, c, planes, depth, across):
    return padded[..., 1 + a : 1 + a + planes, 1 + b : 1 + b + depth, 1 + c : 1 + c + across]


def solve_pair(factor, residual):
    first = lax.linalg.triangular_solve(factor, residual.T, left_side=True, lower=True)
    second = lax.linalg.triangular_solve(
        factor, first, left_side=True, lower=True, transpose_a=True
    )
    return second.T


HALF = [(a, b, c) for a, b, c in DIRECTIONS if (a, b, c) > (0, 0, 0)]


def shift_plane(x, b, c):
    depth, across = x.shape
    valid = None
    if b != 0:
        x = pltpu.roll(x, (-b) % depth, 0)
        rows = lax.broadcasted_iota(jnp.int32, x.shape, 0) + b
        valid = (rows >= 0) & (rows < depth)
    if c != 0:
        x = pltpu.roll(x, (-c) % across, 1)
        cols = lax.broadcasted_iota(jnp.int32, x.shape, 1) + c
        ok = (cols >= 0) & (cols < across)
        valid = ok if valid is None else valid & ok
    if valid is None:
        return x
    return jnp.where(valid, x, 0.0)


def forward_kernel(log_ref, sto_ref, init_ref, forc_ref, out_ref, perm, trans, diag, head_a, head_b):
    planes, depth, across = log_ref.shape
    zero = jnp.zeros((depth, across), jnp.float32)
    for buf in (perm, head_a, head_b):
        buf[0] = zero
        buf[planes + 1] = zero

    def fill(p, carry):
        perm[p + 1] = jnp.exp(log_ref[p])
        head_a[p + 1] = init_ref[p]
        return carry

    lax.fori_loop(0, planes, fill, 0)

    def transmissibility(p, carry):
        own = perm[p + 1]
        for k, (a, b, c) in enumerate(HALF):
            factor = 2.0 ** (1 - abs(a) - abs(b) - abs(c))
            other = shift_plane(perm[p + 1 + a], b, c)
            trans[k, p] = factor * 2.0 * own * other / (own + other)
        return carry

    lax.fori_loop(0, planes, transmissibility, 0)

    def diagonal(p, carry):
        total = sto_ref[p]
        for k, (a, b, c) in enumerate(HALF):
            back = p - a
            inside = (back >= 0) & (back < planes)
            behind = shift_plane(trans[k, jnp.clip(back, 0, planes - 1)], -b, -c)
            total = total + trans[k, p] + jnp.where(inside, behind, 0.0)
        diag[p] = total
        return carry

    lax.fori_loop(0, planes, diagonal, 0)

    def sweep(source, target, padded_target):
        def body(p, carry):
            gathered = None
            for k, (a, b, c) in enumerate(HALF):
                ahead = trans[k, p] * shift_plane(source[p + 1 + a], b, c)
                back = jnp.clip(p - a, 0, planes - 1)
                flow = shift_plane(trans[k, back] * source[p + 1 - a], -b, -c)
                term = ahead + flow
                gathered = term if gathered is None else gathered + term
            value = (1.0 - OMEGA) * source[p + 1] + OMEGA * (forc_ref[p] + gathered) / diag[p]
            if padded_target:
                target[p + 1] = value
            else:
                target[p] = value
            return carry

        lax.fori_loop(0, planes, body, 0)

    sweep(head_a, head_b, True)
    sweep(head_b, head_a, True)
    sweep(head_a, out_ref, False)


def forward_pallas(log_row, storage, head_init, forcing):
    planes, depth, across = log_row.shape
    vmem = pl.BlockSpec(memory_space=pltpu.VMEM)
    return pl.pallas_call(
        forward_kernel,
        out_shape=jax.ShapeDtypeStruct((planes, depth, across), jnp.float32),
        in_specs=[vmem] * 4,
        out_specs=vmem,
        scratch_shapes=[
            pltpu.VMEM((planes + 2, depth, across), jnp.float32),
            pltpu.VMEM((len(HALF), planes, depth, across), jnp.float32),
            pltpu.VMEM((planes, depth, across), jnp.float32),
            pltpu.VMEM((planes + 2, depth, across), jnp.float32),
            pltpu.VMEM((planes + 2, depth, across), jnp.float32),
        ],
        compiler_params=pltpu.CompilerParams(vmem_limit_bytes=66 * 1024 * 1024),
    )(log_row, storage, head_init, forcing)


def shards(
    log_perm,
    storage,
    head_init,
    well_cells,
    well_rates,
    obs_cells,
    obs_values,
    noise_var,
    step_size,
    perturb,
):
    members, planes, depth, across = log_perm.shape
    n_space = lax.axis_size("space")
    n_ens = lax.axis_size("ens")
    cell_count = planes * depth * across
    total_members = members * n_ens
    grid_planes = planes * n_space

    whole_log = lax.all_to_all(log_perm, "space", 0, 1, tiled=True)
    core = lax.axis_index("ens") % 2
    mine = lax.all_gather(jnp.where(core == 0, storage, head_init), "space", axis=0, tiled=True)
    pairs = [(e, e ^ 1) for e in range(n_ens)]
    other = lax.ppermute(mine, "ens", pairs)
    whole_storage = jnp.where(core == 0, mine, other)
    whole_head = jnp.where(core == 0, other, mine)
    source = (
        jnp.zeros((grid_planes * depth * across,), jnp.float32)
        .at[well_cells]
        .add(well_rates)
        .reshape(grid_planes, depth, across)
    )
    forcing = whole_storage * whole_head + source
    field = forward_pallas(whole_log[0], whole_storage, whole_head, forcing)
    picked = field.reshape(-1)[obs_cells]
    head_field = lax.all_to_all(field[None], "space", 1, 0, tiled=True)

    observed = lax.all_gather(picked[None], "space", axis=0, tiled=True)
    both = lax.all_gather(jnp.concatenate([observed, perturb], axis=1), "ens", axis=0, tiled=True)
    obs_count = observed.shape[1]
    every_obs, every_perturb = both[:, :obs_count], both[:, obs_count:]
    mean_obs = jnp.mean(every_obs, axis=0)
    spread = every_obs - mean_obs
    covariance = jnp.dot(spread.T, spread, precision=HIGHEST) / (total_members - 1)
    system = covariance + jnp.diag(noise_var / step_size[0])
    factor_lower = jnp.linalg.cholesky(system)
    gain_rows = solve_pair(factor_lower, obs_values[None, :] + every_perturb - every_obs)
    mixing = jnp.dot(gain_rows, spread.T, precision=HIGHEST)

    flat = log_perm.reshape(members, cell_count)
    column = lax.all_to_all(flat, "ens", 1, 0, tiled=True)
    change = jnp.dot(mixing, column, precision=HIGHEST)
    new_column = column + change / (total_members - 1)
    updated = lax.all_to_all(new_column, "ens", 0, 1, tiled=True).reshape(log_perm.shape)
    return (head_field, updated)


def solution(mesh):
    return jax.shard_map(
        shards,
        mesh=mesh,
        in_specs=(
            P("ens", "space", None, None),
            P("space", None, None),
            P("space", None, None),
            P(),
            P(),
            P(),
            P(),
            P(),
            P(),
            P("ens", None),
        ),
        out_specs=(P("ens", "space", None, None), P("ens", "space", None, None)),
        check_vma=False,
    )
```

```python
import jax
from jax.experimental import pallas as pl
from jax.experimental.pallas import tpu as pltpu
import jax.numpy as jnp
from jax import lax
from jax.sharding import PartitionSpec as P

SWEEPS = 3


OMEGA = 0.8
HIGHEST = lax.Precision.HIGHEST
DIRECTIONS = [
    (a, b, c) for a in (-1, 0, 1) for b in (-1, 0, 1) for c in (-1, 0, 1) if (a, b, c) != (0, 0, 0)
]


def shifted(padded, a, b, c, planes, depth, across):
    return padded[..., 1 + a : 1 + a + planes, 1 + b : 1 + b + depth, 1 + c : 1 + c + across]


def solve_pair(factor, residual):
    first = lax.linalg.triangular_solve(factor, residual.T, left_side=True, lower=True)
    second = lax.linalg.triangular_solve(
        factor, first, left_side=True, lower=True, transpose_a=True
    )
    return second.T


HALF = [(a, b, c) for a, b, c in DIRECTIONS if (a, b, c) > (0, 0, 0)]


def shift_plane(x, b, c):
    depth, across = x.shape
    valid = None
    if b != 0:
        x = pltpu.roll(x, (-b) % depth, 0)
        rows = lax.broadcasted_iota(jnp.int32, x.shape, 0) + b
        valid = (rows >= 0) & (rows < depth)
    if c != 0:
        x = pltpu.roll(x, (-c) % across, 1)
        cols = lax.broadcasted_iota(jnp.int32, x.shape, 1) + c
        ok = (cols >= 0) & (cols < across)
        valid = ok if valid is None else valid & ok
    if valid is None:
        return x
    return jnp.where(valid, x, 0.0)


def forward_kernel(
    log_ref, sto_ref, init_ref, forc_ref, field_ref, out_ref,
    perm, trans, diag, head_a, head_b, send_sems, recv_sems, local_sem,
):
    planes, depth, across = log_ref.shape
    slabs = out_ref.shape[0]
    thick = planes // slabs
    me = lax.axis_index("space")
    ens = lax.axis_index("ens")
    mesh_id = pl.DeviceIdType.MESH

    barrier = pltpu.get_barrier_semaphore()
    for s in range(slabs):
        @pl.when(me != s)
        def _():
            pl.semaphore_signal(barrier, 1, device_id=(s, ens), device_id_type=mesh_id)

    zero = jnp.zeros((depth, across), jnp.float32)
    for buf in (perm, head_a, head_b):
        buf[0] = zero
        buf[planes + 1] = zero

    def fill(p, carry):
        perm[p + 1] = jnp.exp(log_ref[p])
        head_a[p + 1] = init_ref[p]
        return carry

    lax.fori_loop(0, planes, fill, 0)

    def transmissibility(p, carry):
        own = perm[p + 1]
        for k, (a, b, c) in enumerate(HALF):
            factor = 2.0 ** (1 - abs(a) - abs(b) - abs(c))
            other = shift_plane(perm[p + 1 + a], b, c)
            trans[k, p] = factor * 2.0 * own * other / (own + other)
        return carry

    lax.fori_loop(0, planes, transmissibility, 0)

    def diagonal(p, carry):
        total = sto_ref[p]
        for k, (a, b, c) in enumerate(HALF):
            back = p - a
            inside = (back >= 0) & (back < planes)
            behind = shift_plane(trans[k, jnp.clip(back, 0, planes - 1)], -b, -c)
            total = total + trans[k, p] + jnp.where(inside, behind, 0.0)
        diag[p] = total
        return carry

    lax.fori_loop(0, planes, diagonal, 0)

    def relax(source, p):
        gathered = None
        for k, (a, b, c) in enumerate(HALF):
            ahead = trans[k, p] * shift_plane(source[p + 1 + a], b, c)
            back = jnp.clip(p - a, 0, planes - 1)
            flow = shift_plane(trans[k, back] * source[p + 1 - a], -b, -c)
            term = ahead + flow
            gathered = term if gathered is None else gathered + term
        return (1.0 - OMEGA) * source[p + 1] + OMEGA * (forc_ref[p] + gathered) / diag[p]

    def sweep(source, target):
        def body(p, carry):
            target[p + 1] = relax(source, p)
            return carry

        lax.fori_loop(0, planes, body, 0)

    sweep(head_a, head_b)
    sweep(head_b, head_a)
    pl.semaphore_wait(barrier, slabs - 1)

    def send(s):
        return pltpu.make_async_remote_copy(
            src_ref=field_ref.at[pl.ds(s * thick, thick)],
            dst_ref=out_ref.at[me],
            send_sem=send_sems.at[s],
            recv_sem=recv_sems.at[me],
            device_id=(s, ens),
            device_id_type=mesh_id,
        )

    def keep():
        return pltpu.make_async_copy(
            field_ref.at[pl.ds(me * thick, thick)], out_ref.at[me], local_sem
        )

    def last(s, carry):
        for j in range(thick):
            p = s * thick + j
            field_ref[p] = relax(head_a, p)

        @pl.when(s != me)
        def _():
            send(s).start()

        @pl.when(s == me)
        def _():
            keep().start()

        return carry

    lax.fori_loop(0, slabs, last, 0)
    keep().wait()
    for s in range(slabs):
        @pl.when(me != s)
        def _():
            send(s).wait_send()
            pltpu.make_async_remote_copy(
                src_ref=field_ref.at[pl.ds(s * thick, thick)],
                dst_ref=out_ref.at[s],
                send_sem=send_sems.at[s],
                recv_sem=recv_sems.at[s],
                device_id=(s, ens),
                device_id_type=mesh_id,
            ).wait_recv()


def forward_pallas(log_row, storage, head_init, forcing, slabs):
    planes, depth, across = log_row.shape
    vmem = pl.BlockSpec(memory_space=pltpu.VMEM)
    return pl.pallas_call(
        forward_kernel,
        out_shape=(
            jax.ShapeDtypeStruct((planes, depth, across), jnp.float32),
            jax.ShapeDtypeStruct((slabs, planes // slabs, depth, across), jnp.float32),
        ),
        in_specs=[vmem] * 4,
        out_specs=(vmem, pl.BlockSpec(memory_space=pl.ANY)),
        scratch_shapes=[
            pltpu.VMEM((planes + 2, depth, across), jnp.float32),
            pltpu.VMEM((len(HALF), planes, depth, across), jnp.float32),
            pltpu.VMEM((planes, depth, across), jnp.float32),
            pltpu.VMEM((planes + 2, depth, across), jnp.float32),
            pltpu.VMEM((planes + 2, depth, across), jnp.float32),
            pltpu.SemaphoreType.DMA((slabs,)),
            pltpu.SemaphoreType.DMA((slabs,)),
            pltpu.SemaphoreType.DMA,
        ],
        compiler_params=pltpu.CompilerParams(
            vmem_limit_bytes=66 * 1024 * 1024, collective_id=0, has_side_effects=True
        ),
    )(log_row, storage, head_init, forcing)


def shards(
    log_perm,
    storage,
    head_init,
    well_cells,
    well_rates,
    obs_cells,
    obs_values,
    noise_var,
    step_size,
    perturb,
):
    members, planes, depth, across = log_perm.shape
    n_space = lax.axis_size("space")
    n_ens = lax.axis_size("ens")
    cell_count = planes * depth * across
    total_members = members * n_ens
    grid_planes = planes * n_space

    whole_log = lax.all_to_all(log_perm, "space", 0, 1, tiled=True)
    core = lax.axis_index("ens") % 2
    mine = lax.all_gather(jnp.where(core == 0, storage, head_init), "space", axis=0, tiled=True)
    pairs = [(e, e ^ 1) for e in range(n_ens)]
    other = lax.ppermute(mine, "ens", pairs)
    whole_storage = jnp.where(core == 0, mine, other)
    whole_head = jnp.where(core == 0, other, mine)
    source = (
        jnp.zeros((grid_planes * depth * across,), jnp.float32)
        .at[well_cells]
        .add(well_rates)
        .reshape(grid_planes, depth, across)
    )
    forcing = whole_storage * whole_head + source
    field, head_field = forward_pallas(whole_log[0], whole_storage, whole_head, forcing, n_space)
    picked = field.reshape(-1)[obs_cells]

    observed = lax.all_gather(picked[None], "space", axis=0, tiled=True)
    both = lax.all_gather(jnp.concatenate([observed, perturb], axis=1), "ens", axis=0, tiled=True)
    obs_count = observed.shape[1]
    every_obs, every_perturb = both[:, :obs_count], both[:, obs_count:]
    mean_obs = jnp.mean(every_obs, axis=0)
    spread = every_obs - mean_obs
    covariance = jnp.dot(spread.T, spread, precision=HIGHEST) / (total_members - 1)
    system = covariance + jnp.diag(noise_var / step_size[0])
    factor_lower = jnp.linalg.cholesky(system)
    gain_rows = solve_pair(factor_lower, obs_values[None, :] + every_perturb - every_obs)
    mixing = jnp.dot(gain_rows, spread.T, precision=HIGHEST)

    flat = log_perm.reshape(members, cell_count)
    column = lax.all_to_all(flat, "ens", 1, 0, tiled=True)
    change = jnp.dot(mixing, column, precision=HIGHEST)
    new_column = column + change / (total_members - 1)
    updated = lax.all_to_all(new_column, "ens", 0, 1, tiled=True).reshape(log_perm.shape)
    return (head_field, updated)


def solution(mesh):
    return jax.shard_map(
        shards,
        mesh=mesh,
        in_specs=(
            P("ens", "space", None, None),
            P("space", None, None),
            P("space", None, None),
            P(),
            P(),
            P(),
            P(),
            P(),
            P(),
            P("ens", None),
        ),
        out_specs=(P("ens", "space", None, None), P("ens", "space", None, None)),
        check_vma=False,
    )
```

```python
import jax
from jax.experimental import pallas as pl
from jax.experimental.pallas import tpu as pltpu
import jax.numpy as jnp
from jax import lax
from jax.sharding import PartitionSpec as P

SWEEPS = 3


OMEGA = 0.8
HIGHEST = lax.Precision.HIGHEST
DIRECTIONS = [
    (a, b, c) for a in (-1, 0, 1) for b in (-1, 0, 1) for c in (-1, 0, 1) if (a, b, c) != (0, 0, 0)
]


def shifted(padded, a, b, c, planes, depth, across):
    return padded[..., 1 + a : 1 + a + planes, 1 + b : 1 + b + depth, 1 + c : 1 + c + across]


def solve_pair(factor, residual):
    first = lax.linalg.triangular_solve(factor, residual.T, left_side=True, lower=True)
    second = lax.linalg.triangular_solve(
        factor, first, left_side=True, lower=True, transpose_a=True
    )
    return second.T


HALF = [(a, b, c) for a, b, c in DIRECTIONS if (a, b, c) > (0, 0, 0)]


def shift_plane(x, b, c):
    depth, across = x.shape
    valid = None
    if b != 0:
        x = pltpu.roll(x, (-b) % depth, 0)
        rows = lax.broadcasted_iota(jnp.int32, x.shape, 0) + b
        valid = (rows >= 0) & (rows < depth)
    if c != 0:
        x = pltpu.roll(x, (-c) % across, 1)
        cols = lax.broadcasted_iota(jnp.int32, x.shape, 1) + c
        ok = (cols >= 0) & (cols < across)
        valid = ok if valid is None else valid & ok
    if valid is None:
        return x
    return jnp.where(valid, x, 0.0)


def forward_kernel(log_ref, sto_ref, init_ref, forc_ref, out_ref, perm, trans, diag, head_a, head_b):
    planes, depth, across = log_ref.shape
    zero = jnp.zeros((depth, across), jnp.float32)
    for buf in (perm, head_a, head_b):
        buf[0] = zero
        buf[planes + 1] = zero

    def fill(p, carry):
        perm[p + 1] = jnp.exp(log_ref[p])
        head_a[p + 1] = init_ref[p]
        return carry

    lax.fori_loop(0, planes, fill, 0)

    def transmissibility(p, carry):
        own = perm[p + 1]
        for k, (a, b, c) in enumerate(HALF):
            factor = 2.0 ** (1 - abs(a) - abs(b) - abs(c))
            other = shift_plane(perm[p + 1 + a], b, c)
            trans[k, p] = factor * 2.0 * own * other / (own + other)
        return carry

    lax.fori_loop(0, planes, transmissibility, 0)

    def diagonal(p, carry):
        total = sto_ref[p]
        for k, (a, b, c) in enumerate(HALF):
            back = p - a
            inside = (back >= 0) & (back < planes)
            behind = shift_plane(trans[k, jnp.clip(back, 0, planes - 1)], -b, -c)
            total = total + trans[k, p] + jnp.where(inside, behind, 0.0)
        diag[p] = total
        return carry

    lax.fori_loop(0, planes, diagonal, 0)

    def sweep(source, target, padded_target):
        def body(p, carry):
            gathered = None
            for k, (a, b, c) in enumerate(HALF):
                ahead = trans[k, p] * shift_plane(source[p + 1 + a], b, c)
                back = jnp.clip(p - a, 0, planes - 1)
                flow = shift_plane(trans[k, back] * source[p + 1 - a], -b, -c)
                term = ahead + flow
                gathered = term if gathered is None else gathered + term
            value = (1.0 - OMEGA) * source[p + 1] + OMEGA * (forc_ref[p] + gathered) / diag[p]
            if padded_target:
                target[p + 1] = value
            else:
                target[p] = value
            return carry

        lax.fori_loop(0, planes, body, 0)

    sweep(head_a, head_b, True)
    sweep(head_b, head_a, True)
    sweep(head_a, out_ref, False)


def forward_pallas(log_row, storage, head_init, forcing):
    planes, depth, across = log_row.shape
    vmem = pl.BlockSpec(memory_space=pltpu.VMEM)
    return pl.pallas_call(
        forward_kernel,
        out_shape=jax.ShapeDtypeStruct((planes, depth, across), jnp.float32),
        in_specs=[vmem] * 4,
        out_specs=vmem,
        scratch_shapes=[
            pltpu.VMEM((planes + 2, depth, across), jnp.float32),
            pltpu.VMEM((len(HALF), planes, depth, across), jnp.float32),
            pltpu.VMEM((planes, depth, across), jnp.float32),
            pltpu.VMEM((planes + 2, depth, across), jnp.float32),
            pltpu.VMEM((planes + 2, depth, across), jnp.float32),
        ],
        compiler_params=pltpu.CompilerParams(vmem_limit_bytes=66 * 1024 * 1024),
    )(log_row, storage, head_init, forcing)


def gather_kernel(row_ref, out_ref, landing, send_sem, recv_sem):
    total = landing.shape[0]
    n_space = lax.axis_size("space")
    me_s = lax.axis_index("space")
    me_e = lax.axis_index("ens")
    mine = me_e * n_space + me_s
    mesh_id = pl.DeviceIdType.MESH

    barrier = pltpu.get_barrier_semaphore()

    def greet(i, carry):
        @pl.when(i != mine)
        def _():
            pl.semaphore_signal(
                barrier, 1, device_id=(i % n_space, i // n_space), device_id_type=mesh_id
            )

        return carry

    lax.fori_loop(0, total, greet, 0)
    pl.semaphore_wait(barrier, total - 1)

    def send(i, carry):
        @pl.when(i != mine)
        def _():
            pltpu.make_async_remote_copy(
                src_ref=row_ref,
                dst_ref=landing.at[pl.ds(mine, 1)],
                send_sem=send_sem,
                recv_sem=recv_sem,
                device_id=(i % n_space, i // n_space),
                device_id_type=mesh_id,
            ).start()

        return carry

    lax.fori_loop(0, total, send, 0)
    landing[pl.ds(mine, 1)] = row_ref[...]
    partner = (mine + 1) % total
    everything = pltpu.make_async_remote_copy(
        src_ref=landing.at[pl.ds(0, total - 1)],
        dst_ref=landing.at[pl.ds(1, total - 1)],
        send_sem=send_sem,
        recv_sem=recv_sem,
        device_id=(partner % n_space, partner // n_space),
        device_id_type=mesh_id,
    )
    everything.wait_send()
    everything.wait_recv()
    out_ref[...] = landing[...]


def gather_rows(row, total):
    vmem = pl.BlockSpec(memory_space=pltpu.VMEM)
    return pl.pallas_call(
        gather_kernel,
        out_shape=jax.ShapeDtypeStruct((total,) + row.shape[1:], jnp.float32),
        in_specs=[vmem],
        out_specs=vmem,
        scratch_shapes=[
            pltpu.VMEM((total,) + row.shape[1:], jnp.float32),
            pltpu.SemaphoreType.DMA,
            pltpu.SemaphoreType.DMA,
        ],
        compiler_params=pltpu.CompilerParams(collective_id=1, has_side_effects=True),
    )(row)


def shards(
    log_perm,
    storage,
    head_init,
    well_cells,
    well_rates,
    obs_cells,
    obs_values,
    noise_var,
    step_size,
    perturb,
):
    members, planes, depth, across = log_perm.shape
    n_space = lax.axis_size("space")
    n_ens = lax.axis_size("ens")
    cell_count = planes * depth * across
    total_members = members * n_ens
    grid_planes = planes * n_space

    whole_log = lax.all_to_all(log_perm, "space", 0, 1, tiled=True)
    core = lax.axis_index("ens") % 2
    mine = lax.all_gather(jnp.where(core == 0, storage, head_init), "space", axis=0, tiled=True)
    pairs = [(e, e ^ 1) for e in range(n_ens)]
    other = lax.ppermute(mine, "ens", pairs)
    whole_storage = jnp.where(core == 0, mine, other)
    whole_head = jnp.where(core == 0, other, mine)
    source = (
        jnp.zeros((grid_planes * depth * across,), jnp.float32)
        .at[well_cells]
        .add(well_rates)
        .reshape(grid_planes, depth, across)
    )
    forcing = whole_storage * whole_head + source
    field = forward_pallas(whole_log[0], whole_storage, whole_head, forcing)
    picked = field.reshape(-1)[obs_cells]
    head_field = lax.all_to_all(field[None], "space", 1, 0, tiled=True)

    obs_count = picked.shape[0]
    own_perturb = lax.dynamic_index_in_dim(perturb, lax.axis_index("space"), 0, keepdims=False)
    row = jnp.zeros((1, 8, 128), jnp.float32)
    row = row.at[0, 0, :obs_count].set(picked).at[0, 0, obs_count : 2 * obs_count].set(own_perturb)
    rows = gather_rows(row, total_members)
    every_obs = rows[:, 0, :obs_count]
    every_perturb = rows[:, 0, obs_count : 2 * obs_count]
    mean_obs = jnp.mean(every_obs, axis=0)
    spread = every_obs - mean_obs
    covariance = jnp.dot(spread.T, spread, precision=HIGHEST) / (total_members - 1)
    system = covariance + jnp.diag(noise_var / step_size[0])
    factor_lower = jnp.linalg.cholesky(system)
    gain_rows = solve_pair(factor_lower, obs_values[None, :] + every_perturb - every_obs)
    mixing = jnp.dot(gain_rows, spread.T, precision=HIGHEST)

    flat = log_perm.reshape(members, cell_count)
    column = lax.all_to_all(flat, "ens", 1, 0, tiled=True)
    change = jnp.dot(mixing, column, precision=HIGHEST)
    new_column = column + change / (total_members - 1)
    updated = lax.all_to_all(new_column, "ens", 0, 1, tiled=True).reshape(log_perm.shape)
    return (head_field, updated)


def solution(mesh):
    return jax.shard_map(
        shards,
        mesh=mesh,
        in_specs=(
            P("ens", "space", None, None),
            P("space", None, None),
            P("space", None, None),
            P(),
            P(),
            P(),
            P(),
            P(),
            P(),
            P("ens", None),
        ),
        out_specs=(P("ens", "space", None, None), P("ens", "space", None, None)),
        check_vma=False,
    )
```

```python
import jax
from jax.experimental import pallas as pl
from jax.experimental.pallas import tpu as pltpu
import jax.numpy as jnp
from jax import lax
from jax.sharding import PartitionSpec as P

SWEEPS = 3


OMEGA = 0.8
HIGHEST = lax.Precision.HIGHEST
DIRECTIONS = [
    (a, b, c) for a in (-1, 0, 1) for b in (-1, 0, 1) for c in (-1, 0, 1) if (a, b, c) != (0, 0, 0)
]


def shifted(padded, a, b, c, planes, depth, across):
    return padded[..., 1 + a : 1 + a + planes, 1 + b : 1 + b + depth, 1 + c : 1 + c + across]


def solve_pair(factor, residual):
    first = lax.linalg.triangular_solve(factor, residual.T, left_side=True, lower=True)
    second = lax.linalg.triangular_solve(
        factor, first, left_side=True, lower=True, transpose_a=True
    )
    return second.T


HALF = [(a, b, c) for a, b, c in DIRECTIONS if (a, b, c) > (0, 0, 0)]


def shift_plane(x, b, c):
    depth, across = x.shape
    valid = None
    if b != 0:
        x = pltpu.roll(x, (-b) % depth, 0)
        rows = lax.broadcasted_iota(jnp.int32, x.shape, 0) + b
        valid = (rows >= 0) & (rows < depth)
    if c != 0:
        x = pltpu.roll(x, (-c) % across, 1)
        cols = lax.broadcasted_iota(jnp.int32, x.shape, 1) + c
        ok = (cols >= 0) & (cols < across)
        valid = ok if valid is None else valid & ok
    if valid is None:
        return x
    return jnp.where(valid, x, 0.0)


def forward_kernel(log_ref, sto_ref, init_ref, forc_ref, out_ref, perm, trans, diag, head_a, head_b):
    planes, depth, across = log_ref.shape
    zero = jnp.zeros((depth, across), jnp.float32)
    for buf in (perm, head_a, head_b):
        buf[0] = zero
        buf[planes + 1] = zero

    def fill(p, carry):
        perm[p + 1] = jnp.exp(log_ref[p])
        head_a[p + 1] = init_ref[p]
        return carry

    lax.fori_loop(0, planes, fill, 0)

    def transmissibility(p, carry):
        own = perm[p + 1]
        for k, (a, b, c) in enumerate(HALF):
            factor = 2.0 ** (1 - abs(a) - abs(b) - abs(c))
            other = shift_plane(perm[p + 1 + a], b, c)
            trans[k, p] = factor * 2.0 * own * other / (own + other)
        return carry

    lax.fori_loop(0, planes, transmissibility, 0)

    def diagonal(p, carry):
        total = sto_ref[p]
        for k, (a, b, c) in enumerate(HALF):
            back = p - a
            inside = (back >= 0) & (back < planes)
            behind = shift_plane(trans[k, jnp.clip(back, 0, planes - 1)], -b, -c)
            total = total + trans[k, p] + jnp.where(inside, behind, 0.0)
        diag[p] = total
        return carry

    lax.fori_loop(0, planes, diagonal, 0)

    def sweep(source, target, padded_target):
        def body(p, carry):
            gathered = None
            for k, (a, b, c) in enumerate(HALF):
                ahead = trans[k, p] * shift_plane(source[p + 1 + a], b, c)
                back = jnp.clip(p - a, 0, planes - 1)
                flow = shift_plane(trans[k, back] * source[p + 1 - a], -b, -c)
                term = ahead + flow
                gathered = term if gathered is None else gathered + term
            value = (1.0 - OMEGA) * source[p + 1] + OMEGA * (forc_ref[p] + gathered) / diag[p]
            if padded_target:
                target[p + 1] = value
            else:
                target[p] = value
            return carry

        lax.fori_loop(0, planes, body, 0)

    sweep(head_a, head_b, True)
    sweep(head_b, head_a, True)
    sweep(head_a, out_ref, False)


def forward_pallas(log_row, storage, head_init, forcing):
    planes, depth, across = log_row.shape
    vmem = pl.BlockSpec(memory_space=pltpu.VMEM)
    return pl.pallas_call(
        forward_kernel,
        out_shape=jax.ShapeDtypeStruct((planes, depth, across), jnp.float32),
        in_specs=[vmem] * 4,
        out_specs=vmem,
        scratch_shapes=[
            pltpu.VMEM((planes + 2, depth, across), jnp.float32),
            pltpu.VMEM((len(HALF), planes, depth, across), jnp.float32),
            pltpu.VMEM((planes, depth, across), jnp.float32),
            pltpu.VMEM((planes + 2, depth, across), jnp.float32),
            pltpu.VMEM((planes + 2, depth, across), jnp.float32),
        ],
        compiler_params=pltpu.CompilerParams(vmem_limit_bytes=66 * 1024 * 1024),
    )(log_row, storage, head_init, forcing)


def gather_kernel(row_ref, out_ref, landing, send_sem, recv_sem):
    total = landing.shape[0]
    n_space = lax.axis_size("space")
    me_s = lax.axis_index("space")
    me_e = lax.axis_index("ens")
    mine = me_e * n_space + me_s
    mesh_id = pl.DeviceIdType.MESH

    barrier = pltpu.get_barrier_semaphore()

    def greet(i, carry):
        @pl.when(i != mine)
        def _():
            pl.semaphore_signal(
                barrier, 1, device_id=(i % n_space, i // n_space), device_id_type=mesh_id
            )

        return carry

    lax.fori_loop(0, total, greet, 0)
    pl.semaphore_wait(barrier, total - 1)

    def send(i, carry):
        @pl.when(i != mine)
        def _():
            pltpu.make_async_remote_copy(
                src_ref=row_ref,
                dst_ref=landing.at[pl.ds(mine, 1)],
                send_sem=send_sem,
                recv_sem=recv_sem,
                device_id=(i % n_space, i // n_space),
                device_id_type=mesh_id,
            ).start()

        return carry

    lax.fori_loop(0, total, send, 0)
    landing[pl.ds(mine, 1)] = row_ref[...]
    partner = (mine + 1) % total
    everything = pltpu.make_async_remote_copy(
        src_ref=landing.at[pl.ds(0, total - 1)],
        dst_ref=landing.at[pl.ds(1, total - 1)],
        send_sem=send_sem,
        recv_sem=recv_sem,
        device_id=(partner % n_space, partner // n_space),
        device_id_type=mesh_id,
    )
    everything.wait_send()
    everything.wait_recv()
    out_ref[...] = landing[...]


def gather_rows(row, total):
    vmem = pl.BlockSpec(memory_space=pltpu.VMEM)
    return pl.pallas_call(
        gather_kernel,
        out_shape=jax.ShapeDtypeStruct((total,) + row.shape[1:], jnp.float32),
        in_specs=[vmem],
        out_specs=vmem,
        scratch_shapes=[
            pltpu.VMEM((total,) + row.shape[1:], jnp.float32),
            pltpu.SemaphoreType.DMA,
            pltpu.SemaphoreType.DMA,
        ],
        compiler_params=pltpu.CompilerParams(collective_id=1, has_side_effects=True),
    )(row)


def return_kernel(field_ref, column_ref, head_out, update_out,
                  head_send, head_recv, upd_send, upd_recv, local_sems):
    slabs, thick = head_out.shape[0], head_out.shape[1]
    groups = update_out.shape[1] // column_ref.shape[1]
    rows = column_ref.shape[1]
    members = update_out.shape[0]
    me_s = lax.axis_index("space")
    me_e = lax.axis_index("ens")
    mesh_id = pl.DeviceIdType.MESH

    barrier = pltpu.get_barrier_semaphore()
    for s in range(slabs):
        @pl.when(me_s != s)
        def _():
            pl.semaphore_signal(barrier, 1, device_id=(s, me_e), device_id_type=mesh_id)
    for e in range(groups):
        @pl.when(me_e != e)
        def _():
            pl.semaphore_signal(barrier, 1, device_id=(me_s, e), device_id_type=mesh_id)
    pl.semaphore_wait(barrier, slabs - 1 + groups - 1)

    def upd_copy(e, source_e):
        return pltpu.make_async_remote_copy(
            src_ref=column_ref.at[pl.ds(e * members, members)],
            dst_ref=update_out.at[:, pl.ds(source_e * rows, rows)],
            send_sem=upd_send.at[e],
            recv_sem=upd_recv.at[source_e],
            device_id=(me_s, e),
            device_id_type=mesh_id,
        )

    def head_copy(s, source_s):
        return pltpu.make_async_remote_copy(
            src_ref=field_ref.at[pl.ds(s * thick, thick)],
            dst_ref=head_out.at[source_s],
            send_sem=head_send.at[s],
            recv_sem=head_recv.at[source_s],
            device_id=(s, me_e),
            device_id_type=mesh_id,
        )

    keep_upd = pltpu.make_async_copy(
        column_ref.at[pl.ds(me_e * members, members)],
        update_out.at[:, pl.ds(me_e * rows, rows)],
        local_sems.at[0],
    )
    keep_head = pltpu.make_async_copy(
        field_ref.at[pl.ds(me_s * thick, thick)], head_out.at[me_s], local_sems.at[1]
    )
    for e in range(groups):
        @pl.when(me_e != e)
        def _():
            upd_copy(e, me_e).start()
    for s in range(slabs):
        @pl.when(me_s != s)
        def _():
            head_copy(s, me_s).start()
    keep_upd.start()
    keep_head.start()
    keep_upd.wait()
    keep_head.wait()
    for e in range(groups):
        @pl.when(me_e != e)
        def _():
            upd_copy(e, me_e).wait_send()
            upd_copy(e, e).wait_recv()
    for s in range(slabs):
        @pl.when(me_s != s)
        def _():
            head_copy(s, me_s).wait_send()
            head_copy(s, s).wait_recv()


def send_back(field, column, slabs):
    planes, depth, across = field.shape
    total, rows, _ = column.shape
    groups = planes * depth // rows // slabs
    members = total // groups
    anywhere = pl.BlockSpec(memory_space=pl.ANY)
    return pl.pallas_call(
        return_kernel,
        out_shape=(
            jax.ShapeDtypeStruct((slabs, planes // slabs, depth, across), jnp.float32),
            jax.ShapeDtypeStruct((members, groups * rows, across), jnp.float32),
        ),
        in_specs=[anywhere, anywhere],
        out_specs=(anywhere, anywhere),
        scratch_shapes=[
            pltpu.SemaphoreType.DMA((slabs,)),
            pltpu.SemaphoreType.DMA((slabs,)),
            pltpu.SemaphoreType.DMA((groups,)),
            pltpu.SemaphoreType.DMA((groups,)),
            pltpu.SemaphoreType.DMA((2,)),
        ],
        compiler_params=pltpu.CompilerParams(collective_id=2, has_side_effects=True),
    )(field, column)


def shards(
    log_perm,
    storage,
    head_init,
    well_cells,
    well_rates,
    obs_cells,
    obs_values,
    noise_var,
    step_size,
    perturb,
):
    members, planes, depth, across = log_perm.shape
    n_space = lax.axis_size("space")
    n_ens = lax.axis_size("ens")
    cell_count = planes * depth * across
    total_members = members * n_ens
    grid_planes = planes * n_space

    whole_log = lax.all_to_all(log_perm, "space", 0, 1, tiled=True)
    core = lax.axis_index("ens") % 2
    mine = lax.all_gather(jnp.where(core == 0, storage, head_init), "space", axis=0, tiled=True)
    pairs = [(e, e ^ 1) for e in range(n_ens)]
    other = lax.ppermute(mine, "ens", pairs)
    whole_storage = jnp.where(core == 0, mine, other)
    whole_head = jnp.where(core == 0, other, mine)
    source = (
        jnp.zeros((grid_planes * depth * across,), jnp.float32)
        .at[well_cells]
        .add(well_rates)
        .reshape(grid_planes, depth, across)
    )
    forcing = whole_storage * whole_head + source
    field = forward_pallas(whole_log[0], whole_storage, whole_head, forcing)
    picked = field.reshape(-1)[obs_cells]

    obs_count = picked.shape[0]
    own_perturb = lax.dynamic_index_in_dim(perturb, lax.axis_index("space"), 0, keepdims=False)
    row = jnp.zeros((1, 8, 128), jnp.float32)
    row = row.at[0, 0, :obs_count].set(picked).at[0, 0, obs_count : 2 * obs_count].set(own_perturb)
    rows = gather_rows(row, total_members)
    every_obs = rows[:, 0, :obs_count]
    every_perturb = rows[:, 0, obs_count : 2 * obs_count]
    mean_obs = jnp.mean(every_obs, axis=0)
    spread = every_obs - mean_obs
    covariance = jnp.dot(spread.T, spread, precision=HIGHEST) / (total_members - 1)
    system = covariance + jnp.diag(noise_var / step_size[0])
    factor_lower = jnp.linalg.cholesky(system)
    gain_rows = solve_pair(factor_lower, obs_values[None, :] + every_perturb - every_obs)
    mixing = jnp.dot(gain_rows, spread.T, precision=HIGHEST)

    slab_rows = planes * depth
    band = lax.all_to_all(log_perm.reshape(members, slab_rows, across), "ens", 1, 0, tiled=True)
    change = jnp.einsum("jk,kry->jry", mixing, band, precision=HIGHEST)
    new_band = band + change / (total_members - 1)
    head_field, updated = send_back(field, new_band, n_space)
    updated = updated.reshape(log_perm.shape)
    return (head_field, updated)


def solution(mesh):
    return jax.shard_map(
        shards,
        mesh=mesh,
        in_specs=(
            P("ens", "space", None, None),
            P("space", None, None),
            P("space", None, None),
            P(),
            P(),
            P(),
            P(),
            P(),
            P(),
            P("ens", None),
        ),
        out_specs=(P("ens", "space", None, None), P("ens", "space", None, None)),
        check_vma=False,
    )
```

```python
import jax
from jax.experimental import pallas as pl
from jax.experimental.pallas import tpu as pltpu
import jax.numpy as jnp
from jax import lax
from jax.sharding import PartitionSpec as P

SWEEPS = 3


OMEGA = 0.8
HIGHEST = lax.Precision.HIGHEST
DIRECTIONS = [
    (a, b, c) for a in (-1, 0, 1) for b in (-1, 0, 1) for c in (-1, 0, 1) if (a, b, c) != (0, 0, 0)
]


def shifted(padded, a, b, c, planes, depth, across):
    return padded[..., 1 + a : 1 + a + planes, 1 + b : 1 + b + depth, 1 + c : 1 + c + across]


def solve_pair(factor, residual):
    first = lax.linalg.triangular_solve(factor, residual.T, left_side=True, lower=True)
    second = lax.linalg.triangular_solve(
        factor, first, left_side=True, lower=True, transpose_a=True
    )
    return second.T


HALF = [(a, b, c) for a, b, c in DIRECTIONS if (a, b, c) > (0, 0, 0)]


def shift_plane(x, b, c):
    depth, across = x.shape
    valid = None
    if b != 0:
        x = pltpu.roll(x, (-b) % depth, 0)
        rows = lax.broadcasted_iota(jnp.int32, x.shape, 0) + b
        valid = (rows >= 0) & (rows < depth)
    if c != 0:
        x = pltpu.roll(x, (-c) % across, 1)
        cols = lax.broadcasted_iota(jnp.int32, x.shape, 1) + c
        ok = (cols >= 0) & (cols < across)
        valid = ok if valid is None else valid & ok
    if valid is None:
        return x
    return jnp.where(valid, x, 0.0)


def forward_kernel(log_ref, sto_ref, init_ref, forc_ref, out_ref, perm, trans, diag, head_a, head_b):
    planes, depth, across = log_ref.shape
    zero = jnp.zeros((depth, across), jnp.float32)
    for buf in (perm, head_a, head_b):
        buf[0] = zero
        buf[planes + 1] = zero

    def fill(p, carry):
        perm[p + 1] = jnp.exp(log_ref[p])
        head_a[p + 1] = init_ref[p]
        return carry

    lax.fori_loop(0, planes, fill, 0)

    def transmissibility(p, carry):
        own = perm[p + 1]
        for k, (a, b, c) in enumerate(HALF):
            factor = 2.0 ** (1 - abs(a) - abs(b) - abs(c))
            other = shift_plane(perm[p + 1 + a], b, c)
            trans[k, p] = factor * 2.0 * own * other / (own + other)
        return carry

    lax.fori_loop(0, planes, transmissibility, 0)

    def diagonal(p, carry):
        total = sto_ref[p]
        for k, (a, b, c) in enumerate(HALF):
            back = p - a
            inside = (back >= 0) & (back < planes)
            behind = shift_plane(trans[k, jnp.clip(back, 0, planes - 1)], -b, -c)
            total = total + trans[k, p] + jnp.where(inside, behind, 0.0)
        diag[p] = total
        return carry

    lax.fori_loop(0, planes, diagonal, 0)

    def sweep(source, target, padded_target):
        def body(p, carry):
            gathered = None
            for k, (a, b, c) in enumerate(HALF):
                ahead = trans[k, p] * shift_plane(source[p + 1 + a], b, c)
                back = jnp.clip(p - a, 0, planes - 1)
                flow = shift_plane(trans[k, back] * source[p + 1 - a], -b, -c)
                term = ahead + flow
                gathered = term if gathered is None else gathered + term
            value = (1.0 - OMEGA) * source[p + 1] + OMEGA * (forc_ref[p] + gathered) / diag[p]
            if padded_target:
                target[p + 1] = value
            else:
                target[p] = value
            return carry

        lax.fori_loop(0, planes, body, 0)

    sweep(head_a, head_b, True)
    sweep(head_b, head_a, True)
    sweep(head_a, out_ref, False)


def forward_pallas(log_row, storage, head_init, forcing):
    planes, depth, across = log_row.shape
    vmem = pl.BlockSpec(memory_space=pltpu.VMEM)
    return pl.pallas_call(
        forward_kernel,
        out_shape=jax.ShapeDtypeStruct((planes, depth, across), jnp.float32),
        in_specs=[vmem] * 4,
        out_specs=vmem,
        scratch_shapes=[
            pltpu.VMEM((planes + 2, depth, across), jnp.float32),
            pltpu.VMEM((len(HALF), planes, depth, across), jnp.float32),
            pltpu.VMEM((planes, depth, across), jnp.float32),
            pltpu.VMEM((planes + 2, depth, across), jnp.float32),
            pltpu.VMEM((planes + 2, depth, across), jnp.float32),
        ],
        compiler_params=pltpu.CompilerParams(vmem_limit_bytes=66 * 1024 * 1024),
    )(log_row, storage, head_init, forcing)


def gather_kernel(row_ref, out_ref, landing, send_sem, recv_sem):
    total = landing.shape[0]
    n_space = lax.axis_size("space")
    me_s = lax.axis_index("space")
    me_e = lax.axis_index("ens")
    mine = me_e * n_space + me_s
    mesh_id = pl.DeviceIdType.MESH

    barrier = pltpu.get_barrier_semaphore()

    def greet(i, carry):
        @pl.when(i != mine)
        def _():
            pl.semaphore_signal(
                barrier, 1, device_id=(i % n_space, i // n_space), device_id_type=mesh_id
            )

        return carry

    lax.fori_loop(0, total, greet, 0)
    pl.semaphore_wait(barrier, total - 1)

    def send(i, carry):
        @pl.when(i != mine)
        def _():
            pltpu.make_async_remote_copy(
                src_ref=row_ref,
                dst_ref=landing.at[pl.ds(mine, 1)],
                send_sem=send_sem,
                recv_sem=recv_sem,
                device_id=(i % n_space, i // n_space),
                device_id_type=mesh_id,
            ).start()

        return carry

    lax.fori_loop(0, total, send, 0)
    landing[pl.ds(mine, 1)] = row_ref[...]
    partner = (mine + 1) % total
    everything = pltpu.make_async_remote_copy(
        src_ref=landing.at[pl.ds(0, total - 1)],
        dst_ref=landing.at[pl.ds(1, total - 1)],
        send_sem=send_sem,
        recv_sem=recv_sem,
        device_id=(partner % n_space, partner // n_space),
        device_id_type=mesh_id,
    )
    everything.wait_send()
    everything.wait_recv()
    out_ref[...] = landing[...]


def gather_rows(row, total):
    vmem = pl.BlockSpec(memory_space=pltpu.VMEM)
    return pl.pallas_call(
        gather_kernel,
        out_shape=jax.ShapeDtypeStruct((total,) + row.shape[1:], jnp.float32),
        in_specs=[vmem],
        out_specs=vmem,
        scratch_shapes=[
            pltpu.VMEM((total,) + row.shape[1:], jnp.float32),
            pltpu.SemaphoreType.DMA,
            pltpu.SemaphoreType.DMA,
        ],
        compiler_params=pltpu.CompilerParams(collective_id=1, has_side_effects=True),
    )(row)


def return_kernel(column_ref, update_out, upd_send, upd_recv, local_sem):
    groups = update_out.shape[1] // column_ref.shape[1]
    rows = column_ref.shape[1]
    members = update_out.shape[0]
    me_s = lax.axis_index("space")
    me_e = lax.axis_index("ens")
    mesh_id = pl.DeviceIdType.MESH

    barrier = pltpu.get_barrier_semaphore()
    for e in range(groups):
        @pl.when(me_e != e)
        def _():
            pl.semaphore_signal(barrier, 1, device_id=(me_s, e), device_id_type=mesh_id)
    pl.semaphore_wait(barrier, groups - 1)

    def upd_copy(e, source_e):
        return pltpu.make_async_remote_copy(
            src_ref=column_ref.at[pl.ds(e * members, members)],
            dst_ref=update_out.at[:, pl.ds(source_e * rows, rows)],
            send_sem=upd_send.at[e],
            recv_sem=upd_recv.at[source_e],
            device_id=(me_s, e),
            device_id_type=mesh_id,
        )

    keep_upd = pltpu.make_async_copy(
        column_ref.at[pl.ds(me_e * members, members)],
        update_out.at[:, pl.ds(me_e * rows, rows)],
        local_sem,
    )
    for e in range(groups):
        @pl.when(me_e != e)
        def _():
            upd_copy(e, me_e).start()
    keep_upd.start()
    keep_upd.wait()
    for e in range(groups):
        @pl.when(me_e != e)
        def _():
            upd_copy(e, me_e).wait_send()
            upd_copy(e, e).wait_recv()


def send_back(column, slab_rows):
    total, rows, across = column.shape
    groups = slab_rows // rows
    members = total // groups
    anywhere = pl.BlockSpec(memory_space=pl.ANY)
    return pl.pallas_call(
        return_kernel,
        out_shape=jax.ShapeDtypeStruct((members, slab_rows, across), jnp.float32),
        in_specs=[anywhere],
        out_specs=anywhere,
        scratch_shapes=[
            pltpu.SemaphoreType.DMA((groups,)),
            pltpu.SemaphoreType.DMA((groups,)),
            pltpu.SemaphoreType.DMA,
        ],
        compiler_params=pltpu.CompilerParams(collective_id=2, has_side_effects=True),
    )(column)


def shards(
    log_perm,
    storage,
    head_init,
    well_cells,
    well_rates,
    obs_cells,
    obs_values,
    noise_var,
    step_size,
    perturb,
):
    members, planes, depth, across = log_perm.shape
    n_space = lax.axis_size("space")
    n_ens = lax.axis_size("ens")
    cell_count = planes * depth * across
    total_members = members * n_ens
    grid_planes = planes * n_space

    whole_log = lax.all_to_all(log_perm, "space", 0, 1, tiled=True)
    core = lax.axis_index("ens") % 2
    mine = lax.all_gather(jnp.where(core == 0, storage, head_init), "space", axis=0, tiled=True)
    pairs = [(e, e ^ 1) for e in range(n_ens)]
    other = lax.ppermute(mine, "ens", pairs)
    whole_storage = jnp.where(core == 0, mine, other)
    whole_head = jnp.where(core == 0, other, mine)
    source = (
        jnp.zeros((grid_planes * depth * across,), jnp.float32)
        .at[well_cells]
        .add(well_rates)
        .reshape(grid_planes, depth, across)
    )
    forcing = whole_storage * whole_head + source
    field = forward_pallas(whole_log[0], whole_storage, whole_head, forcing)
    picked = field.reshape(-1)[obs_cells]
    head_field = lax.all_to_all(field[None], "space", 1, 0, tiled=True)

    obs_count = picked.shape[0]
    own_perturb = lax.dynamic_index_in_dim(perturb, lax.axis_index("space"), 0, keepdims=False)
    row = jnp.zeros((1, 8, 128), jnp.float32)
    row = row.at[0, 0, :obs_count].set(picked).at[0, 0, obs_count : 2 * obs_count].set(own_perturb)
    rows = gather_rows(row, total_members)
    every_obs = rows[:, 0, :obs_count]
    every_perturb = rows[:, 0, obs_count : 2 * obs_count]
    mean_obs = jnp.mean(every_obs, axis=0)
    spread = every_obs - mean_obs
    covariance = jnp.dot(spread.T, spread, precision=HIGHEST) / (total_members - 1)
    system = covariance + jnp.diag(noise_var / step_size[0])
    factor_lower = jnp.linalg.cholesky(system)
    gain_rows = solve_pair(factor_lower, obs_values[None, :] + every_perturb - every_obs)
    mixing = jnp.dot(gain_rows, spread.T, precision=HIGHEST)

    slab_rows = planes * depth
    band = lax.all_to_all(log_perm.reshape(members, slab_rows, across), "ens", 1, 0, tiled=True)
    change = jnp.einsum("jk,kry->jry", mixing, band, precision=HIGHEST)
    new_band = band + change / (total_members - 1)
    updated = send_back(new_band, slab_rows)
    updated = updated.reshape(log_perm.shape)
    return (head_field, updated)


def solution(mesh):
    return jax.shard_map(
        shards,
        mesh=mesh,
        in_specs=(
            P("ens", "space", None, None),
            P("space", None, None),
            P("space", None, None),
            P(),
            P(),
            P(),
            P(),
            P(),
            P(),
            P("ens", None),
        ),
        out_specs=(P("ens", "space", None, None), P("ens", "space", None, None)),
        check_vma=False,
    )
```

```python
import jax
from jax.experimental import pallas as pl
from jax.experimental.pallas import tpu as pltpu
import jax.numpy as jnp
from jax import lax
from jax.sharding import PartitionSpec as P

SWEEPS = 3


OMEGA = 0.8
HIGHEST = lax.Precision.HIGHEST
DIRECTIONS = [
    (a, b, c) for a in (-1, 0, 1) for b in (-1, 0, 1) for c in (-1, 0, 1) if (a, b, c) != (0, 0, 0)
]


def shifted(padded, a, b, c, planes, depth, across):
    return padded[..., 1 + a : 1 + a + planes, 1 + b : 1 + b + depth, 1 + c : 1 + c + across]


def solve_pair(factor, residual):
    first = lax.linalg.triangular_solve(factor, residual.T, left_side=True, lower=True)
    second = lax.linalg.triangular_solve(
        factor, first, left_side=True, lower=True, transpose_a=True
    )
    return second.T


HALF = [(a, b, c) for a, b, c in DIRECTIONS if (a, b, c) > (0, 0, 0)]


def shift_plane(x, b, c):
    depth, across = x.shape
    valid = None
    if b != 0:
        x = pltpu.roll(x, (-b) % depth, 0)
        rows = lax.broadcasted_iota(jnp.int32, x.shape, 0) + b
        valid = (rows >= 0) & (rows < depth)
    if c != 0:
        x = pltpu.roll(x, (-c) % across, 1)
        cols = lax.broadcasted_iota(jnp.int32, x.shape, 1) + c
        ok = (cols >= 0) & (cols < across)
        valid = ok if valid is None else valid & ok
    if valid is None:
        return x
    return jnp.where(valid, x, 0.0)


def forward_kernel(log_ref, sto_ref, init_ref, forc_ref, out_ref, perm, trans, diag, head_a, head_b):
    planes, depth, across = log_ref.shape
    zero = jnp.zeros((depth, across), jnp.float32)
    for buf in (perm, head_a, head_b):
        buf[0] = zero
        buf[planes + 1] = zero

    def fill(p, carry):
        perm[p + 1] = jnp.exp(log_ref[p])
        head_a[p + 1] = init_ref[p]
        return carry

    lax.fori_loop(0, planes, fill, 0)

    def transmissibility(p, carry):
        own = perm[p + 1]
        for k, (a, b, c) in enumerate(HALF):
            factor = 2.0 ** (1 - abs(a) - abs(b) - abs(c))
            other = shift_plane(perm[p + 1 + a], b, c)
            trans[k, p] = factor * 2.0 * own * other / (own + other)
        return carry

    lax.fori_loop(0, planes, transmissibility, 0)

    def diagonal(p, carry):
        total = sto_ref[p]
        for k, (a, b, c) in enumerate(HALF):
            back = p - a
            inside = (back >= 0) & (back < planes)
            behind = shift_plane(trans[k, jnp.clip(back, 0, planes - 1)], -b, -c)
            total = total + trans[k, p] + jnp.where(inside, behind, 0.0)
        diag[p] = total
        return carry

    lax.fori_loop(0, planes, diagonal, 0)

    def sweep(source, target, padded_target):
        def body(p, carry):
            gathered = None
            for k, (a, b, c) in enumerate(HALF):
                ahead = trans[k, p] * shift_plane(source[p + 1 + a], b, c)
                back = jnp.clip(p - a, 0, planes - 1)
                flow = shift_plane(trans[k, back] * source[p + 1 - a], -b, -c)
                term = ahead + flow
                gathered = term if gathered is None else gathered + term
            value = (1.0 - OMEGA) * source[p + 1] + OMEGA * (forc_ref[p] + gathered) / diag[p]
            if padded_target:
                target[p + 1] = value
            else:
                target[p] = value
            return carry

        lax.fori_loop(0, planes, body, 0)

    sweep(head_a, head_b, True)
    sweep(head_b, head_a, True)
    sweep(head_a, out_ref, False)


def forward_pallas(log_row, storage, head_init, forcing):
    planes, depth, across = log_row.shape
    vmem = pl.BlockSpec(memory_space=pltpu.VMEM)
    return pl.pallas_call(
        forward_kernel,
        out_shape=jax.ShapeDtypeStruct((planes, depth, across), jnp.float32),
        in_specs=[vmem] * 4,
        out_specs=vmem,
        scratch_shapes=[
            pltpu.VMEM((planes + 2, depth, across), jnp.float32),
            pltpu.VMEM((len(HALF), planes, depth, across), jnp.float32),
            pltpu.VMEM((planes, depth, across), jnp.float32),
            pltpu.VMEM((planes + 2, depth, across), jnp.float32),
            pltpu.VMEM((planes + 2, depth, across), jnp.float32),
        ],
        compiler_params=pltpu.CompilerParams(vmem_limit_bytes=66 * 1024 * 1024),
    )(log_row, storage, head_init, forcing)


def gather_kernel(row_ref, out_ref, landing, send_sem, recv_sem):
    total = landing.shape[0]
    n_space = lax.axis_size("space")
    me_s = lax.axis_index("space")
    me_e = lax.axis_index("ens")
    mine = me_e * n_space + me_s
    mesh_id = pl.DeviceIdType.MESH

    barrier = pltpu.get_barrier_semaphore()

    def greet(i, carry):
        @pl.when(i != mine)
        def _():
            pl.semaphore_signal(
                barrier, 1, device_id=(i % n_space, i // n_space), device_id_type=mesh_id
            )

        return carry

    lax.fori_loop(0, total, greet, 0)
    pl.semaphore_wait(barrier, total - 1)

    def send(i, carry):
        @pl.when(i != mine)
        def _():
            pltpu.make_async_remote_copy(
                src_ref=row_ref,
                dst_ref=landing.at[pl.ds(mine, 1)],
                send_sem=send_sem,
                recv_sem=recv_sem,
                device_id=(i % n_space, i // n_space),
                device_id_type=mesh_id,
            ).start()

        return carry

    lax.fori_loop(0, total, send, 0)
    landing[pl.ds(mine, 1)] = row_ref[...]
    partner = (mine + 1) % total
    everything = pltpu.make_async_remote_copy(
        src_ref=landing.at[pl.ds(0, total - 1)],
        dst_ref=landing.at[pl.ds(1, total - 1)],
        send_sem=send_sem,
        recv_sem=recv_sem,
        device_id=(partner % n_space, partner // n_space),
        device_id_type=mesh_id,
    )
    everything.wait_send()
    everything.wait_recv()
    out_ref[...] = landing[...]


def gather_rows(row, total):
    vmem = pl.BlockSpec(memory_space=pltpu.VMEM)
    return pl.pallas_call(
        gather_kernel,
        out_shape=jax.ShapeDtypeStruct((total,) + row.shape[1:], jnp.float32),
        in_specs=[vmem],
        out_specs=vmem,
        scratch_shapes=[
            pltpu.VMEM((total,) + row.shape[1:], jnp.float32),
            pltpu.SemaphoreType.DMA,
            pltpu.SemaphoreType.DMA,
        ],
        compiler_params=pltpu.CompilerParams(collective_id=1, has_side_effects=True),
    )(row)


def return_kernel(column_ref, update_out, upd_send, upd_recv, local_sem):
    groups = update_out.shape[1] // column_ref.shape[1]
    rows = column_ref.shape[1]
    members = update_out.shape[0]
    me_s = lax.axis_index("space")
    me_e = lax.axis_index("ens")
    mesh_id = pl.DeviceIdType.MESH

    barrier = pltpu.get_barrier_semaphore()
    for e in range(groups):
        @pl.when(me_e != e)
        def _():
            pl.semaphore_signal(barrier, 1, device_id=(me_s, e), device_id_type=mesh_id)
    pl.semaphore_wait(barrier, groups - 1)

    def upd_copy(e, source_e):
        return pltpu.make_async_remote_copy(
            src_ref=column_ref.at[pl.ds(e * members, members)],
            dst_ref=update_out.at[:, pl.ds(source_e * rows, rows)],
            send_sem=upd_send.at[e],
            recv_sem=upd_recv.at[source_e],
            device_id=(me_s, e),
            device_id_type=mesh_id,
        )

    keep_upd = pltpu.make_async_copy(
        column_ref.at[pl.ds(me_e * members, members)],
        update_out.at[:, pl.ds(me_e * rows, rows)],
        local_sem,
    )
    for e in range(groups):
        @pl.when(me_e != e)
        def _():
            upd_copy(e, me_e).start()
    keep_upd.start()
    keep_upd.wait()
    for e in range(groups):
        @pl.when(me_e != e)
        def _():
            upd_copy(e, me_e).wait_send()
            upd_copy(e, e).wait_recv()


def send_back(column, slab_rows):
    total, rows, across = column.shape
    groups = slab_rows // rows
    members = total // groups
    anywhere = pl.BlockSpec(memory_space=pl.ANY)
    return pl.pallas_call(
        return_kernel,
        out_shape=jax.ShapeDtypeStruct((members, slab_rows, across), jnp.float32),
        in_specs=[anywhere],
        out_specs=anywhere,
        scratch_shapes=[
            pltpu.SemaphoreType.DMA((groups,)),
            pltpu.SemaphoreType.DMA((groups,)),
            pltpu.SemaphoreType.DMA,
        ],
        compiler_params=pltpu.CompilerParams(collective_id=2, has_side_effects=True),
    )(column)


def shards(
    log_perm,
    storage,
    head_init,
    well_cells,
    well_rates,
    obs_cells,
    obs_values,
    noise_var,
    step_size,
    perturb,
):
    members, planes, depth, across = log_perm.shape
    n_space = lax.axis_size("space")
    n_ens = lax.axis_size("ens")
    cell_count = planes * depth * across
    total_members = members * n_ens
    grid_planes = planes * n_space

    whole_log = lax.all_to_all(log_perm, "space", 0, 1, tiled=True)
    slab_rows = planes * depth
    by_rows, whole_log = lax.optimization_barrier(
        (log_perm.reshape(members, slab_rows, across), whole_log)
    )
    core = lax.axis_index("ens") % 2
    mine = lax.all_gather(jnp.where(core == 0, storage, head_init), "space", axis=0, tiled=True)
    pairs = [(e, e ^ 1) for e in range(n_ens)]
    other = lax.ppermute(mine, "ens", pairs)
    whole_storage = jnp.where(core == 0, mine, other)
    whole_head = jnp.where(core == 0, other, mine)
    source = (
        jnp.zeros((grid_planes * depth * across,), jnp.float32)
        .at[well_cells]
        .add(well_rates)
        .reshape(grid_planes, depth, across)
    )
    forcing = whole_storage * whole_head + source
    field = forward_pallas(whole_log[0], whole_storage, whole_head, forcing)
    picked = field.reshape(-1)[obs_cells]
    head_field = lax.all_to_all(field[None], "space", 1, 0, tiled=True)

    obs_count = picked.shape[0]
    own_perturb = lax.dynamic_index_in_dim(perturb, lax.axis_index("space"), 0, keepdims=False)
    row = jnp.zeros((1, 8, 128), jnp.float32)
    row = row.at[0, 0, :obs_count].set(picked).at[0, 0, obs_count : 2 * obs_count].set(own_perturb)
    rows = gather_rows(row, total_members)
    every_obs = rows[:, 0, :obs_count]
    every_perturb = rows[:, 0, obs_count : 2 * obs_count]
    mean_obs = jnp.mean(every_obs, axis=0)
    spread = every_obs - mean_obs
    covariance = jnp.dot(spread.T, spread, precision=HIGHEST) / (total_members - 1)
    system = covariance + jnp.diag(noise_var / step_size[0])
    factor_lower = jnp.linalg.cholesky(system)
    gain_rows = solve_pair(factor_lower, obs_values[None, :] + every_perturb - every_obs)
    mixing = jnp.dot(gain_rows, spread.T, precision=HIGHEST)

    band = lax.all_to_all(by_rows, "ens", 1, 0, tiled=True)
    change = jnp.einsum("jk,kry->jry", mixing, band, precision=HIGHEST)
    new_band = band + change / (total_members - 1)
    updated = send_back(new_band, slab_rows)
    updated = updated.reshape(log_perm.shape)
    return (head_field, updated)


def solution(mesh):
    return jax.shard_map(
        shards,
        mesh=mesh,
        in_specs=(
            P("ens", "space", None, None),
            P("space", None, None),
            P("space", None, None),
            P(),
            P(),
            P(),
            P(),
            P(),
            P(),
            P("ens", None),
        ),
        out_specs=(P("ens", "space", None, None), P("ens", "space", None, None)),
        check_vma=False,
    )
```

```python
import jax
from jax.experimental import pallas as pl
from jax.experimental.pallas import tpu as pltpu
import jax.numpy as jnp
from jax import lax
from jax.sharding import PartitionSpec as P

SWEEPS = 3


OMEGA = 0.8
HIGHEST = lax.Precision.HIGHEST
DIRECTIONS = [
    (a, b, c) for a in (-1, 0, 1) for b in (-1, 0, 1) for c in (-1, 0, 1) if (a, b, c) != (0, 0, 0)
]


def shifted(padded, a, b, c, planes, depth, across):
    return padded[..., 1 + a : 1 + a + planes, 1 + b : 1 + b + depth, 1 + c : 1 + c + across]


def solve_pair(factor, residual):
    first = lax.linalg.triangular_solve(factor, residual.T, left_side=True, lower=True)
    second = lax.linalg.triangular_solve(
        factor, first, left_side=True, lower=True, transpose_a=True
    )
    return second.T


HALF = [(a, b, c) for a, b, c in DIRECTIONS if (a, b, c) > (0, 0, 0)]


def shift_plane(x, b, c):
    depth, across = x.shape
    valid = None
    if b != 0:
        x = pltpu.roll(x, (-b) % depth, 0)
        rows = lax.broadcasted_iota(jnp.int32, x.shape, 0) + b
        valid = (rows >= 0) & (rows < depth)
    if c != 0:
        x = pltpu.roll(x, (-c) % across, 1)
        cols = lax.broadcasted_iota(jnp.int32, x.shape, 1) + c
        ok = (cols >= 0) & (cols < across)
        valid = ok if valid is None else valid & ok
    if valid is None:
        return x
    return jnp.where(valid, x, 0.0)


def forward_kernel(log_ref, sto_ref, init_ref, forc_ref, out_ref, perm, trans, diag, head_a, head_b):
    planes, depth, across = log_ref.shape
    zero = jnp.zeros((depth, across), jnp.float32)
    for buf in (perm, head_a, head_b):
        buf[0] = zero
        buf[planes + 1] = zero

    def fill(p, carry):
        perm[p + 1] = jnp.exp(log_ref[p])
        head_a[p + 1] = init_ref[p]
        return carry

    lax.fori_loop(0, planes, fill, 0)

    def transmissibility(p, carry):
        own = perm[p + 1]
        for k, (a, b, c) in enumerate(HALF):
            factor = 2.0 ** (1 - abs(a) - abs(b) - abs(c))
            other = shift_plane(perm[p + 1 + a], b, c)
            trans[k, p] = factor * 2.0 * own * other / (own + other)
        return carry

    lax.fori_loop(0, planes, transmissibility, 0)

    def diagonal(p, carry):
        total = sto_ref[p]
        for k, (a, b, c) in enumerate(HALF):
            back = p - a
            inside = (back >= 0) & (back < planes)
            behind = shift_plane(trans[k, jnp.clip(back, 0, planes - 1)], -b, -c)
            total = total + trans[k, p] + jnp.where(inside, behind, 0.0)
        diag[p] = total
        return carry

    lax.fori_loop(0, planes, diagonal, 0)

    def sweep(source, target, padded_target):
        def body(p, carry):
            gathered = None
            for k, (a, b, c) in enumerate(HALF):
                ahead = trans[k, p] * shift_plane(source[p + 1 + a], b, c)
                back = jnp.clip(p - a, 0, planes - 1)
                flow = shift_plane(trans[k, back] * source[p + 1 - a], -b, -c)
                term = ahead + flow
                gathered = term if gathered is None else gathered + term
            value = (1.0 - OMEGA) * source[p + 1] + OMEGA * (forc_ref[p] + gathered) / diag[p]
            if padded_target:
                target[p + 1] = value
            else:
                target[p] = value
            return carry

        lax.fori_loop(0, planes, body, 0)

    sweep(head_a, head_b, True)
    sweep(head_b, head_a, True)
    sweep(head_a, out_ref, False)


def forward_pallas(log_row, storage, head_init, forcing):
    planes, depth, across = log_row.shape
    vmem = pl.BlockSpec(memory_space=pltpu.VMEM)
    return pl.pallas_call(
        forward_kernel,
        out_shape=jax.ShapeDtypeStruct((planes, depth, across), jnp.float32),
        in_specs=[vmem] * 4,
        out_specs=vmem,
        scratch_shapes=[
            pltpu.VMEM((planes + 2, depth, across), jnp.float32),
            pltpu.VMEM((len(HALF), planes, depth, across), jnp.float32),
            pltpu.VMEM((planes, depth, across), jnp.float32),
            pltpu.VMEM((planes + 2, depth, across), jnp.float32),
            pltpu.VMEM((planes + 2, depth, across), jnp.float32),
        ],
        compiler_params=pltpu.CompilerParams(vmem_limit_bytes=66 * 1024 * 1024),
    )(log_row, storage, head_init, forcing)


def gather_kernel(row_ref, out_ref, landing, send_sem, recv_sem):
    total = landing.shape[0]
    n_space = lax.axis_size("space")
    me_s = lax.axis_index("space")
    me_e = lax.axis_index("ens")
    mine = me_e * n_space + me_s
    mesh_id = pl.DeviceIdType.MESH

    barrier = pltpu.get_barrier_semaphore()

    def greet(i, carry):
        @pl.when(i != mine)
        def _():
            pl.semaphore_signal(
                barrier, 1, device_id=(i % n_space, i // n_space), device_id_type=mesh_id
            )

        return carry

    lax.fori_loop(0, total, greet, 0)
    pl.semaphore_wait(barrier, total - 1)

    def send(i, carry):
        @pl.when(i != mine)
        def _():
            pltpu.make_async_remote_copy(
                src_ref=row_ref,
                dst_ref=landing.at[pl.ds(mine, 1)],
                send_sem=send_sem,
                recv_sem=recv_sem,
                device_id=(i % n_space, i // n_space),
                device_id_type=mesh_id,
            ).start()

        return carry

    lax.fori_loop(0, total, send, 0)
    landing[pl.ds(mine, 1)] = row_ref[...]
    partner = (mine + 1) % total
    everything = pltpu.make_async_remote_copy(
        src_ref=landing.at[pl.ds(0, total - 1)],
        dst_ref=landing.at[pl.ds(1, total - 1)],
        send_sem=send_sem,
        recv_sem=recv_sem,
        device_id=(partner % n_space, partner // n_space),
        device_id_type=mesh_id,
    )
    everything.wait_send()
    everything.wait_recv()
    out_ref[...] = landing[...]


def gather_rows(row, total):
    vmem = pl.BlockSpec(memory_space=pltpu.VMEM)
    return pl.pallas_call(
        gather_kernel,
        out_shape=jax.ShapeDtypeStruct((total,) + row.shape[1:], jnp.float32),
        in_specs=[vmem],
        out_specs=vmem,
        scratch_shapes=[
            pltpu.VMEM((total,) + row.shape[1:], jnp.float32),
            pltpu.SemaphoreType.DMA,
            pltpu.SemaphoreType.DMA,
        ],
        compiler_params=pltpu.CompilerParams(collective_id=1, has_side_effects=True),
    )(row)


def return_kernel(column_ref, update_out, upd_send, upd_recv, local_sem):
    groups = update_out.shape[1] // column_ref.shape[1]
    rows = column_ref.shape[1]
    members = update_out.shape[0]
    me_s = lax.axis_index("space")
    me_e = lax.axis_index("ens")
    mesh_id = pl.DeviceIdType.MESH

    barrier = pltpu.get_barrier_semaphore()
    for e in range(groups):
        @pl.when(me_e != e)
        def _():
            pl.semaphore_signal(barrier, 1, device_id=(me_s, e), device_id_type=mesh_id)
    pl.semaphore_wait(barrier, groups - 1)

    def upd_copy(e, source_e):
        return pltpu.make_async_remote_copy(
            src_ref=column_ref.at[pl.ds(e * members, members)],
            dst_ref=update_out.at[:, pl.ds(source_e * rows, rows)],
            send_sem=upd_send.at[e],
            recv_sem=upd_recv.at[source_e],
            device_id=(me_s, e),
            device_id_type=mesh_id,
        )

    keep_upd = pltpu.make_async_copy(
        column_ref.at[pl.ds(me_e * members, members)],
        update_out.at[:, pl.ds(me_e * rows, rows)],
        local_sem,
    )
    for e in range(groups):
        @pl.when(me_e != e)
        def _():
            upd_copy(e, me_e).start()
    keep_upd.start()
    keep_upd.wait()
    for e in range(groups):
        @pl.when(me_e != e)
        def _():
            upd_copy(e, me_e).wait_send()
            upd_copy(e, e).wait_recv()


def send_back(column, slab_rows):
    total, rows, across = column.shape
    groups = slab_rows // rows
    members = total // groups
    anywhere = pl.BlockSpec(memory_space=pl.ANY)
    return pl.pallas_call(
        return_kernel,
        out_shape=jax.ShapeDtypeStruct((members, slab_rows, across), jnp.float32),
        in_specs=[anywhere],
        out_specs=anywhere,
        scratch_shapes=[
            pltpu.SemaphoreType.DMA((groups,)),
            pltpu.SemaphoreType.DMA((groups,)),
            pltpu.SemaphoreType.DMA,
        ],
        compiler_params=pltpu.CompilerParams(collective_id=2, has_side_effects=True),
    )(column)


def gather_grid(slab, n_space, n_ens):
    rows = n_space // 2
    me_s = lax.axis_index("space")
    z, half = me_s // 2, me_s % 2
    pieces = [(slab, me_s)]
    for flip in (0, 1):
        for dz in range(1 - flip, rows):
            pairs = []
            for s in range(n_space):
                zs, hs = s // 2, s % 2
                t = ((zs + dz) % rows) * 2 + (hs ^ flip)
                for e in range(n_ens):
                    pairs.append((s * n_ens + e, t * n_ens + (e ^ (2 * flip))))
            got = lax.ppermute(slab, ("space", "ens"), pairs)
            pieces.append((got, ((z - dz) % rows) * 2 + (half ^ flip)))
    thick = slab.shape[0]
    grid = jnp.zeros((n_space * thick,) + slab.shape[1:], slab.dtype)
    for got, source in pieces:
        grid = lax.dynamic_update_slice_in_dim(grid, got, source * thick, axis=0)
    return grid


def shards(
    log_perm,
    storage,
    head_init,
    well_cells,
    well_rates,
    obs_cells,
    obs_values,
    noise_var,
    step_size,
    perturb,
):
    members, planes, depth, across = log_perm.shape
    n_space = lax.axis_size("space")
    n_ens = lax.axis_size("ens")
    cell_count = planes * depth * across
    total_members = members * n_ens
    grid_planes = planes * n_space

    whole_log = lax.all_to_all(log_perm, "space", 0, 1, tiled=True)
    core = lax.axis_index("ens") % 2
    mine = gather_grid(jnp.where(core == 0, storage, head_init), n_space, n_ens)
    pairs = [(e, e ^ 1) for e in range(n_ens)]
    other = lax.ppermute(mine, "ens", pairs)
    whole_storage = jnp.where(core == 0, mine, other)
    whole_head = jnp.where(core == 0, other, mine)
    source = (
        jnp.zeros((grid_planes * depth * across,), jnp.float32)
        .at[well_cells]
        .add(well_rates)
        .reshape(grid_planes, depth, across)
    )
    forcing = whole_storage * whole_head + source
    field = forward_pallas(whole_log[0], whole_storage, whole_head, forcing)
    picked = field.reshape(-1)[obs_cells]
    head_field = lax.all_to_all(field[None], "space", 1, 0, tiled=True)

    obs_count = picked.shape[0]
    own_perturb = lax.dynamic_index_in_dim(perturb, lax.axis_index("space"), 0, keepdims=False)
    row = jnp.zeros((1, 8, 128), jnp.float32)
    row = row.at[0, 0, :obs_count].set(picked).at[0, 0, obs_count : 2 * obs_count].set(own_perturb)
    rows = gather_rows(row, total_members)
    every_obs = rows[:, 0, :obs_count]
    every_perturb = rows[:, 0, obs_count : 2 * obs_count]
    mean_obs = jnp.mean(every_obs, axis=0)
    spread = every_obs - mean_obs
    covariance = jnp.dot(spread.T, spread, precision=HIGHEST) / (total_members - 1)
    system = covariance + jnp.diag(noise_var / step_size[0])
    factor_lower = jnp.linalg.cholesky(system)
    gain_rows = solve_pair(factor_lower, obs_values[None, :] + every_perturb - every_obs)
    mixing = jnp.dot(gain_rows, spread.T, precision=HIGHEST)

    slab_rows = planes * depth
    band = lax.all_to_all(log_perm.reshape(members, slab_rows, across), "ens", 1, 0, tiled=True)
    change = jnp.einsum("jk,kry->jry", mixing, band, precision=HIGHEST)
    new_band = band + change / (total_members - 1)
    updated = send_back(new_band, slab_rows)
    updated = updated.reshape(log_perm.shape)
    return (head_field, updated)


def solution(mesh):
    return jax.shard_map(
        shards,
        mesh=mesh,
        in_specs=(
            P("ens", "space", None, None),
            P("space", None, None),
            P("space", None, None),
            P(),
            P(),
            P(),
            P(),
            P(),
            P(),
            P("ens", None),
        ),
        out_specs=(P("ens", "space", None, None), P("ens", "space", None, None)),
        check_vma=False,
    )
```

```python
import jax
from jax.experimental import pallas as pl
from jax.experimental.pallas import tpu as pltpu
import jax.numpy as jnp
from jax import lax
from jax.sharding import PartitionSpec as P

SWEEPS = 3


OMEGA = 0.8
HIGHEST = lax.Precision.HIGHEST
DIRECTIONS = [
    (a, b, c) for a in (-1, 0, 1) for b in (-1, 0, 1) for c in (-1, 0, 1) if (a, b, c) != (0, 0, 0)
]


def shifted(padded, a, b, c, planes, depth, across):
    return padded[..., 1 + a : 1 + a + planes, 1 + b : 1 + b + depth, 1 + c : 1 + c + across]


def solve_pair(factor, residual):
    first = lax.linalg.triangular_solve(factor, residual.T, left_side=True, lower=True)
    second = lax.linalg.triangular_solve(
        factor, first, left_side=True, lower=True, transpose_a=True
    )
    return second.T


HALF = [(a, b, c) for a, b, c in DIRECTIONS if (a, b, c) > (0, 0, 0)]


def shift_plane(x, b, c):
    depth, across = x.shape
    valid = None
    if b != 0:
        x = pltpu.roll(x, (-b) % depth, 0)
        rows = lax.broadcasted_iota(jnp.int32, x.shape, 0) + b
        valid = (rows >= 0) & (rows < depth)
    if c != 0:
        x = pltpu.roll(x, (-c) % across, 1)
        cols = lax.broadcasted_iota(jnp.int32, x.shape, 1) + c
        ok = (cols >= 0) & (cols < across)
        valid = ok if valid is None else valid & ok
    if valid is None:
        return x
    return jnp.where(valid, x, 0.0)


def forward_kernel(
    log_ref, sto_ref, init_ref, forc_ref, rows_ref, out_ref, band_ref,
    perm, trans, diag, head_a, head_b, band_send, band_recv, local_sem,
):
    planes, depth, across = log_ref.shape
    members, slab_rows, _ = rows_ref.shape
    groups = band_ref.shape[0] // members
    rows = slab_rows // groups
    me_s = lax.axis_index("space")
    me_e = lax.axis_index("ens")
    mesh_id = pl.DeviceIdType.MESH
    barrier = pltpu.get_barrier_semaphore()
    for e in range(groups):
        @pl.when(me_e != e)
        def _():
            pl.semaphore_signal(barrier, 1, device_id=(me_s, e), device_id_type=mesh_id)

    def band_copy(e, source_e):
        return pltpu.make_async_remote_copy(
            src_ref=rows_ref.at[:, pl.ds(e * rows, rows)],
            dst_ref=band_ref.at[pl.ds(source_e * members, members)],
            send_sem=band_send.at[e],
            recv_sem=band_recv.at[source_e],
            device_id=(me_s, e),
            device_id_type=mesh_id,
        )

    keep_band = pltpu.make_async_copy(
        rows_ref.at[:, pl.ds(me_e * rows, rows)],
        band_ref.at[pl.ds(me_e * members, members)],
        local_sem,
    )
    zero = jnp.zeros((depth, across), jnp.float32)
    for buf in (perm, head_a, head_b):
        buf[0] = zero
        buf[planes + 1] = zero

    def fill(p, carry):
        perm[p + 1] = jnp.exp(log_ref[p])
        head_a[p + 1] = init_ref[p]
        return carry

    lax.fori_loop(0, planes, fill, 0)

    def transmissibility(p, carry):
        own = perm[p + 1]
        for k, (a, b, c) in enumerate(HALF):
            factor = 2.0 ** (1 - abs(a) - abs(b) - abs(c))
            other = shift_plane(perm[p + 1 + a], b, c)
            trans[k, p] = factor * 2.0 * own * other / (own + other)
        return carry

    lax.fori_loop(0, planes, transmissibility, 0)

    pl.semaphore_wait(barrier, groups - 1)
    for e in range(groups):
        @pl.when(me_e != e)
        def _():
            band_copy(e, me_e).start()
    keep_band.start()

    def diagonal(p, carry):
        total = sto_ref[p]
        for k, (a, b, c) in enumerate(HALF):
            back = p - a
            inside = (back >= 0) & (back < planes)
            behind = shift_plane(trans[k, jnp.clip(back, 0, planes - 1)], -b, -c)
            total = total + trans[k, p] + jnp.where(inside, behind, 0.0)
        diag[p] = total
        return carry

    lax.fori_loop(0, planes, diagonal, 0)

    def sweep(source, target, padded_target):
        def body(p, carry):
            gathered = None
            for k, (a, b, c) in enumerate(HALF):
                ahead = trans[k, p] * shift_plane(source[p + 1 + a], b, c)
                back = jnp.clip(p - a, 0, planes - 1)
                flow = shift_plane(trans[k, back] * source[p + 1 - a], -b, -c)
                term = ahead + flow
                gathered = term if gathered is None else gathered + term
            value = (1.0 - OMEGA) * source[p + 1] + OMEGA * (forc_ref[p] + gathered) / diag[p]
            if padded_target:
                target[p + 1] = value
            else:
                target[p] = value
            return carry

        lax.fori_loop(0, planes, body, 0)

    sweep(head_a, head_b, True)
    sweep(head_b, head_a, True)
    sweep(head_a, out_ref, False)
    keep_band.wait()
    for e in range(groups):
        @pl.when(me_e != e)
        def _():
            band_copy(e, me_e).wait_send()
            band_copy(e, e).wait_recv()


def forward_pallas(log_row, storage, head_init, forcing, by_rows, groups):
    planes, depth, across = log_row.shape
    members, slab_rows, _ = by_rows.shape
    vmem = pl.BlockSpec(memory_space=pltpu.VMEM)
    anywhere = pl.BlockSpec(memory_space=pl.ANY)
    return pl.pallas_call(
        forward_kernel,
        out_shape=(
            jax.ShapeDtypeStruct((planes, depth, across), jnp.float32),
            jax.ShapeDtypeStruct((members * groups, slab_rows // groups, across), jnp.float32),
        ),
        in_specs=[vmem] * 4 + [anywhere],
        out_specs=(vmem, anywhere),
        scratch_shapes=[
            pltpu.VMEM((planes + 2, depth, across), jnp.float32),
            pltpu.VMEM((len(HALF), planes, depth, across), jnp.float32),
            pltpu.VMEM((planes, depth, across), jnp.float32),
            pltpu.VMEM((planes + 2, depth, across), jnp.float32),
            pltpu.VMEM((planes + 2, depth, across), jnp.float32),
            pltpu.SemaphoreType.DMA((groups,)),
            pltpu.SemaphoreType.DMA((groups,)),
            pltpu.SemaphoreType.DMA,
        ],
        compiler_params=pltpu.CompilerParams(
            vmem_limit_bytes=66 * 1024 * 1024, collective_id=3, has_side_effects=True
        ),
    )(log_row, storage, head_init, forcing, by_rows)


def gather_kernel(row_ref, out_ref, landing, send_sem, recv_sem):
    total = landing.shape[0]
    n_space = lax.axis_size("space")
    me_s = lax.axis_index("space")
    me_e = lax.axis_index("ens")
    mine = me_e * n_space + me_s
    mesh_id = pl.DeviceIdType.MESH

    barrier = pltpu.get_barrier_semaphore()

    def greet(i, carry):
        @pl.when(i != mine)
        def _():
            pl.semaphore_signal(
                barrier, 1, device_id=(i % n_space, i // n_space), device_id_type=mesh_id
            )

        return carry

    lax.fori_loop(0, total, greet, 0)
    pl.semaphore_wait(barrier, total - 1)

    def send(i, carry):
        @pl.when(i != mine)
        def _():
            pltpu.make_async_remote_copy(
                src_ref=row_ref,
                dst_ref=landing.at[pl.ds(mine, 1)],
                send_sem=send_sem,
                recv_sem=recv_sem,
                device_id=(i % n_space, i // n_space),
                device_id_type=mesh_id,
            ).start()

        return carry

    lax.fori_loop(0, total, send, 0)
    landing[pl.ds(mine, 1)] = row_ref[...]
    partner = (mine + 1) % total
    everything = pltpu.make_async_remote_copy(
        src_ref=landing.at[pl.ds(0, total - 1)],
        dst_ref=landing.at[pl.ds(1, total - 1)],
        send_sem=send_sem,
        recv_sem=recv_sem,
        device_id=(partner % n_space, partner // n_space),
        device_id_type=mesh_id,
    )
    everything.wait_send()
    everything.wait_recv()
    out_ref[...] = landing[...]


def gather_rows(row, total):
    vmem = pl.BlockSpec(memory_space=pltpu.VMEM)
    return pl.pallas_call(
        gather_kernel,
        out_shape=jax.ShapeDtypeStruct((total,) + row.shape[1:], jnp.float32),
        in_specs=[vmem],
        out_specs=vmem,
        scratch_shapes=[
            pltpu.VMEM((total,) + row.shape[1:], jnp.float32),
            pltpu.SemaphoreType.DMA,
            pltpu.SemaphoreType.DMA,
        ],
        compiler_params=pltpu.CompilerParams(collective_id=1, has_side_effects=True),
    )(row)


def return_kernel(column_ref, update_out, upd_send, upd_recv, local_sem):
    groups = update_out.shape[1] // column_ref.shape[1]
    rows = column_ref.shape[1]
    members = update_out.shape[0]
    me_s = lax.axis_index("space")
    me_e = lax.axis_index("ens")
    mesh_id = pl.DeviceIdType.MESH

    barrier = pltpu.get_barrier_semaphore()
    for e in range(groups):
        @pl.when(me_e != e)
        def _():
            pl.semaphore_signal(barrier, 1, device_id=(me_s, e), device_id_type=mesh_id)
    pl.semaphore_wait(barrier, groups - 1)

    def upd_copy(e, source_e):
        return pltpu.make_async_remote_copy(
            src_ref=column_ref.at[pl.ds(e * members, members)],
            dst_ref=update_out.at[:, pl.ds(source_e * rows, rows)],
            send_sem=upd_send.at[e],
            recv_sem=upd_recv.at[source_e],
            device_id=(me_s, e),
            device_id_type=mesh_id,
        )

    keep_upd = pltpu.make_async_copy(
        column_ref.at[pl.ds(me_e * members, members)],
        update_out.at[:, pl.ds(me_e * rows, rows)],
        local_sem,
    )
    for e in range(groups):
        @pl.when(me_e != e)
        def _():
            upd_copy(e, me_e).start()
    keep_upd.start()
    keep_upd.wait()
    for e in range(groups):
        @pl.when(me_e != e)
        def _():
            upd_copy(e, me_e).wait_send()
            upd_copy(e, e).wait_recv()


def send_back(column, slab_rows):
    total, rows, across = column.shape
    groups = slab_rows // rows
    members = total // groups
    anywhere = pl.BlockSpec(memory_space=pl.ANY)
    return pl.pallas_call(
        return_kernel,
        out_shape=jax.ShapeDtypeStruct((members, slab_rows, across), jnp.float32),
        in_specs=[anywhere],
        out_specs=anywhere,
        scratch_shapes=[
            pltpu.SemaphoreType.DMA((groups,)),
            pltpu.SemaphoreType.DMA((groups,)),
            pltpu.SemaphoreType.DMA,
        ],
        compiler_params=pltpu.CompilerParams(collective_id=2, has_side_effects=True),
    )(column)


def gather_grid(slab, n_space, n_ens):
    rows = n_space // 2
    me_s = lax.axis_index("space")
    z, half = me_s // 2, me_s % 2
    pieces = [(slab, me_s)]
    for flip in (0, 1):
        for dz in range(1 - flip, rows):
            pairs = []
            for s in range(n_space):
                zs, hs = s // 2, s % 2
                t = ((zs + dz) % rows) * 2 + (hs ^ flip)
                for e in range(n_ens):
                    pairs.append((s * n_ens + e, t * n_ens + (e ^ (2 * flip))))
            got = lax.ppermute(slab, ("space", "ens"), pairs)
            pieces.append((got, ((z - dz) % rows) * 2 + (half ^ flip)))
    thick = slab.shape[0]
    grid = jnp.zeros((n_space * thick,) + slab.shape[1:], slab.dtype)
    for got, source in pieces:
        grid = lax.dynamic_update_slice_in_dim(grid, got, source * thick, axis=0)
    return grid


def shards(
    log_perm,
    storage,
    head_init,
    well_cells,
    well_rates,
    obs_cells,
    obs_values,
    noise_var,
    step_size,
    perturb,
):
    members, planes, depth, across = log_perm.shape
    n_space = lax.axis_size("space")
    n_ens = lax.axis_size("ens")
    cell_count = planes * depth * across
    total_members = members * n_ens
    grid_planes = planes * n_space

    whole_log = lax.all_to_all(log_perm, "space", 0, 1, tiled=True)
    core = lax.axis_index("ens") % 2
    mine = gather_grid(jnp.where(core == 0, storage, head_init), n_space, n_ens)
    pairs = [(e, e ^ 1) for e in range(n_ens)]
    other = lax.ppermute(mine, "ens", pairs)
    whole_storage = jnp.where(core == 0, mine, other)
    whole_head = jnp.where(core == 0, other, mine)
    source = (
        jnp.zeros((grid_planes * depth * across,), jnp.float32)
        .at[well_cells]
        .add(well_rates)
        .reshape(grid_planes, depth, across)
    )
    forcing = whole_storage * whole_head + source
    slab_rows = planes * depth
    by_rows = log_perm.reshape(members, slab_rows, across)
    field, band = forward_pallas(
        whole_log[0], whole_storage, whole_head, forcing, by_rows, n_ens
    )
    picked = field.reshape(-1)[obs_cells]
    head_field = lax.all_to_all(field[None], "space", 1, 0, tiled=True)

    obs_count = picked.shape[0]
    own_perturb = lax.dynamic_index_in_dim(perturb, lax.axis_index("space"), 0, keepdims=False)
    row = jnp.zeros((1, 8, 128), jnp.float32)
    row = row.at[0, 0, :obs_count].set(picked).at[0, 0, obs_count : 2 * obs_count].set(own_perturb)
    rows = gather_rows(row, total_members)
    every_obs = rows[:, 0, :obs_count]
    every_perturb = rows[:, 0, obs_count : 2 * obs_count]
    mean_obs = jnp.mean(every_obs, axis=0)
    spread = every_obs - mean_obs
    covariance = jnp.dot(spread.T, spread, precision=HIGHEST) / (total_members - 1)
    system = covariance + jnp.diag(noise_var / step_size[0])
    factor_lower = jnp.linalg.cholesky(system)
    gain_rows = solve_pair(factor_lower, obs_values[None, :] + every_perturb - every_obs)
    mixing = jnp.dot(gain_rows, spread.T, precision=HIGHEST)

    change = jnp.einsum("jk,kry->jry", mixing, band, precision=HIGHEST)
    new_band = band + change / (total_members - 1)
    updated = send_back(new_band, slab_rows)
    updated = updated.reshape(log_perm.shape)
    return (head_field, updated)


def solution(mesh):
    return jax.shard_map(
        shards,
        mesh=mesh,
        in_specs=(
            P("ens", "space", None, None),
            P("space", None, None),
            P("space", None, None),
            P(),
            P(),
            P(),
            P(),
            P(),
            P(),
            P("ens", None),
        ),
        out_specs=(P("ens", "space", None, None), P("ens", "space", None, None)),
        check_vma=False,
    )
```

```python
import jax
from jax.experimental import pallas as pl
from jax.experimental.pallas import tpu as pltpu
import jax.numpy as jnp
from jax import lax
from jax.sharding import PartitionSpec as P

SWEEPS = 3


OMEGA = 0.8
HIGHEST = lax.Precision.HIGHEST
DIRECTIONS = [
    (a, b, c) for a in (-1, 0, 1) for b in (-1, 0, 1) for c in (-1, 0, 1) if (a, b, c) != (0, 0, 0)
]


def shifted(padded, a, b, c, planes, depth, across):
    return padded[..., 1 + a : 1 + a + planes, 1 + b : 1 + b + depth, 1 + c : 1 + c + across]


def solve_pair(factor, residual):
    first = lax.linalg.triangular_solve(factor, residual.T, left_side=True, lower=True)
    second = lax.linalg.triangular_solve(
        factor, first, left_side=True, lower=True, transpose_a=True
    )
    return second.T


HALF = [(a, b, c) for a, b, c in DIRECTIONS if (a, b, c) > (0, 0, 0)]


def shift_plane(x, b, c):
    depth, across = x.shape
    valid = None
    if b != 0:
        x = pltpu.roll(x, (-b) % depth, 0)
        rows = lax.broadcasted_iota(jnp.int32, x.shape, 0) + b
        valid = (rows >= 0) & (rows < depth)
    if c != 0:
        x = pltpu.roll(x, (-c) % across, 1)
        cols = lax.broadcasted_iota(jnp.int32, x.shape, 1) + c
        ok = (cols >= 0) & (cols < across)
        valid = ok if valid is None else valid & ok
    if valid is None:
        return x
    return jnp.where(valid, x, 0.0)


def forward_kernel(
    log_ref, sto_ref, init_ref, forc_ref, rows_ref, out_ref, band_ref,
    perm, trans, diag, head_a, head_b, band_send, band_recv, local_sem,
):
    planes, depth, across = log_ref.shape
    members, slab_rows, _ = rows_ref.shape
    groups = band_ref.shape[0] // members
    rows = slab_rows // groups
    me_s = lax.axis_index("space")
    me_e = lax.axis_index("ens")
    mesh_id = pl.DeviceIdType.MESH
    barrier = pltpu.get_barrier_semaphore()
    for e in range(groups):
        @pl.when(me_e != e)
        def _():
            pl.semaphore_signal(barrier, 1, device_id=(me_s, e), device_id_type=mesh_id)

    def band_copy(e, source_e):
        return pltpu.make_async_remote_copy(
            src_ref=rows_ref.at[:, pl.ds(e * rows, rows)],
            dst_ref=band_ref.at[pl.ds(source_e * members, members)],
            send_sem=band_send.at[e],
            recv_sem=band_recv.at[source_e],
            device_id=(me_s, e),
            device_id_type=mesh_id,
        )

    keep_band = pltpu.make_async_copy(
        rows_ref.at[:, pl.ds(me_e * rows, rows)],
        band_ref.at[pl.ds(me_e * members, members)],
        local_sem,
    )
    zero = jnp.zeros((depth, across), jnp.float32)
    for buf in (perm, head_a, head_b):
        buf[0] = zero
        buf[planes + 1] = zero

    def fill(p, carry):
        perm[p + 1] = jnp.exp(log_ref[p])
        head_a[p + 1] = init_ref[p]
        return carry

    lax.fori_loop(0, planes, fill, 0)

    def transmissibility(p, carry):
        own = perm[p + 1]
        for k, (a, b, c) in enumerate(HALF):
            factor = 2.0 ** (1 - abs(a) - abs(b) - abs(c))
            other = shift_plane(perm[p + 1 + a], b, c)
            trans[k, p] = factor * 2.0 * own * other / (own + other)
        return carry

    lax.fori_loop(0, planes, transmissibility, 0)

    pl.semaphore_wait(barrier, groups - 1)
    for e in range(groups):
        @pl.when(me_e != e)
        def _():
            band_copy(e, me_e).start()
    keep_band.start()

    def diagonal(p, carry):
        total = sto_ref[p]
        for k, (a, b, c) in enumerate(HALF):
            back = p - a
            inside = (back >= 0) & (back < planes)
            behind = shift_plane(trans[k, jnp.clip(back, 0, planes - 1)], -b, -c)
            total = total + trans[k, p] + jnp.where(inside, behind, 0.0)
        diag[p] = total
        return carry

    lax.fori_loop(0, planes, diagonal, 0)

    def sweep(source, target, padded_target):
        def body(p, carry):
            gathered = None
            for k, (a, b, c) in enumerate(HALF):
                ahead = trans[k, p] * shift_plane(source[p + 1 + a], b, c)
                back = jnp.clip(p - a, 0, planes - 1)
                flow = shift_plane(trans[k, back] * source[p + 1 - a], -b, -c)
                term = ahead + flow
                gathered = term if gathered is None else gathered + term
            value = (1.0 - OMEGA) * source[p + 1] + OMEGA * (forc_ref[p] + gathered) / diag[p]
            if padded_target:
                target[p + 1] = value
            else:
                target[p] = value
            return carry

        lax.fori_loop(0, planes, body, 0)

    sweep(head_a, head_b, True)
    sweep(head_b, head_a, True)
    sweep(head_a, out_ref, False)
    keep_band.wait()
    for e in range(groups):
        @pl.when(me_e != e)
        def _():
            band_copy(e, me_e).wait_send()
            band_copy(e, e).wait_recv()


def forward_pallas(log_row, storage, head_init, forcing, by_rows, groups):
    planes, depth, across = log_row.shape
    members, slab_rows, _ = by_rows.shape
    vmem = pl.BlockSpec(memory_space=pltpu.VMEM)
    anywhere = pl.BlockSpec(memory_space=pl.ANY)
    return pl.pallas_call(
        forward_kernel,
        out_shape=(
            jax.ShapeDtypeStruct((planes, depth, across), jnp.float32),
            jax.ShapeDtypeStruct((members * groups, slab_rows // groups, across), jnp.float32),
        ),
        in_specs=[vmem] * 4 + [anywhere],
        out_specs=(vmem, anywhere),
        scratch_shapes=[
            pltpu.VMEM((planes + 2, depth, across), jnp.float32),
            pltpu.VMEM((len(HALF), planes, depth, across), jnp.float32),
            pltpu.VMEM((planes, depth, across), jnp.float32),
            pltpu.VMEM((planes + 2, depth, across), jnp.float32),
            pltpu.VMEM((planes + 2, depth, across), jnp.float32),
            pltpu.SemaphoreType.DMA((groups,)),
            pltpu.SemaphoreType.DMA((groups,)),
            pltpu.SemaphoreType.DMA,
        ],
        compiler_params=pltpu.CompilerParams(
            vmem_limit_bytes=66 * 1024 * 1024, collective_id=3, has_side_effects=True
        ),
    )(log_row, storage, head_init, forcing, by_rows)


def gather_kernel(row_ref, out_ref, landing, send_sem, recv_sem):
    total = landing.shape[0]
    n_space = lax.axis_size("space")
    me_s = lax.axis_index("space")
    me_e = lax.axis_index("ens")
    mine = me_e * n_space + me_s
    mesh_id = pl.DeviceIdType.MESH

    barrier = pltpu.get_barrier_semaphore()

    def greet(i, carry):
        @pl.when(i != mine)
        def _():
            pl.semaphore_signal(
                barrier, 1, device_id=(i % n_space, i // n_space), device_id_type=mesh_id
            )

        return carry

    lax.fori_loop(0, total, greet, 0)
    pl.semaphore_wait(barrier, total - 1)

    def send(i, carry):
        @pl.when(i != mine)
        def _():
            pltpu.make_async_remote_copy(
                src_ref=row_ref,
                dst_ref=landing.at[pl.ds(mine, 1)],
                send_sem=send_sem,
                recv_sem=recv_sem,
                device_id=(i % n_space, i // n_space),
                device_id_type=mesh_id,
            ).start()

        return carry

    lax.fori_loop(0, total, send, 0)
    landing[pl.ds(mine, 1)] = row_ref[...]
    partner = (mine + 1) % total
    everything = pltpu.make_async_remote_copy(
        src_ref=landing.at[pl.ds(0, total - 1)],
        dst_ref=landing.at[pl.ds(1, total - 1)],
        send_sem=send_sem,
        recv_sem=recv_sem,
        device_id=(partner % n_space, partner // n_space),
        device_id_type=mesh_id,
    )
    everything.wait_send()
    everything.wait_recv()
    out_ref[...] = landing[...]


def gather_rows(row, total):
    vmem = pl.BlockSpec(memory_space=pltpu.VMEM)
    return pl.pallas_call(
        gather_kernel,
        out_shape=jax.ShapeDtypeStruct((total,) + row.shape[1:], jnp.float32),
        in_specs=[vmem],
        out_specs=vmem,
        scratch_shapes=[
            pltpu.VMEM((total,) + row.shape[1:], jnp.float32),
            pltpu.SemaphoreType.DMA,
            pltpu.SemaphoreType.DMA,
        ],
        compiler_params=pltpu.CompilerParams(collective_id=1, has_side_effects=True),
    )(row)


def return_kernel(column_ref, update_out, upd_send, upd_recv, local_sem):
    groups = update_out.shape[1] // column_ref.shape[1]
    rows = column_ref.shape[1]
    members = update_out.shape[0]
    me_s = lax.axis_index("space")
    me_e = lax.axis_index("ens")
    mesh_id = pl.DeviceIdType.MESH

    barrier = pltpu.get_barrier_semaphore()
    for e in range(groups):
        @pl.when(me_e != e)
        def _():
            pl.semaphore_signal(barrier, 1, device_id=(me_s, e), device_id_type=mesh_id)
    pl.semaphore_wait(barrier, groups - 1)

    def upd_copy(e, source_e):
        return pltpu.make_async_remote_copy(
            src_ref=column_ref.at[pl.ds(e * members, members)],
            dst_ref=update_out.at[:, pl.ds(source_e * rows, rows)],
            send_sem=upd_send.at[e],
            recv_sem=upd_recv.at[source_e],
            device_id=(me_s, e),
            device_id_type=mesh_id,
        )

    keep_upd = pltpu.make_async_copy(
        column_ref.at[pl.ds(me_e * members, members)],
        update_out.at[:, pl.ds(me_e * rows, rows)],
        local_sem,
    )
    for e in range(groups):
        @pl.when(me_e != e)
        def _():
            upd_copy(e, me_e).start()
    keep_upd.start()
    keep_upd.wait()
    for e in range(groups):
        @pl.when(me_e != e)
        def _():
            upd_copy(e, me_e).wait_send()
            upd_copy(e, e).wait_recv()


def send_back(column, slab_rows):
    total, rows, across = column.shape
    groups = slab_rows // rows
    members = total // groups
    anywhere = pl.BlockSpec(memory_space=pl.ANY)
    return pl.pallas_call(
        return_kernel,
        out_shape=jax.ShapeDtypeStruct((members, slab_rows, across), jnp.float32),
        in_specs=[anywhere],
        out_specs=anywhere,
        scratch_shapes=[
            pltpu.SemaphoreType.DMA((groups,)),
            pltpu.SemaphoreType.DMA((groups,)),
            pltpu.SemaphoreType.DMA,
        ],
        compiler_params=pltpu.CompilerParams(collective_id=2, has_side_effects=True),
    )(column)


def gather_grid(slab, n_space, n_ens):
    rows = n_space // 2
    me_s = lax.axis_index("space")
    z, half = me_s // 2, me_s % 2
    pieces = [(slab, me_s)]
    for flip in (0, 1):
        for dz in range(1 - flip, rows):
            pairs = []
            for s in range(n_space):
                zs, hs = s // 2, s % 2
                t = ((zs + dz) % rows) * 2 + (hs ^ flip)
                for e in range(n_ens):
                    pairs.append((s * n_ens + e, t * n_ens + (e ^ (2 * flip))))
            got = lax.ppermute(slab, ("space", "ens"), pairs)
            pieces.append((got, ((z - dz) % rows) * 2 + (half ^ flip)))
    thick = slab.shape[0]
    grid = jnp.zeros((n_space * thick,) + slab.shape[1:], slab.dtype)
    for got, source in pieces:
        grid = lax.dynamic_update_slice_in_dim(grid, got, source * thick, axis=0)
    return grid


def gather_particle(log_perm, n_space, n_ens):
    rows = n_space // 2
    me_s = lax.axis_index("space")
    z, half = me_s // 2, me_s % 2
    pieces = [(lax.dynamic_index_in_dim(log_perm, me_s, 0, keepdims=False), me_s)]
    for flip in (0, 1):
        for dz in range(1 - flip, rows):
            pairs = []
            for s in range(n_space):
                zs, hs = s // 2, s % 2
                t = ((zs + dz) % rows) * 2 + (hs ^ flip)
                for e in range(n_ens):
                    pairs.append((s * n_ens + e, t * n_ens + e))
            target = ((z + dz) % rows) * 2 + (half ^ flip)
            outgoing = lax.dynamic_index_in_dim(log_perm, target, 0, keepdims=False)
            got = lax.ppermute(outgoing, ("space", "ens"), pairs)
            pieces.append((got, ((z - dz) % rows) * 2 + (half ^ flip)))
    thick = log_perm.shape[1]
    whole = jnp.zeros((n_space * thick,) + log_perm.shape[2:], log_perm.dtype)
    for got, source in pieces:
        whole = lax.dynamic_update_slice_in_dim(whole, got, source * thick, axis=0)
    return whole


def shards(
    log_perm,
    storage,
    head_init,
    well_cells,
    well_rates,
    obs_cells,
    obs_values,
    noise_var,
    step_size,
    perturb,
):
    members, planes, depth, across = log_perm.shape
    n_space = lax.axis_size("space")
    n_ens = lax.axis_size("ens")
    cell_count = planes * depth * across
    total_members = members * n_ens
    grid_planes = planes * n_space

    whole_log = gather_particle(log_perm, n_space, n_ens)
    core = lax.axis_index("ens") % 2
    mine = gather_grid(jnp.where(core == 0, storage, head_init), n_space, n_ens)
    pairs = [(e, e ^ 1) for e in range(n_ens)]
    other = lax.ppermute(mine, "ens", pairs)
    whole_storage = jnp.where(core == 0, mine, other)
    whole_head = jnp.where(core == 0, other, mine)
    source = (
        jnp.zeros((grid_planes * depth * across,), jnp.float32)
        .at[well_cells]
        .add(well_rates)
        .reshape(grid_planes, depth, across)
    )
    forcing = whole_storage * whole_head + source
    slab_rows = planes * depth
    by_rows = log_perm.reshape(members, slab_rows, across)
    field, band = forward_pallas(
        whole_log, whole_storage, whole_head, forcing, by_rows, n_ens
    )
    picked = field.reshape(-1)[obs_cells]
    head_field = lax.all_to_all(field[None], "space", 1, 0, tiled=True)

    obs_count = picked.shape[0]
    own_perturb = lax.dynamic_index_in_dim(perturb, lax.axis_index("space"), 0, keepdims=False)
    row = jnp.zeros((1, 8, 128), jnp.float32)
    row = row.at[0, 0, :obs_count].set(picked).at[0, 0, obs_count : 2 * obs_count].set(own_perturb)
    rows = gather_rows(row, total_members)
    every_obs = rows[:, 0, :obs_count]
    every_perturb = rows[:, 0, obs_count : 2 * obs_count]
    mean_obs = jnp.mean(every_obs, axis=0)
    spread = every_obs - mean_obs
    covariance = jnp.dot(spread.T, spread, precision=HIGHEST) / (total_members - 1)
    system = covariance + jnp.diag(noise_var / step_size[0])
    factor_lower = jnp.linalg.cholesky(system)
    gain_rows = solve_pair(factor_lower, obs_values[None, :] + every_perturb - every_obs)
    mixing = jnp.dot(gain_rows, spread.T, precision=HIGHEST)

    change = jnp.einsum("jk,kry->jry", mixing, band, precision=HIGHEST)
    new_band = band + change / (total_members - 1)
    updated = send_back(new_band, slab_rows)
    updated = updated.reshape(log_perm.shape)
    return (head_field, updated)


def solution(mesh):
    return jax.shard_map(
        shards,
        mesh=mesh,
        in_specs=(
            P("ens", "space", None, None),
            P("space", None, None),
            P("space", None, None),
            P(),
            P(),
            P(),
            P(),
            P(),
            P(),
            P("ens", None),
        ),
        out_specs=(P("ens", "space", None, None), P("ens", "space", None, None)),
        check_vma=False,
    )
```

```python
import jax
from jax.experimental import pallas as pl
from jax.experimental.pallas import tpu as pltpu
import jax.numpy as jnp
from jax import lax
from jax.sharding import PartitionSpec as P

SWEEPS = 3


OMEGA = 0.8
HIGHEST = lax.Precision.HIGHEST
DIRECTIONS = [
    (a, b, c) for a in (-1, 0, 1) for b in (-1, 0, 1) for c in (-1, 0, 1) if (a, b, c) != (0, 0, 0)
]


def shifted(padded, a, b, c, planes, depth, across):
    return padded[..., 1 + a : 1 + a + planes, 1 + b : 1 + b + depth, 1 + c : 1 + c + across]


def solve_pair(factor, residual):
    first = lax.linalg.triangular_solve(factor, residual.T, left_side=True, lower=True)
    second = lax.linalg.triangular_solve(
        factor, first, left_side=True, lower=True, transpose_a=True
    )
    return second.T


HALF = [(a, b, c) for a, b, c in DIRECTIONS if (a, b, c) > (0, 0, 0)]


def shift_plane(x, b, c):
    depth, across = x.shape
    valid = None
    if b != 0:
        x = pltpu.roll(x, (-b) % depth, 0)
        rows = lax.broadcasted_iota(jnp.int32, x.shape, 0) + b
        valid = (rows >= 0) & (rows < depth)
    if c != 0:
        x = pltpu.roll(x, (-c) % across, 1)
        cols = lax.broadcasted_iota(jnp.int32, x.shape, 1) + c
        ok = (cols >= 0) & (cols < across)
        valid = ok if valid is None else valid & ok
    if valid is None:
        return x
    return jnp.where(valid, x, 0.0)


def forward_kernel(
    log_ref, sto_ref, init_ref, forc_ref, rows_ref, out_ref, band_ref,
    perm, trans, diag, head_a, head_b, band_send, band_recv, local_sem,
):
    planes, depth, across = log_ref.shape
    members, slab_rows, _ = rows_ref.shape
    groups = band_ref.shape[0] // members
    rows = slab_rows // groups
    me_s = lax.axis_index("space")
    me_e = lax.axis_index("ens")
    mesh_id = pl.DeviceIdType.MESH
    barrier = pltpu.get_barrier_semaphore()
    for e in range(groups):
        @pl.when(me_e != e)
        def _():
            pl.semaphore_signal(barrier, 1, device_id=(me_s, e), device_id_type=mesh_id)

    def band_copy(e, source_e):
        return pltpu.make_async_remote_copy(
            src_ref=rows_ref.at[:, pl.ds(e * rows, rows)],
            dst_ref=band_ref.at[pl.ds(source_e * members, members)],
            send_sem=band_send.at[e],
            recv_sem=band_recv.at[source_e],
            device_id=(me_s, e),
            device_id_type=mesh_id,
        )

    keep_band = pltpu.make_async_copy(
        rows_ref.at[:, pl.ds(me_e * rows, rows)],
        band_ref.at[pl.ds(me_e * members, members)],
        local_sem,
    )
    zero = jnp.zeros((depth, across), jnp.float32)
    for buf in (perm, head_a, head_b):
        buf[0] = zero
        buf[planes + 1] = zero

    def fill(p, carry):
        perm[p + 1] = jnp.exp(log_ref[p])
        head_a[p + 1] = init_ref[p]
        return carry

    lax.fori_loop(0, planes, fill, 0)

    def transmissibility(p, carry):
        own = perm[p + 1]
        for k, (a, b, c) in enumerate(HALF):
            factor = 2.0 ** (1 - abs(a) - abs(b) - abs(c))
            other = shift_plane(perm[p + 1 + a], b, c)
            trans[k, p] = factor * 2.0 * own * other / (own + other)
        return carry

    lax.fori_loop(0, planes, transmissibility, 0)

    pl.semaphore_wait(barrier, groups - 1)
    for e in range(groups):
        @pl.when(me_e != e)
        def _():
            band_copy(e, me_e).start()
    keep_band.start()

    def diagonal(p, carry):
        total = sto_ref[p]
        for k, (a, b, c) in enumerate(HALF):
            back = p - a
            inside = (back >= 0) & (back < planes)
            behind = shift_plane(trans[k, jnp.clip(back, 0, planes - 1)], -b, -c)
            total = total + trans[k, p] + jnp.where(inside, behind, 0.0)
        diag[p] = total
        return carry

    lax.fori_loop(0, planes, diagonal, 0)

    def sweep(source, target, padded_target):
        def body(p, carry):
            gathered = None
            for k, (a, b, c) in enumerate(HALF):
                ahead = trans[k, p] * shift_plane(source[p + 1 + a], b, c)
                back = jnp.clip(p - a, 0, planes - 1)
                flow = shift_plane(trans[k, back] * source[p + 1 - a], -b, -c)
                term = ahead + flow
                gathered = term if gathered is None else gathered + term
            value = (1.0 - OMEGA) * source[p + 1] + OMEGA * (forc_ref[p] + gathered) / diag[p]
            if padded_target:
                target[p + 1] = value
            else:
                target[p] = value
            return carry

        lax.fori_loop(0, planes, body, 0)

    sweep(head_a, head_b, True)
    sweep(head_b, head_a, True)
    sweep(head_a, out_ref, False)
    keep_band.wait()
    for e in range(groups):
        @pl.when(me_e != e)
        def _():
            band_copy(e, me_e).wait_send()
            band_copy(e, e).wait_recv()


def forward_pallas(log_row, storage, head_init, forcing, by_rows, groups):
    planes, depth, across = log_row.shape
    members, slab_rows, _ = by_rows.shape
    vmem = pl.BlockSpec(memory_space=pltpu.VMEM)
    anywhere = pl.BlockSpec(memory_space=pl.ANY)
    return pl.pallas_call(
        forward_kernel,
        out_shape=(
            jax.ShapeDtypeStruct((planes, depth, across), jnp.float32),
            jax.ShapeDtypeStruct((members * groups, slab_rows // groups, across), jnp.float32),
        ),
        in_specs=[vmem] * 4 + [anywhere],
        out_specs=(vmem, anywhere),
        scratch_shapes=[
            pltpu.VMEM((planes + 2, depth, across), jnp.float32),
            pltpu.VMEM((len(HALF), planes, depth, across), jnp.float32),
            pltpu.VMEM((planes, depth, across), jnp.float32),
            pltpu.VMEM((planes + 2, depth, across), jnp.float32),
            pltpu.VMEM((planes + 2, depth, across), jnp.float32),
            pltpu.SemaphoreType.DMA((groups,)),
            pltpu.SemaphoreType.DMA((groups,)),
            pltpu.SemaphoreType.DMA,
        ],
        compiler_params=pltpu.CompilerParams(
            vmem_limit_bytes=66 * 1024 * 1024, collective_id=3, has_side_effects=True
        ),
    )(log_row, storage, head_init, forcing, by_rows)


def gather_kernel(row_ref, out_ref, landing, send_sem, recv_sem):
    total = landing.shape[0]
    n_space = lax.axis_size("space")
    me_s = lax.axis_index("space")
    me_e = lax.axis_index("ens")
    mine = me_e * n_space + me_s
    mesh_id = pl.DeviceIdType.MESH

    barrier = pltpu.get_barrier_semaphore()

    def greet(i, carry):
        @pl.when(i != mine)
        def _():
            pl.semaphore_signal(
                barrier, 1, device_id=(i % n_space, i // n_space), device_id_type=mesh_id
            )

        return carry

    lax.fori_loop(0, total, greet, 0)
    pl.semaphore_wait(barrier, total - 1)

    def send(i, carry):
        @pl.when(i != mine)
        def _():
            pltpu.make_async_remote_copy(
                src_ref=row_ref,
                dst_ref=landing.at[pl.ds(mine, 1)],
                send_sem=send_sem,
                recv_sem=recv_sem,
                device_id=(i % n_space, i // n_space),
                device_id_type=mesh_id,
            ).start()

        return carry

    lax.fori_loop(0, total, send, 0)
    landing[pl.ds(mine, 1)] = row_ref[...]
    partner = (mine + 1) % total
    everything = pltpu.make_async_remote_copy(
        src_ref=landing.at[pl.ds(0, total - 1)],
        dst_ref=landing.at[pl.ds(1, total - 1)],
        send_sem=send_sem,
        recv_sem=recv_sem,
        device_id=(partner % n_space, partner // n_space),
        device_id_type=mesh_id,
    )
    everything.wait_send()
    everything.wait_recv()
    out_ref[...] = landing[...]


def gather_rows(row, total):
    vmem = pl.BlockSpec(memory_space=pltpu.VMEM)
    return pl.pallas_call(
        gather_kernel,
        out_shape=jax.ShapeDtypeStruct((total,) + row.shape[1:], jnp.float32),
        in_specs=[vmem],
        out_specs=vmem,
        scratch_shapes=[
            pltpu.VMEM((total,) + row.shape[1:], jnp.float32),
            pltpu.SemaphoreType.DMA,
            pltpu.SemaphoreType.DMA,
        ],
        compiler_params=pltpu.CompilerParams(collective_id=1, has_side_effects=True),
    )(row)


def return_kernel(column_ref, update_out, upd_send, upd_recv, local_sem):
    groups = update_out.shape[1] // column_ref.shape[1]
    rows = column_ref.shape[1]
    members = update_out.shape[0]
    me_s = lax.axis_index("space")
    me_e = lax.axis_index("ens")
    mesh_id = pl.DeviceIdType.MESH

    barrier = pltpu.get_barrier_semaphore()
    for e in range(groups):
        @pl.when(me_e != e)
        def _():
            pl.semaphore_signal(barrier, 1, device_id=(me_s, e), device_id_type=mesh_id)
    pl.semaphore_wait(barrier, groups - 1)

    def upd_copy(e, source_e):
        return pltpu.make_async_remote_copy(
            src_ref=column_ref.at[pl.ds(e * members, members)],
            dst_ref=update_out.at[:, pl.ds(source_e * rows, rows)],
            send_sem=upd_send.at[e],
            recv_sem=upd_recv.at[source_e],
            device_id=(me_s, e),
            device_id_type=mesh_id,
        )

    keep_upd = pltpu.make_async_copy(
        column_ref.at[pl.ds(me_e * members, members)],
        update_out.at[:, pl.ds(me_e * rows, rows)],
        local_sem,
    )
    for e in range(groups):
        @pl.when(me_e != e)
        def _():
            upd_copy(e, me_e).start()
    keep_upd.start()
    keep_upd.wait()
    for e in range(groups):
        @pl.when(me_e != e)
        def _():
            upd_copy(e, me_e).wait_send()
            upd_copy(e, e).wait_recv()


def send_back(column, slab_rows):
    total, rows, across = column.shape
    groups = slab_rows // rows
    members = total // groups
    anywhere = pl.BlockSpec(memory_space=pl.ANY)
    return pl.pallas_call(
        return_kernel,
        out_shape=jax.ShapeDtypeStruct((members, slab_rows, across), jnp.float32),
        in_specs=[anywhere],
        out_specs=anywhere,
        scratch_shapes=[
            pltpu.SemaphoreType.DMA((groups,)),
            pltpu.SemaphoreType.DMA((groups,)),
            pltpu.SemaphoreType.DMA,
        ],
        compiler_params=pltpu.CompilerParams(collective_id=2, has_side_effects=True),
    )(column)


def gather_grid(slab, n_space, n_ens):
    rows = n_space // 2
    me_s = lax.axis_index("space")
    z, half = me_s // 2, me_s % 2
    pieces = [(slab, me_s)]
    for flip in (0, 1):
        for dz in range(1 - flip, rows):
            pairs = []
            for s in range(n_space):
                zs, hs = s // 2, s % 2
                t = ((zs + dz) % rows) * 2 + (hs ^ flip)
                for e in range(n_ens):
                    pairs.append((s * n_ens + e, t * n_ens + (e ^ (2 * flip))))
            got = lax.ppermute(slab, ("space", "ens"), pairs)
            pieces.append((got, ((z - dz) % rows) * 2 + (half ^ flip)))
    thick = slab.shape[0]
    grid = jnp.zeros((n_space * thick,) + slab.shape[1:], slab.dtype)
    for got, source in pieces:
        grid = lax.dynamic_update_slice_in_dim(grid, got, source * thick, axis=0)
    return grid


def shards(
    log_perm,
    storage,
    head_init,
    well_cells,
    well_rates,
    obs_cells,
    obs_values,
    noise_var,
    step_size,
    perturb,
):
    members, planes, depth, across = log_perm.shape
    n_space = lax.axis_size("space")
    n_ens = lax.axis_size("ens")
    cell_count = planes * depth * across
    total_members = members * n_ens
    grid_planes = planes * n_space

    whole_log = lax.all_to_all(log_perm, "space", 0, 1, tiled=True)
    both_grids = gather_grid(jnp.stack([storage, head_init], axis=1), n_space, n_ens)
    whole_storage, whole_head = both_grids[:, 0], both_grids[:, 1]
    source = (
        jnp.zeros((grid_planes * depth * across,), jnp.float32)
        .at[well_cells]
        .add(well_rates)
        .reshape(grid_planes, depth, across)
    )
    forcing = whole_storage * whole_head + source
    slab_rows = planes * depth
    by_rows = log_perm.reshape(members, slab_rows, across)
    field, band = forward_pallas(
        whole_log[0], whole_storage, whole_head, forcing, by_rows, n_ens
    )
    picked = field.reshape(-1)[obs_cells]
    head_field = lax.all_to_all(field[None], "space", 1, 0, tiled=True)

    obs_count = picked.shape[0]
    own_perturb = lax.dynamic_index_in_dim(perturb, lax.axis_index("space"), 0, keepdims=False)
    row = jnp.zeros((1, 8, 128), jnp.float32)
    row = row.at[0, 0, :obs_count].set(picked).at[0, 0, obs_count : 2 * obs_count].set(own_perturb)
    rows = gather_rows(row, total_members)
    every_obs = rows[:, 0, :obs_count]
    every_perturb = rows[:, 0, obs_count : 2 * obs_count]
    mean_obs = jnp.mean(every_obs, axis=0)
    spread = every_obs - mean_obs
    covariance = jnp.dot(spread.T, spread, precision=HIGHEST) / (total_members - 1)
    system = covariance + jnp.diag(noise_var / step_size[0])
    factor_lower = jnp.linalg.cholesky(system)
    gain_rows = solve_pair(factor_lower, obs_values[None, :] + every_perturb - every_obs)
    mixing = jnp.dot(gain_rows, spread.T, precision=HIGHEST)

    change = jnp.einsum("jk,kry->jry", mixing, band, precision=HIGHEST)
    new_band = band + change / (total_members - 1)
    updated = send_back(new_band, slab_rows)
    updated = updated.reshape(log_perm.shape)
    return (head_field, updated)


def solution(mesh):
    return jax.shard_map(
        shards,
        mesh=mesh,
        in_specs=(
            P("ens", "space", None, None),
            P("space", None, None),
            P("space", None, None),
            P(),
            P(),
            P(),
            P(),
            P(),
            P(),
            P("ens", None),
        ),
        out_specs=(P("ens", "space", None, None), P("ens", "space", None, None)),
        check_vma=False,
    )
```

```python
import jax
from jax.experimental import pallas as pl
from jax.experimental.pallas import tpu as pltpu
import jax.numpy as jnp
from jax import lax
from jax.sharding import PartitionSpec as P

SWEEPS = 3


OMEGA = 0.8
HIGHEST = lax.Precision.HIGHEST
DIRECTIONS = [
    (a, b, c) for a in (-1, 0, 1) for b in (-1, 0, 1) for c in (-1, 0, 1) if (a, b, c) != (0, 0, 0)
]


def shifted(padded, a, b, c, planes, depth, across):
    return padded[..., 1 + a : 1 + a + planes, 1 + b : 1 + b + depth, 1 + c : 1 + c + across]


def solve_pair(factor, residual):
    first = lax.linalg.triangular_solve(factor, residual.T, left_side=True, lower=True)
    second = lax.linalg.triangular_solve(
        factor, first, left_side=True, lower=True, transpose_a=True
    )
    return second.T


HALF = [(a, b, c) for a, b, c in DIRECTIONS if (a, b, c) > (0, 0, 0)]


def shift_plane(x, b, c):
    depth, across = x.shape
    valid = None
    if b != 0:
        x = pltpu.roll(x, (-b) % depth, 0)
        rows = lax.broadcasted_iota(jnp.int32, x.shape, 0) + b
        valid = (rows >= 0) & (rows < depth)
    if c != 0:
        x = pltpu.roll(x, (-c) % across, 1)
        cols = lax.broadcasted_iota(jnp.int32, x.shape, 1) + c
        ok = (cols >= 0) & (cols < across)
        valid = ok if valid is None else valid & ok
    if valid is None:
        return x
    return jnp.where(valid, x, 0.0)


def forward_kernel(
    log_ref, sto_ref, init_ref, forc_ref, rows_ref, out_ref, band_ref,
    perm, trans, diag, head_a, head_b, band_send, band_recv, local_sem,
):
    planes, depth, across = log_ref.shape
    members, slab_rows, _ = rows_ref.shape
    groups = band_ref.shape[0] // members
    rows = slab_rows // groups
    me_s = lax.axis_index("space")
    me_e = lax.axis_index("ens")
    mesh_id = pl.DeviceIdType.MESH
    barrier = pltpu.get_barrier_semaphore()
    for e in range(groups):
        @pl.when(me_e != e)
        def _():
            pl.semaphore_signal(barrier, 1, device_id=(me_s, e), device_id_type=mesh_id)

    def band_copy(e, source_e):
        return pltpu.make_async_remote_copy(
            src_ref=rows_ref.at[:, pl.ds(e * rows, rows)],
            dst_ref=band_ref.at[pl.ds(source_e * members, members)],
            send_sem=band_send.at[e],
            recv_sem=band_recv.at[source_e],
            device_id=(me_s, e),
            device_id_type=mesh_id,
        )

    keep_band = pltpu.make_async_copy(
        rows_ref.at[:, pl.ds(me_e * rows, rows)],
        band_ref.at[pl.ds(me_e * members, members)],
        local_sem,
    )
    zero = jnp.zeros((depth, across), jnp.float32)
    for buf in (perm, head_a, head_b):
        buf[0] = zero
        buf[planes + 1] = zero

    def fill(p, carry):
        perm[p + 1] = jnp.exp(log_ref[p])
        head_a[p + 1] = init_ref[p]
        return carry

    lax.fori_loop(0, planes, fill, 0)

    def transmissibility(p, carry):
        own = perm[p + 1]
        for k, (a, b, c) in enumerate(HALF):
            factor = 2.0 ** (1 - abs(a) - abs(b) - abs(c))
            other = shift_plane(perm[p + 1 + a], b, c)
            trans[k, p] = factor * 2.0 * own * other / (own + other)
        return carry

    lax.fori_loop(0, planes, transmissibility, 0)

    pl.semaphore_wait(barrier, groups - 1)
    for e in range(groups):
        @pl.when(me_e != e)
        def _():
            band_copy(e, me_e).start()
    keep_band.start()

    def diagonal(p, carry):
        total = sto_ref[p]
        for k, (a, b, c) in enumerate(HALF):
            back = p - a
            inside = (back >= 0) & (back < planes)
            behind = shift_plane(trans[k, jnp.clip(back, 0, planes - 1)], -b, -c)
            total = total + trans[k, p] + jnp.where(inside, behind, 0.0)
        diag[p] = total
        return carry

    lax.fori_loop(0, planes, diagonal, 0)

    def sweep(source, target, padded_target):
        def body(p, carry):
            gathered = None
            for k, (a, b, c) in enumerate(HALF):
                ahead = trans[k, p] * shift_plane(source[p + 1 + a], b, c)
                back = jnp.clip(p - a, 0, planes - 1)
                flow = shift_plane(trans[k, back] * source[p + 1 - a], -b, -c)
                term = ahead + flow
                gathered = term if gathered is None else gathered + term
            value = (1.0 - OMEGA) * source[p + 1] + OMEGA * (forc_ref[p] + gathered) / diag[p]
            if padded_target:
                target[p + 1] = value
            else:
                target[p] = value
            return carry

        lax.fori_loop(0, planes, body, 0)

    sweep(head_a, head_b, True)
    sweep(head_b, head_a, True)
    sweep(head_a, out_ref, False)
    keep_band.wait()
    for e in range(groups):
        @pl.when(me_e != e)
        def _():
            band_copy(e, me_e).wait_send()
            band_copy(e, e).wait_recv()


def forward_pallas(log_row, storage, head_init, forcing, by_rows, groups):
    planes, depth, across = log_row.shape
    members, slab_rows, _ = by_rows.shape
    vmem = pl.BlockSpec(memory_space=pltpu.VMEM)
    anywhere = pl.BlockSpec(memory_space=pl.ANY)
    return pl.pallas_call(
        forward_kernel,
        out_shape=(
            jax.ShapeDtypeStruct((planes, depth, across), jnp.float32),
            jax.ShapeDtypeStruct((members * groups, slab_rows // groups, across), jnp.float32),
        ),
        in_specs=[vmem] * 4 + [anywhere],
        out_specs=(vmem, anywhere),
        scratch_shapes=[
            pltpu.VMEM((planes + 2, depth, across), jnp.float32),
            pltpu.VMEM((len(HALF), planes, depth, across), jnp.float32),
            pltpu.VMEM((planes, depth, across), jnp.float32),
            pltpu.VMEM((planes + 2, depth, across), jnp.float32),
            pltpu.VMEM((planes + 2, depth, across), jnp.float32),
            pltpu.SemaphoreType.DMA((groups,)),
            pltpu.SemaphoreType.DMA((groups,)),
            pltpu.SemaphoreType.DMA,
        ],
        compiler_params=pltpu.CompilerParams(
            vmem_limit_bytes=66 * 1024 * 1024, collective_id=3, has_side_effects=True
        ),
    )(log_row, storage, head_init, forcing, by_rows)


def gather_kernel(row_ref, out_ref, landing, send_sem, recv_sem):
    total = landing.shape[0]
    n_space = lax.axis_size("space")
    me_s = lax.axis_index("space")
    me_e = lax.axis_index("ens")
    mine = me_e * n_space + me_s
    mesh_id = pl.DeviceIdType.MESH

    barrier = pltpu.get_barrier_semaphore()

    def greet(i, carry):
        @pl.when(i != mine)
        def _():
            pl.semaphore_signal(
                barrier, 1, device_id=(i % n_space, i // n_space), device_id_type=mesh_id
            )

        return carry

    lax.fori_loop(0, total, greet, 0)
    pl.semaphore_wait(barrier, total - 1)

    def send(i, carry):
        @pl.when(i != mine)
        def _():
            pltpu.make_async_remote_copy(
                src_ref=row_ref,
                dst_ref=landing.at[pl.ds(mine, 1)],
                send_sem=send_sem,
                recv_sem=recv_sem,
                device_id=(i % n_space, i // n_space),
                device_id_type=mesh_id,
            ).start()

        return carry

    lax.fori_loop(0, total, send, 0)
    landing[pl.ds(mine, 1)] = row_ref[...]
    partner = (mine + 1) % total
    everything = pltpu.make_async_remote_copy(
        src_ref=landing.at[pl.ds(0, total - 1)],
        dst_ref=landing.at[pl.ds(1, total - 1)],
        send_sem=send_sem,
        recv_sem=recv_sem,
        device_id=(partner % n_space, partner // n_space),
        device_id_type=mesh_id,
    )
    everything.wait_send()
    everything.wait_recv()
    out_ref[...] = landing[...]


def gather_rows(row, total):
    vmem = pl.BlockSpec(memory_space=pltpu.VMEM)
    return pl.pallas_call(
        gather_kernel,
        out_shape=jax.ShapeDtypeStruct((total,) + row.shape[1:], jnp.float32),
        in_specs=[vmem],
        out_specs=vmem,
        scratch_shapes=[
            pltpu.VMEM((total,) + row.shape[1:], jnp.float32),
            pltpu.SemaphoreType.DMA,
            pltpu.SemaphoreType.DMA,
        ],
        compiler_params=pltpu.CompilerParams(collective_id=1, has_side_effects=True),
    )(row)


def return_kernel(column_ref, update_out, upd_send, upd_recv, local_sem):
    groups = update_out.shape[1] // column_ref.shape[1]
    rows = column_ref.shape[1]
    members = update_out.shape[0]
    me_s = lax.axis_index("space")
    me_e = lax.axis_index("ens")
    mesh_id = pl.DeviceIdType.MESH

    barrier = pltpu.get_barrier_semaphore()
    for e in range(groups):
        @pl.when(me_e != e)
        def _():
            pl.semaphore_signal(barrier, 1, device_id=(me_s, e), device_id_type=mesh_id)
    pl.semaphore_wait(barrier, groups - 1)

    def upd_copy(e, source_e):
        return pltpu.make_async_remote_copy(
            src_ref=column_ref.at[pl.ds(e * members, members)],
            dst_ref=update_out.at[:, pl.ds(source_e * rows, rows)],
            send_sem=upd_send.at[e],
            recv_sem=upd_recv.at[source_e],
            device_id=(me_s, e),
            device_id_type=mesh_id,
        )

    keep_upd = pltpu.make_async_copy(
        column_ref.at[pl.ds(me_e * members, members)],
        update_out.at[:, pl.ds(me_e * rows, rows)],
        local_sem,
    )
    for e in range(groups):
        @pl.when(me_e != e)
        def _():
            upd_copy(e, me_e).start()
    keep_upd.start()
    keep_upd.wait()
    for e in range(groups):
        @pl.when(me_e != e)
        def _():
            upd_copy(e, me_e).wait_send()
            upd_copy(e, e).wait_recv()


def send_back(column, slab_rows):
    total, rows, across = column.shape
    groups = slab_rows // rows
    members = total // groups
    anywhere = pl.BlockSpec(memory_space=pl.ANY)
    return pl.pallas_call(
        return_kernel,
        out_shape=jax.ShapeDtypeStruct((members, slab_rows, across), jnp.float32),
        in_specs=[anywhere],
        out_specs=anywhere,
        scratch_shapes=[
            pltpu.SemaphoreType.DMA((groups,)),
            pltpu.SemaphoreType.DMA((groups,)),
            pltpu.SemaphoreType.DMA,
        ],
        compiler_params=pltpu.CompilerParams(collective_id=2, has_side_effects=True),
    )(column)


def gather_grid(slab, n_space, n_ens):
    rows = n_space // 2
    me_s = lax.axis_index("space")
    z, half = me_s // 2, me_s % 2
    pieces = [(slab, me_s)]
    for flip in (0, 1):
        for dz in range(1 - flip, rows):
            pairs = []
            for s in range(n_space):
                zs, hs = s // 2, s % 2
                t = ((zs + dz) % rows) * 2 + (hs ^ flip)
                for e in range(n_ens):
                    pairs.append((s * n_ens + e, t * n_ens + (e ^ (2 * flip))))
            got = lax.ppermute(slab, ("space", "ens"), pairs)
            pieces.append((got, ((z - dz) % rows) * 2 + (half ^ flip)))
    thick = slab.shape[0]
    grid = jnp.zeros((n_space * thick,) + slab.shape[1:], slab.dtype)
    for got, source in pieces:
        grid = lax.dynamic_update_slice_in_dim(grid, got, source * thick, axis=0)
    return grid


def particle_kernel(log_ref, whole_ref, send_sems, recv_sems, local_sem):
    slabs, thick = log_ref.shape[0], log_ref.shape[1]
    me_s = lax.axis_index("space")
    me_e = lax.axis_index("ens")
    mesh_id = pl.DeviceIdType.MESH
    barrier = pltpu.get_barrier_semaphore()
    for s in range(slabs):
        @pl.when(me_s != s)
        def _():
            pl.semaphore_signal(barrier, 1, device_id=(s, me_e), device_id_type=mesh_id)
    pl.semaphore_wait(barrier, slabs - 1)

    def send(t, source_s):
        return pltpu.make_async_remote_copy(
            src_ref=log_ref.at[t],
            dst_ref=whole_ref.at[pl.ds(source_s * thick, thick)],
            send_sem=send_sems.at[t],
            recv_sem=recv_sems.at[source_s],
            device_id=(t, me_e),
            device_id_type=mesh_id,
        )

    keep = pltpu.make_async_copy(
        log_ref.at[me_s], whole_ref.at[pl.ds(me_s * thick, thick)], local_sem
    )
    for t in range(slabs):
        @pl.when(me_s != t)
        def _():
            send(t, me_s).start()
    keep.start()
    keep.wait()
    for t in range(slabs):
        @pl.when(me_s != t)
        def _():
            send(t, me_s).wait_send()
            send(t, t).wait_recv()


def gather_particle(log_perm):
    slabs, thick, depth, across = log_perm.shape
    anywhere = pl.BlockSpec(memory_space=pl.ANY)
    return pl.pallas_call(
        particle_kernel,
        out_shape=jax.ShapeDtypeStruct((slabs * thick, depth, across), jnp.float32),
        in_specs=[anywhere],
        out_specs=anywhere,
        scratch_shapes=[
            pltpu.SemaphoreType.DMA((slabs,)),
            pltpu.SemaphoreType.DMA((slabs,)),
            pltpu.SemaphoreType.DMA,
        ],
        compiler_params=pltpu.CompilerParams(collective_id=4, has_side_effects=True),
    )(log_perm)


def shards(
    log_perm,
    storage,
    head_init,
    well_cells,
    well_rates,
    obs_cells,
    obs_values,
    noise_var,
    step_size,
    perturb,
):
    members, planes, depth, across = log_perm.shape
    n_space = lax.axis_size("space")
    n_ens = lax.axis_size("ens")
    cell_count = planes * depth * across
    total_members = members * n_ens
    grid_planes = planes * n_space

    whole_log = gather_particle(log_perm)
    core = lax.axis_index("ens") % 2
    mine = gather_grid(jnp.where(core == 0, storage, head_init), n_space, n_ens)
    pairs = [(e, e ^ 1) for e in range(n_ens)]
    other = lax.ppermute(mine, "ens", pairs)
    whole_storage = jnp.where(core == 0, mine, other)
    whole_head = jnp.where(core == 0, other, mine)
    source = (
        jnp.zeros((grid_planes * depth * across,), jnp.float32)
        .at[well_cells]
        .add(well_rates)
        .reshape(grid_planes, depth, across)
    )
    forcing = whole_storage * whole_head + source
    slab_rows = planes * depth
    by_rows = log_perm.reshape(members, slab_rows, across)
    field, band = forward_pallas(
        whole_log, whole_storage, whole_head, forcing, by_rows, n_ens
    )
    picked = field.reshape(-1)[obs_cells]
    head_field = lax.all_to_all(field[None], "space", 1, 0, tiled=True)

    obs_count = picked.shape[0]
    own_perturb = lax.dynamic_index_in_dim(perturb, lax.axis_index("space"), 0, keepdims=False)
    row = jnp.zeros((1, 8, 128), jnp.float32)
    row = row.at[0, 0, :obs_count].set(picked).at[0, 0, obs_count : 2 * obs_count].set(own_perturb)
    rows = gather_rows(row, total_members)
    every_obs = rows[:, 0, :obs_count]
    every_perturb = rows[:, 0, obs_count : 2 * obs_count]
    mean_obs = jnp.mean(every_obs, axis=0)
    spread = every_obs - mean_obs
    covariance = jnp.dot(spread.T, spread, precision=HIGHEST) / (total_members - 1)
    system = covariance + jnp.diag(noise_var / step_size[0])
    factor_lower = jnp.linalg.cholesky(system)
    gain_rows = solve_pair(factor_lower, obs_values[None, :] + every_perturb - every_obs)
    mixing = jnp.dot(gain_rows, spread.T, precision=HIGHEST)

    change = jnp.einsum("jk,kry->jry", mixing, band, precision=HIGHEST)
    new_band = band + change / (total_members - 1)
    updated = send_back(new_band, slab_rows)
    updated = updated.reshape(log_perm.shape)
    return (head_field, updated)


def solution(mesh):
    return jax.shard_map(
        shards,
        mesh=mesh,
        in_specs=(
            P("ens", "space", None, None),
            P("space", None, None),
            P("space", None, None),
            P(),
            P(),
            P(),
            P(),
            P(),
            P(),
            P("ens", None),
        ),
        out_specs=(P("ens", "space", None, None), P("ens", "space", None, None)),
        check_vma=False,
    )
```

```python
import jax
from jax.experimental import pallas as pl
from jax.experimental.pallas import tpu as pltpu
import jax.numpy as jnp
from jax import lax
from jax.sharding import PartitionSpec as P

SWEEPS = 3


OMEGA = 0.8
HIGHEST = lax.Precision.HIGHEST
DIRECTIONS = [
    (a, b, c) for a in (-1, 0, 1) for b in (-1, 0, 1) for c in (-1, 0, 1) if (a, b, c) != (0, 0, 0)
]


def shifted(padded, a, b, c, planes, depth, across):
    return padded[..., 1 + a : 1 + a + planes, 1 + b : 1 + b + depth, 1 + c : 1 + c + across]


def solve_pair(factor, residual):
    first = lax.linalg.triangular_solve(factor, residual.T, left_side=True, lower=True)
    second = lax.linalg.triangular_solve(
        factor, first, left_side=True, lower=True, transpose_a=True
    )
    return second.T


HALF = [(a, b, c) for a, b, c in DIRECTIONS if (a, b, c) > (0, 0, 0)]


def shift_plane(x, b, c):
    depth, across = x.shape
    valid = None
    if b != 0:
        x = pltpu.roll(x, (-b) % depth, 0)
        rows = lax.broadcasted_iota(jnp.int32, x.shape, 0) + b
        valid = (rows >= 0) & (rows < depth)
    if c != 0:
        x = pltpu.roll(x, (-c) % across, 1)
        cols = lax.broadcasted_iota(jnp.int32, x.shape, 1) + c
        ok = (cols >= 0) & (cols < across)
        valid = ok if valid is None else valid & ok
    if valid is None:
        return x
    return jnp.where(valid, x, 0.0)


def roll_plane(x, b, c):
    depth, across = x.shape
    if b != 0:
        x = pltpu.roll(x, (-b) % depth, 0)
    if c != 0:
        x = pltpu.roll(x, (-c) % across, 1)
    return x


def forward_kernel(
    log_ref, sto_ref, init_ref, forc_ref, rows_ref, out_ref, band_ref,
    perm, trans, diag, head_a, head_b, band_send, band_recv, local_sem,
):
    planes, depth, across = log_ref.shape
    members, slab_rows, _ = rows_ref.shape
    groups = band_ref.shape[0] // members
    rows = slab_rows // groups
    me_s = lax.axis_index("space")
    me_e = lax.axis_index("ens")
    mesh_id = pl.DeviceIdType.MESH
    barrier = pltpu.get_barrier_semaphore()
    for e in range(groups):
        @pl.when(me_e != e)
        def _():
            pl.semaphore_signal(barrier, 1, device_id=(me_s, e), device_id_type=mesh_id)

    def band_copy(e, source_e):
        return pltpu.make_async_remote_copy(
            src_ref=rows_ref.at[:, pl.ds(e * rows, rows)],
            dst_ref=band_ref.at[pl.ds(source_e * members, members)],
            send_sem=band_send.at[e],
            recv_sem=band_recv.at[source_e],
            device_id=(me_s, e),
            device_id_type=mesh_id,
        )

    keep_band = pltpu.make_async_copy(
        rows_ref.at[:, pl.ds(me_e * rows, rows)],
        band_ref.at[pl.ds(me_e * members, members)],
        local_sem,
    )
    zero = jnp.zeros((depth, across), jnp.float32)
    for buf in (perm, head_a, head_b):
        buf[0] = zero
        buf[planes + 1] = zero

    def fill(p, carry):
        perm[p + 1] = jnp.exp(log_ref[p])
        head_a[p + 1] = init_ref[p]
        return carry

    lax.fori_loop(0, planes, fill, 0)

    def transmissibility(p, carry):
        own = perm[p + 1]
        for k, (a, b, c) in enumerate(HALF):
            factor = 2.0 ** (1 - abs(a) - abs(b) - abs(c))
            other = shift_plane(perm[p + 1 + a], b, c)
            trans[k, p] = factor * 2.0 * own * other / (own + other)
        return carry

    lax.fori_loop(0, planes, transmissibility, 0)

    pl.semaphore_wait(barrier, groups - 1)
    for e in range(groups):
        @pl.when(me_e != e)
        def _():
            band_copy(e, me_e).start()
    keep_band.start()

    def diagonal(p, carry):
        total = sto_ref[p]
        for k, (a, b, c) in enumerate(HALF):
            back = p - a
            inside = (back >= 0) & (back < planes)
            behind = roll_plane(trans[k, jnp.clip(back, 0, planes - 1)], -b, -c)
            total = total + trans[k, p] + jnp.where(inside, behind, 0.0)
        diag[p] = total
        return carry

    lax.fori_loop(0, planes, diagonal, 0)

    def sweep(source, target, padded_target):
        def body(p, carry):
            gathered = None
            for k, (a, b, c) in enumerate(HALF):
                ahead = trans[k, p] * roll_plane(source[p + 1 + a], b, c)
                back = jnp.clip(p - a, 0, planes - 1)
                flow = roll_plane(trans[k, back] * source[p + 1 - a], -b, -c)
                term = ahead + flow
                gathered = term if gathered is None else gathered + term
            value = (1.0 - OMEGA) * source[p + 1] + OMEGA * (forc_ref[p] + gathered) / diag[p]
            if padded_target:
                target[p + 1] = value
            else:
                target[p] = value
            return carry

        lax.fori_loop(0, planes, body, 0)

    sweep(head_a, head_b, True)
    sweep(head_b, head_a, True)
    sweep(head_a, out_ref, False)
    keep_band.wait()
    for e in range(groups):
        @pl.when(me_e != e)
        def _():
            band_copy(e, me_e).wait_send()
            band_copy(e, e).wait_recv()


def forward_pallas(log_row, storage, head_init, forcing, by_rows, groups):
    planes, depth, across = log_row.shape
    members, slab_rows, _ = by_rows.shape
    vmem = pl.BlockSpec(memory_space=pltpu.VMEM)
    anywhere = pl.BlockSpec(memory_space=pl.ANY)
    return pl.pallas_call(
        forward_kernel,
        out_shape=(
            jax.ShapeDtypeStruct((planes, depth, across), jnp.float32),
            jax.ShapeDtypeStruct((members * groups, slab_rows // groups, across), jnp.float32),
        ),
        in_specs=[vmem] * 4 + [anywhere],
        out_specs=(vmem, anywhere),
        scratch_shapes=[
            pltpu.VMEM((planes + 2, depth, across), jnp.float32),
            pltpu.VMEM((len(HALF), planes, depth, across), jnp.float32),
            pltpu.VMEM((planes, depth, across), jnp.float32),
            pltpu.VMEM((planes + 2, depth, across), jnp.float32),
            pltpu.VMEM((planes + 2, depth, across), jnp.float32),
            pltpu.SemaphoreType.DMA((groups,)),
            pltpu.SemaphoreType.DMA((groups,)),
            pltpu.SemaphoreType.DMA,
        ],
        compiler_params=pltpu.CompilerParams(
            vmem_limit_bytes=66 * 1024 * 1024, collective_id=3, has_side_effects=True
        ),
    )(log_row, storage, head_init, forcing, by_rows)


def gather_kernel(row_ref, out_ref, landing, send_sem, recv_sem):
    total = landing.shape[0]
    n_space = lax.axis_size("space")
    me_s = lax.axis_index("space")
    me_e = lax.axis_index("ens")
    mine = me_e * n_space + me_s
    mesh_id = pl.DeviceIdType.MESH

    barrier = pltpu.get_barrier_semaphore()

    def greet(i, carry):
        @pl.when(i != mine)
        def _():
            pl.semaphore_signal(
                barrier, 1, device_id=(i % n_space, i // n_space), device_id_type=mesh_id
            )

        return carry

    lax.fori_loop(0, total, greet, 0)
    pl.semaphore_wait(barrier, total - 1)

    def send(i, carry):
        @pl.when(i != mine)
        def _():
            pltpu.make_async_remote_copy(
                src_ref=row_ref,
                dst_ref=landing.at[pl.ds(mine, 1)],
                send_sem=send_sem,
                recv_sem=recv_sem,
                device_id=(i % n_space, i // n_space),
                device_id_type=mesh_id,
            ).start()

        return carry

    lax.fori_loop(0, total, send, 0)
    landing[pl.ds(mine, 1)] = row_ref[...]
    partner = (mine + 1) % total
    everything = pltpu.make_async_remote_copy(
        src_ref=landing.at[pl.ds(0, total - 1)],
        dst_ref=landing.at[pl.ds(1, total - 1)],
        send_sem=send_sem,
        recv_sem=recv_sem,
        device_id=(partner % n_space, partner // n_space),
        device_id_type=mesh_id,
    )
    everything.wait_send()
    everything.wait_recv()
    out_ref[...] = landing[...]


def gather_rows(row, total):
    vmem = pl.BlockSpec(memory_space=pltpu.VMEM)
    return pl.pallas_call(
        gather_kernel,
        out_shape=jax.ShapeDtypeStruct((total,) + row.shape[1:], jnp.float32),
        in_specs=[vmem],
        out_specs=vmem,
        scratch_shapes=[
            pltpu.VMEM((total,) + row.shape[1:], jnp.float32),
            pltpu.SemaphoreType.DMA,
            pltpu.SemaphoreType.DMA,
        ],
        compiler_params=pltpu.CompilerParams(collective_id=1, has_side_effects=True),
    )(row)


def return_kernel(column_ref, update_out, upd_send, upd_recv, local_sem):
    groups = update_out.shape[1] // column_ref.shape[1]
    rows = column_ref.shape[1]
    members = update_out.shape[0]
    me_s = lax.axis_index("space")
    me_e = lax.axis_index("ens")
    mesh_id = pl.DeviceIdType.MESH

    barrier = pltpu.get_barrier_semaphore()
    for e in range(groups):
        @pl.when(me_e != e)
        def _():
            pl.semaphore_signal(barrier, 1, device_id=(me_s, e), device_id_type=mesh_id)
    pl.semaphore_wait(barrier, groups - 1)

    def upd_copy(e, source_e):
        return pltpu.make_async_remote_copy(
            src_ref=column_ref.at[pl.ds(e * members, members)],
            dst_ref=update_out.at[:, pl.ds(source_e * rows, rows)],
            send_sem=upd_send.at[e],
            recv_sem=upd_recv.at[source_e],
            device_id=(me_s, e),
            device_id_type=mesh_id,
        )

    keep_upd = pltpu.make_async_copy(
        column_ref.at[pl.ds(me_e * members, members)],
        update_out.at[:, pl.ds(me_e * rows, rows)],
        local_sem,
    )
    for e in range(groups):
        @pl.when(me_e != e)
        def _():
            upd_copy(e, me_e).start()
    keep_upd.start()
    keep_upd.wait()
    for e in range(groups):
        @pl.when(me_e != e)
        def _():
            upd_copy(e, me_e).wait_send()
            upd_copy(e, e).wait_recv()


def send_back(column, slab_rows):
    total, rows, across = column.shape
    groups = slab_rows // rows
    members = total // groups
    anywhere = pl.BlockSpec(memory_space=pl.ANY)
    return pl.pallas_call(
        return_kernel,
        out_shape=jax.ShapeDtypeStruct((members, slab_rows, across), jnp.float32),
        in_specs=[anywhere],
        out_specs=anywhere,
        scratch_shapes=[
            pltpu.SemaphoreType.DMA((groups,)),
            pltpu.SemaphoreType.DMA((groups,)),
            pltpu.SemaphoreType.DMA,
        ],
        compiler_params=pltpu.CompilerParams(collective_id=2, has_side_effects=True),
    )(column)


def gather_grid(slab, n_space, n_ens):
    rows = n_space // 2
    me_s = lax.axis_index("space")
    z, half = me_s // 2, me_s % 2
    pieces = [(slab, me_s)]
    for flip in (0, 1):
        for dz in range(1 - flip, rows):
            pairs = []
            for s in range(n_space):
                zs, hs = s // 2, s % 2
                t = ((zs + dz) % rows) * 2 + (hs ^ flip)
                for e in range(n_ens):
                    pairs.append((s * n_ens + e, t * n_ens + (e ^ (2 * flip))))
            got = lax.ppermute(slab, ("space", "ens"), pairs)
            pieces.append((got, ((z - dz) % rows) * 2 + (half ^ flip)))
    thick = slab.shape[0]
    grid = jnp.zeros((n_space * thick,) + slab.shape[1:], slab.dtype)
    for got, source in pieces:
        grid = lax.dynamic_update_slice_in_dim(grid, got, source * thick, axis=0)
    return grid


def shards(
    log_perm,
    storage,
    head_init,
    well_cells,
    well_rates,
    obs_cells,
    obs_values,
    noise_var,
    step_size,
    perturb,
):
    members, planes, depth, across = log_perm.shape
    n_space = lax.axis_size("space")
    n_ens = lax.axis_size("ens")
    cell_count = planes * depth * across
    total_members = members * n_ens
    grid_planes = planes * n_space

    whole_log = lax.all_to_all(log_perm, "space", 0, 1, tiled=True)
    core = lax.axis_index("ens") % 2
    mine = gather_grid(jnp.where(core == 0, storage, head_init), n_space, n_ens)
    pairs = [(e, e ^ 1) for e in range(n_ens)]
    other = lax.ppermute(mine, "ens", pairs)
    whole_storage = jnp.where(core == 0, mine, other)
    whole_head = jnp.where(core == 0, other, mine)
    source = (
        jnp.zeros((grid_planes * depth * across,), jnp.float32)
        .at[well_cells]
        .add(well_rates)
        .reshape(grid_planes, depth, across)
    )
    forcing = whole_storage * whole_head + source
    slab_rows = planes * depth
    by_rows = log_perm.reshape(members, slab_rows, across)
    field, band = forward_pallas(
        whole_log[0], whole_storage, whole_head, forcing, by_rows, n_ens
    )
    picked = field.reshape(-1)[obs_cells]
    head_field = lax.all_to_all(field[None], "space", 1, 0, tiled=True)

    obs_count = picked.shape[0]
    own_perturb = lax.dynamic_index_in_dim(perturb, lax.axis_index("space"), 0, keepdims=False)
    row = jnp.zeros((1, 8, 128), jnp.float32)
    row = row.at[0, 0, :obs_count].set(picked).at[0, 0, obs_count : 2 * obs_count].set(own_perturb)
    rows = gather_rows(row, total_members)
    every_obs = rows[:, 0, :obs_count]
    every_perturb = rows[:, 0, obs_count : 2 * obs_count]
    mean_obs = jnp.mean(every_obs, axis=0)
    spread = every_obs - mean_obs
    covariance = jnp.dot(spread.T, spread, precision=HIGHEST) / (total_members - 1)
    system = covariance + jnp.diag(noise_var / step_size[0])
    factor_lower = jnp.linalg.cholesky(system)
    gain_rows = solve_pair(factor_lower, obs_values[None, :] + every_perturb - every_obs)
    mixing = jnp.dot(gain_rows, spread.T, precision=HIGHEST)

    change = jnp.einsum("jk,kry->jry", mixing, band, precision=HIGHEST)
    new_band = band + change / (total_members - 1)
    updated = send_back(new_band, slab_rows)
    updated = updated.reshape(log_perm.shape)
    return (head_field, updated)


def solution(mesh):
    return jax.shard_map(
        shards,
        mesh=mesh,
        in_specs=(
            P("ens", "space", None, None),
            P("space", None, None),
            P("space", None, None),
            P(),
            P(),
            P(),
            P(),
            P(),
            P(),
            P("ens", None),
        ),
        out_specs=(P("ens", "space", None, None), P("ens", "space", None, None)),
        check_vma=False,
    )
```

```python
import jax
from jax.experimental import pallas as pl
from jax.experimental.pallas import tpu as pltpu
import jax.numpy as jnp
from jax import lax
from jax.sharding import PartitionSpec as P

SWEEPS = 3


OMEGA = 0.8
HIGHEST = lax.Precision.HIGHEST
DIRECTIONS = [
    (a, b, c) for a in (-1, 0, 1) for b in (-1, 0, 1) for c in (-1, 0, 1) if (a, b, c) != (0, 0, 0)
]


def shifted(padded, a, b, c, planes, depth, across):
    return padded[..., 1 + a : 1 + a + planes, 1 + b : 1 + b + depth, 1 + c : 1 + c + across]


def solve_pair(factor, residual):
    first = lax.linalg.triangular_solve(factor, residual.T, left_side=True, lower=True)
    second = lax.linalg.triangular_solve(
        factor, first, left_side=True, lower=True, transpose_a=True
    )
    return second.T


HALF = [(a, b, c) for a, b, c in DIRECTIONS if (a, b, c) > (0, 0, 0)]


def shift_plane(x, b, c):
    depth, across = x.shape
    valid = None
    if b != 0:
        x = pltpu.roll(x, (-b) % depth, 0)
        rows = lax.broadcasted_iota(jnp.int32, x.shape, 0) + b
        valid = (rows >= 0) & (rows < depth)
    if c != 0:
        x = pltpu.roll(x, (-c) % across, 1)
        cols = lax.broadcasted_iota(jnp.int32, x.shape, 1) + c
        ok = (cols >= 0) & (cols < across)
        valid = ok if valid is None else valid & ok
    if valid is None:
        return x
    return jnp.where(valid, x, 0.0)


def roll_plane(x, b, c):
    depth, across = x.shape
    if b != 0:
        x = pltpu.roll(x, (-b) % depth, 0)
    if c != 0:
        x = pltpu.roll(x, (-c) % across, 1)
    return x


def forward_kernel(
    log_ref, sto_ref, init_ref, forc_ref, rows_ref, out_ref, band_ref,
    perm, trans, diag, head_a, head_b, band_send, band_recv, local_sem,
):
    planes, depth, across = log_ref.shape
    members, slab_rows, _ = rows_ref.shape
    groups = band_ref.shape[0] // members
    rows = slab_rows // groups
    me_s = lax.axis_index("space")
    me_e = lax.axis_index("ens")
    mesh_id = pl.DeviceIdType.MESH
    barrier = pltpu.get_barrier_semaphore()
    for e in range(groups):
        @pl.when(me_e != e)
        def _():
            pl.semaphore_signal(barrier, 1, device_id=(me_s, e), device_id_type=mesh_id)

    def band_copy(e, source_e):
        return pltpu.make_async_remote_copy(
            src_ref=rows_ref.at[:, pl.ds(e * rows, rows)],
            dst_ref=band_ref.at[pl.ds(source_e * members, members)],
            send_sem=band_send.at[e],
            recv_sem=band_recv.at[source_e],
            device_id=(me_s, e),
            device_id_type=mesh_id,
        )

    keep_band = pltpu.make_async_copy(
        rows_ref.at[:, pl.ds(me_e * rows, rows)],
        band_ref.at[pl.ds(me_e * members, members)],
        local_sem,
    )
    zero = jnp.zeros((depth, across), jnp.float32)
    for buf in (perm, head_a, head_b):
        buf[0] = zero
        buf[planes + 1] = zero

    def fill(p, carry):
        perm[p + 1] = jnp.exp(log_ref[p])
        head_a[p + 1] = init_ref[p]
        return carry

    lax.fori_loop(0, planes, fill, 0)

    def transmissibility(p, carry):
        own = perm[p + 1]
        for k, (a, b, c) in enumerate(HALF):
            factor = 2.0 ** (1 - abs(a) - abs(b) - abs(c))
            other = shift_plane(perm[p + 1 + a], b, c)
            trans[k, p] = factor * 2.0 * own * other / (own + other)
        return carry

    lax.fori_loop(0, planes, transmissibility, 0)

    pl.semaphore_wait(barrier, groups - 1)
    for e in range(groups):
        @pl.when(me_e != e)
        def _():
            band_copy(e, me_e).start()
    keep_band.start()

    def diagonal(p, carry):
        total = sto_ref[p]
        for k, (a, b, c) in enumerate(HALF):
            back = p - a
            inside = (back >= 0) & (back < planes)
            behind = roll_plane(trans[k, jnp.clip(back, 0, planes - 1)], -b, -c)
            total = total + trans[k, p] + jnp.where(inside, behind, 0.0)
        diag[p] = total
        return carry

    lax.fori_loop(0, planes, diagonal, 0)

    def sweep(source, target, padded_target):
        def body(p, carry):
            gathered = None
            for k, (a, b, c) in enumerate(HALF):
                ahead = trans[k, p] * roll_plane(source[p + 1 + a], b, c)
                back = jnp.clip(p - a, 0, planes - 1)
                flow = roll_plane(trans[k, back] * source[p + 1 - a], -b, -c)
                term = ahead + flow
                gathered = term if gathered is None else gathered + term
            value = (1.0 - OMEGA) * source[p + 1] + OMEGA * (forc_ref[p] + gathered) / diag[p]
            if padded_target:
                target[p + 1] = value
            else:
                target[p] = value
            return carry

        lax.fori_loop(0, planes, body, 0)

    sweep(head_a, head_b, True)
    sweep(head_b, head_a, True)
    sweep(head_a, out_ref, False)
    keep_band.wait()
    for e in range(groups):
        @pl.when(me_e != e)
        def _():
            band_copy(e, me_e).wait_send()
            band_copy(e, e).wait_recv()


def forward_pallas(log_row, storage, head_init, forcing, by_rows, groups):
    planes, depth, across = log_row.shape
    members, slab_rows, _ = by_rows.shape
    vmem = pl.BlockSpec(memory_space=pltpu.VMEM)
    anywhere = pl.BlockSpec(memory_space=pl.ANY)
    return pl.pallas_call(
        forward_kernel,
        out_shape=(
            jax.ShapeDtypeStruct((planes, depth, across), jnp.float32),
            jax.ShapeDtypeStruct((members * groups, slab_rows // groups, across), jnp.float32),
        ),
        in_specs=[vmem] * 4 + [anywhere],
        out_specs=(vmem, anywhere),
        scratch_shapes=[
            pltpu.VMEM((planes + 2, depth, across), jnp.float32),
            pltpu.VMEM((len(HALF), planes, depth, across), jnp.float32),
            pltpu.VMEM((planes, depth, across), jnp.float32),
            pltpu.VMEM((planes + 2, depth, across), jnp.float32),
            pltpu.VMEM((planes + 2, depth, across), jnp.float32),
            pltpu.SemaphoreType.DMA((groups,)),
            pltpu.SemaphoreType.DMA((groups,)),
            pltpu.SemaphoreType.DMA,
        ],
        compiler_params=pltpu.CompilerParams(
            vmem_limit_bytes=66 * 1024 * 1024, collective_id=3, has_side_effects=True
        ),
    )(log_row, storage, head_init, forcing, by_rows)


def gather_kernel(row_ref, out_ref, landing, send_sem, recv_sem):
    total = landing.shape[0]
    n_space = lax.axis_size("space")
    me_s = lax.axis_index("space")
    me_e = lax.axis_index("ens")
    mine = me_e * n_space + me_s
    mesh_id = pl.DeviceIdType.MESH

    barrier = pltpu.get_barrier_semaphore()

    def greet(i, carry):
        @pl.when(i != mine)
        def _():
            pl.semaphore_signal(
                barrier, 1, device_id=(i % n_space, i // n_space), device_id_type=mesh_id
            )

        return carry

    lax.fori_loop(0, total, greet, 0)
    pl.semaphore_wait(barrier, total - 1)

    def send(i, carry):
        @pl.when(i != mine)
        def _():
            pltpu.make_async_remote_copy(
                src_ref=row_ref,
                dst_ref=landing.at[pl.ds(mine, 1)],
                send_sem=send_sem,
                recv_sem=recv_sem,
                device_id=(i % n_space, i // n_space),
                device_id_type=mesh_id,
            ).start()

        return carry

    lax.fori_loop(0, total, send, 0)
    landing[pl.ds(mine, 1)] = row_ref[...]
    partner = (mine + 1) % total
    everything = pltpu.make_async_remote_copy(
        src_ref=landing.at[pl.ds(0, total - 1)],
        dst_ref=landing.at[pl.ds(1, total - 1)],
        send_sem=send_sem,
        recv_sem=recv_sem,
        device_id=(partner % n_space, partner // n_space),
        device_id_type=mesh_id,
    )
    everything.wait_send()
    everything.wait_recv()
    out_ref[...] = landing[...]


def gather_rows(row, total):
    vmem = pl.BlockSpec(memory_space=pltpu.VMEM)
    return pl.pallas_call(
        gather_kernel,
        out_shape=jax.ShapeDtypeStruct((total,) + row.shape[1:], jnp.float32),
        in_specs=[vmem],
        out_specs=vmem,
        scratch_shapes=[
            pltpu.VMEM((total,) + row.shape[1:], jnp.float32),
            pltpu.SemaphoreType.DMA,
            pltpu.SemaphoreType.DMA,
        ],
        compiler_params=pltpu.CompilerParams(collective_id=1, has_side_effects=True),
    )(row)


def return_kernel(column_ref, update_out, upd_send, upd_recv, local_sem):
    groups = update_out.shape[1] // column_ref.shape[1]
    rows = column_ref.shape[1]
    members = update_out.shape[0]
    me_s = lax.axis_index("space")
    me_e = lax.axis_index("ens")
    mesh_id = pl.DeviceIdType.MESH

    barrier = pltpu.get_barrier_semaphore()
    for e in range(groups):
        @pl.when(me_e != e)
        def _():
            pl.semaphore_signal(barrier, 1, device_id=(me_s, e), device_id_type=mesh_id)
    pl.semaphore_wait(barrier, groups - 1)

    def upd_copy(e, source_e):
        return pltpu.make_async_remote_copy(
            src_ref=column_ref.at[pl.ds(e * members, members)],
            dst_ref=update_out.at[:, pl.ds(source_e * rows, rows)],
            send_sem=upd_send.at[e],
            recv_sem=upd_recv.at[source_e],
            device_id=(me_s, e),
            device_id_type=mesh_id,
        )

    keep_upd = pltpu.make_async_copy(
        column_ref.at[pl.ds(me_e * members, members)],
        update_out.at[:, pl.ds(me_e * rows, rows)],
        local_sem,
    )
    for e in range(groups):
        @pl.when(me_e != e)
        def _():
            upd_copy(e, me_e).start()
    keep_upd.start()
    keep_upd.wait()
    for e in range(groups):
        @pl.when(me_e != e)
        def _():
            upd_copy(e, me_e).wait_send()
            upd_copy(e, e).wait_recv()


def send_back(column, slab_rows):
    total, rows, across = column.shape
    groups = slab_rows // rows
    members = total // groups
    anywhere = pl.BlockSpec(memory_space=pl.ANY)
    return pl.pallas_call(
        return_kernel,
        out_shape=jax.ShapeDtypeStruct((members, slab_rows, across), jnp.float32),
        in_specs=[anywhere],
        out_specs=anywhere,
        scratch_shapes=[
            pltpu.SemaphoreType.DMA((groups,)),
            pltpu.SemaphoreType.DMA((groups,)),
            pltpu.SemaphoreType.DMA,
        ],
        compiler_params=pltpu.CompilerParams(collective_id=2, has_side_effects=True),
    )(column)


def gather_grid(slab, n_space, n_ens):
    rows = n_space // 2
    me_s = lax.axis_index("space")
    z, half = me_s // 2, me_s % 2
    pieces = [(slab, me_s)]
    for flip in (0, 1):
        for dz in range(1 - flip, rows):
            pairs = []
            for s in range(n_space):
                zs, hs = s // 2, s % 2
                t = ((zs + dz) % rows) * 2 + (hs ^ flip)
                for e in range(n_ens):
                    pairs.append((s * n_ens + e, t * n_ens + (e ^ (2 * flip))))
            got = lax.ppermute(slab, ("space", "ens"), pairs)
            pieces.append((got, ((z - dz) % rows) * 2 + (half ^ flip)))
    thick = slab.shape[0]
    grid = jnp.zeros((n_space * thick,) + slab.shape[1:], slab.dtype)
    for got, source in pieces:
        grid = lax.dynamic_update_slice_in_dim(grid, got, source * thick, axis=0)
    return grid


def grid_kernel(slab_ref, mine_ref, other_ref, send_sems, recv_sems, local_sem, pair_sems):
    thick = slab_ref.shape[0]
    rows = mine_ref.shape[0] // thick // 2
    me_s = lax.axis_index("space")
    me_e = lax.axis_index("ens")
    z, half = me_s // 2, me_s % 2
    across_x = me_e + 2 - 4 * ((me_e // 2) % 2)
    partner = me_e + 1 - 2 * (me_e % 2)
    mesh_id = pl.DeviceIdType.MESH
    patterns = [(0, dz) for dz in range(1, rows)] + [(1, dz) for dz in range(rows)]

    def place(flip, dz, sign):
        s = ((z + sign * dz + rows) % rows) * 2 + (half + flip) % 2
        return s, (across_x if flip else me_e)

    barrier = pltpu.get_barrier_semaphore()
    friends = [place(0, dz, 1) for dz in range(1, rows)] + [place(1, dz, 1) for dz in range(rows)]
    for s, e in friends + [(me_s, partner)]:
        pl.semaphore_signal(barrier, 1, device_id=(s, e), device_id_type=mesh_id)
    pl.semaphore_wait(barrier, len(friends) + 1)

    def push(k, flip, dz, sign):
        s, e = place(flip, dz, sign)
        where = me_s if sign > 0 else s
        return pltpu.make_async_remote_copy(
            src_ref=slab_ref,
            dst_ref=mine_ref.at[pl.ds(where * thick, thick)],
            send_sem=send_sems.at[k],
            recv_sem=recv_sems.at[k],
            device_id=(s, e),
            device_id_type=mesh_id,
        )

    keep = pltpu.make_async_copy(slab_ref, mine_ref.at[pl.ds(me_s * thick, thick)], local_sem)
    for k, (flip, dz) in enumerate(patterns):
        push(k, flip, dz, 1).start()
    keep.start()
    keep.wait()
    for k, (flip, dz) in enumerate(patterns):
        push(k, flip, dz, 1).wait_send()
        push(k, flip, dz, -1).wait_recv()
    swap = pltpu.make_async_remote_copy(
        src_ref=mine_ref,
        dst_ref=other_ref,
        send_sem=pair_sems.at[0],
        recv_sem=pair_sems.at[1],
        device_id=(me_s, partner),
        device_id_type=mesh_id,
    )
    swap.start()
    swap.wait_send()
    swap.wait_recv()


def gather_grids(slab, n_space):
    thick, depth, across = slab.shape
    anywhere = pl.BlockSpec(memory_space=pl.ANY)
    grid = jax.ShapeDtypeStruct((n_space * thick, depth, across), jnp.float32)
    return pl.pallas_call(
        grid_kernel,
        out_shape=(grid, grid),
        in_specs=[anywhere],
        out_specs=(anywhere, anywhere),
        scratch_shapes=[
            pltpu.SemaphoreType.DMA((n_space - 1,)),
            pltpu.SemaphoreType.DMA((n_space - 1,)),
            pltpu.SemaphoreType.DMA,
            pltpu.SemaphoreType.DMA((2,)),
        ],
        compiler_params=pltpu.CompilerParams(collective_id=5, has_side_effects=True),
    )(slab)


def shards(
    log_perm,
    storage,
    head_init,
    well_cells,
    well_rates,
    obs_cells,
    obs_values,
    noise_var,
    step_size,
    perturb,
):
    members, planes, depth, across = log_perm.shape
    n_space = lax.axis_size("space")
    n_ens = lax.axis_size("ens")
    cell_count = planes * depth * across
    total_members = members * n_ens
    grid_planes = planes * n_space

    whole_log = lax.all_to_all(log_perm, "space", 0, 1, tiled=True)
    core = lax.axis_index("ens") % 2
    mine, other = gather_grids(jnp.where(core == 0, storage, head_init), n_space)
    whole_storage = jnp.where(core == 0, mine, other)
    whole_head = jnp.where(core == 0, other, mine)
    source = (
        jnp.zeros((grid_planes * depth * across,), jnp.float32)
        .at[well_cells]
        .add(well_rates)
        .reshape(grid_planes, depth, across)
    )
    forcing = whole_storage * whole_head + source
    slab_rows = planes * depth
    by_rows = log_perm.reshape(members, slab_rows, across)
    field, band = forward_pallas(
        whole_log[0], whole_storage, whole_head, forcing, by_rows, n_ens
    )
    picked = field.reshape(-1)[obs_cells]
    head_field = lax.all_to_all(field[None], "space", 1, 0, tiled=True)

    obs_count = picked.shape[0]
    own_perturb = lax.dynamic_index_in_dim(perturb, lax.axis_index("space"), 0, keepdims=False)
    row = jnp.zeros((1, 8, 128), jnp.float32)
    row = row.at[0, 0, :obs_count].set(picked).at[0, 0, obs_count : 2 * obs_count].set(own_perturb)
    rows = gather_rows(row, total_members)
    every_obs = rows[:, 0, :obs_count]
    every_perturb = rows[:, 0, obs_count : 2 * obs_count]
    mean_obs = jnp.mean(every_obs, axis=0)
    spread = every_obs - mean_obs
    covariance = jnp.dot(spread.T, spread, precision=HIGHEST) / (total_members - 1)
    system = covariance + jnp.diag(noise_var / step_size[0])
    factor_lower = jnp.linalg.cholesky(system)
    gain_rows = solve_pair(factor_lower, obs_values[None, :] + every_perturb - every_obs)
    mixing = jnp.dot(gain_rows, spread.T, precision=HIGHEST)

    change = jnp.einsum("jk,kry->jry", mixing, band, precision=HIGHEST)
    new_band = band + change / (total_members - 1)
    updated = send_back(new_band, slab_rows)
    updated = updated.reshape(log_perm.shape)
    return (head_field, updated)


def solution(mesh):
    return jax.shard_map(
        shards,
        mesh=mesh,
        in_specs=(
            P("ens", "space", None, None),
            P("space", None, None),
            P("space", None, None),
            P(),
            P(),
            P(),
            P(),
            P(),
            P(),
            P("ens", None),
        ),
        out_specs=(P("ens", "space", None, None), P("ens", "space", None, None)),
        check_vma=False,
    )
```

```python
import jax
from jax.experimental import pallas as pl
from jax.experimental.pallas import tpu as pltpu
import jax.numpy as jnp
from jax import lax
from jax.sharding import PartitionSpec as P

SWEEPS = 3


OMEGA = 0.8
HIGHEST = lax.Precision.HIGHEST
DIRECTIONS = [
    (a, b, c) for a in (-1, 0, 1) for b in (-1, 0, 1) for c in (-1, 0, 1) if (a, b, c) != (0, 0, 0)
]


def shifted(padded, a, b, c, planes, depth, across):
    return padded[..., 1 + a : 1 + a + planes, 1 + b : 1 + b + depth, 1 + c : 1 + c + across]


def solve_pair(factor, residual):
    first = lax.linalg.triangular_solve(factor, residual.T, left_side=True, lower=True)
    second = lax.linalg.triangular_solve(
        factor, first, left_side=True, lower=True, transpose_a=True
    )
    return second.T


HALF = [(a, b, c) for a, b, c in DIRECTIONS if (a, b, c) > (0, 0, 0)]


def shift_plane(x, b, c):
    depth, across = x.shape
    valid = None
    if b != 0:
        x = pltpu.roll(x, (-b) % depth, 0)
        rows = lax.broadcasted_iota(jnp.int32, x.shape, 0) + b
        valid = (rows >= 0) & (rows < depth)
    if c != 0:
        x = pltpu.roll(x, (-c) % across, 1)
        cols = lax.broadcasted_iota(jnp.int32, x.shape, 1) + c
        ok = (cols >= 0) & (cols < across)
        valid = ok if valid is None else valid & ok
    if valid is None:
        return x
    return jnp.where(valid, x, 0.0)


def roll_plane(x, b, c):
    depth, across = x.shape
    if b != 0:
        x = pltpu.roll(x, (-b) % depth, 0)
    if c != 0:
        x = pltpu.roll(x, (-c) % across, 1)
    return x


def forward_kernel(
    log_ref, sto_ref, init_ref, forc_ref, rows_ref, out_ref, band_ref,
    perm, trans, diag, head_a, head_b, band_send, band_recv, local_sem,
):
    planes, depth, across = log_ref.shape
    members, slab_rows, _ = rows_ref.shape
    groups = band_ref.shape[0] // members
    rows = slab_rows // groups
    me_s = lax.axis_index("space")
    me_e = lax.axis_index("ens")
    mesh_id = pl.DeviceIdType.MESH
    barrier = pltpu.get_barrier_semaphore()
    for e in range(groups):
        @pl.when(me_e != e)
        def _():
            pl.semaphore_signal(barrier, 1, device_id=(me_s, e), device_id_type=mesh_id)

    def band_copy(e, source_e):
        return pltpu.make_async_remote_copy(
            src_ref=rows_ref.at[:, pl.ds(e * rows, rows)],
            dst_ref=band_ref.at[pl.ds(source_e * members, members)],
            send_sem=band_send.at[e],
            recv_sem=band_recv.at[source_e],
            device_id=(me_s, e),
            device_id_type=mesh_id,
        )

    keep_band = pltpu.make_async_copy(
        rows_ref.at[:, pl.ds(me_e * rows, rows)],
        band_ref.at[pl.ds(me_e * members, members)],
        local_sem,
    )
    zero = jnp.zeros((depth, across), jnp.float32)
    for buf in (perm, head_a, head_b):
        buf[0] = zero
        buf[planes + 1] = zero

    def fill(p, carry):
        perm[p + 1] = jnp.exp(log_ref[p])
        head_a[p + 1] = init_ref[p]
        return carry

    lax.fori_loop(0, planes, fill, 0)

    def transmissibility(p, carry):
        own = perm[p + 1]
        for k, (a, b, c) in enumerate(HALF):
            factor = 2.0 ** (1 - abs(a) - abs(b) - abs(c))
            other = shift_plane(perm[p + 1 + a], b, c)
            trans[k, p] = factor * 2.0 * own * other / (own + other)
        return carry

    lax.fori_loop(0, planes, transmissibility, 0)

    pl.semaphore_wait(barrier, groups - 1)
    for e in range(groups):
        @pl.when(me_e != e)
        def _():
            band_copy(e, me_e).start()
    keep_band.start()

    def diagonal(p, carry):
        total = sto_ref[p]
        for k, (a, b, c) in enumerate(HALF):
            back = p - a
            inside = (back >= 0) & (back < planes)
            behind = roll_plane(trans[k, jnp.clip(back, 0, planes - 1)], -b, -c)
            total = total + trans[k, p] + jnp.where(inside, behind, 0.0)
        diag[p] = total
        return carry

    lax.fori_loop(0, planes, diagonal, 0)

    def sweep(source, target, padded_target):
        def body(p, carry):
            gathered = None
            for k, (a, b, c) in enumerate(HALF):
                ahead = trans[k, p] * roll_plane(source[p + 1 + a], b, c)
                back = jnp.clip(p - a, 0, planes - 1)
                flow = roll_plane(trans[k, back] * source[p + 1 - a], -b, -c)
                term = ahead + flow
                gathered = term if gathered is None else gathered + term
            value = (1.0 - OMEGA) * source[p + 1] + OMEGA * (forc_ref[p] + gathered) / diag[p]
            if padded_target:
                target[p + 1] = value
            else:
                target[p] = value
            return carry

        lax.fori_loop(0, planes, body, 0)

    sweep(head_a, head_b, True)
    sweep(head_b, head_a, True)
    sweep(head_a, out_ref, False)
    keep_band.wait()
    for e in range(groups):
        @pl.when(me_e != e)
        def _():
            band_copy(e, me_e).wait_send()
            band_copy(e, e).wait_recv()


def forward_pallas(log_row, storage, head_init, forcing, by_rows, groups):
    planes, depth, across = log_row.shape
    members, slab_rows, _ = by_rows.shape
    vmem = pl.BlockSpec(memory_space=pltpu.VMEM)
    anywhere = pl.BlockSpec(memory_space=pl.ANY)
    return pl.pallas_call(
        forward_kernel,
        out_shape=(
            jax.ShapeDtypeStruct((planes, depth, across), jnp.float32),
            jax.ShapeDtypeStruct((members * groups, slab_rows // groups, across), jnp.float32),
        ),
        in_specs=[vmem] * 4 + [anywhere],
        out_specs=(vmem, anywhere),
        scratch_shapes=[
            pltpu.VMEM((planes + 2, depth, across), jnp.float32),
            pltpu.VMEM((len(HALF), planes, depth, across), jnp.float32),
            pltpu.VMEM((planes, depth, across), jnp.float32),
            pltpu.VMEM((planes + 2, depth, across), jnp.float32),
            pltpu.VMEM((planes + 2, depth, across), jnp.float32),
            pltpu.SemaphoreType.DMA((groups,)),
            pltpu.SemaphoreType.DMA((groups,)),
            pltpu.SemaphoreType.DMA,
        ],
        compiler_params=pltpu.CompilerParams(
            vmem_limit_bytes=66 * 1024 * 1024, collective_id=3, has_side_effects=True
        ),
    )(log_row, storage, head_init, forcing, by_rows)


def gather_kernel(row_ref, out_ref, landing, send_sem, recv_sem):
    total = landing.shape[0]
    n_space = lax.axis_size("space")
    me_s = lax.axis_index("space")
    me_e = lax.axis_index("ens")
    mine = me_e * n_space + me_s
    mesh_id = pl.DeviceIdType.MESH

    barrier = pltpu.get_barrier_semaphore()

    def greet(i, carry):
        @pl.when(i != mine)
        def _():
            pl.semaphore_signal(
                barrier, 1, device_id=(i % n_space, i // n_space), device_id_type=mesh_id
            )

        return carry

    lax.fori_loop(0, total, greet, 0)
    pl.semaphore_wait(barrier, total - 1)

    def send(i, carry):
        @pl.when(i != mine)
        def _():
            pltpu.make_async_remote_copy(
                src_ref=row_ref,
                dst_ref=landing.at[pl.ds(mine, 1)],
                send_sem=send_sem,
                recv_sem=recv_sem,
                device_id=(i % n_space, i // n_space),
                device_id_type=mesh_id,
            ).start()

        return carry

    lax.fori_loop(0, total, send, 0)
    landing[pl.ds(mine, 1)] = row_ref[...]
    partner = (mine + 1) % total
    everything = pltpu.make_async_remote_copy(
        src_ref=landing.at[pl.ds(0, total - 1)],
        dst_ref=landing.at[pl.ds(1, total - 1)],
        send_sem=send_sem,
        recv_sem=recv_sem,
        device_id=(partner % n_space, partner // n_space),
        device_id_type=mesh_id,
    )
    everything.wait_send()
    everything.wait_recv()
    out_ref[...] = landing[...]


def gather_rows(row, total):
    vmem = pl.BlockSpec(memory_space=pltpu.VMEM)
    return pl.pallas_call(
        gather_kernel,
        out_shape=jax.ShapeDtypeStruct((total,) + row.shape[1:], jnp.float32),
        in_specs=[vmem],
        out_specs=vmem,
        scratch_shapes=[
            pltpu.VMEM((total,) + row.shape[1:], jnp.float32),
            pltpu.SemaphoreType.DMA,
            pltpu.SemaphoreType.DMA,
        ],
        compiler_params=pltpu.CompilerParams(collective_id=1, has_side_effects=True),
    )(row)


def return_kernel(column_ref, update_out, upd_send, upd_recv, local_sem):
    groups = update_out.shape[1] // column_ref.shape[1]
    rows = column_ref.shape[1]
    members = update_out.shape[0]
    me_s = lax.axis_index("space")
    me_e = lax.axis_index("ens")
    mesh_id = pl.DeviceIdType.MESH

    barrier = pltpu.get_barrier_semaphore()
    for e in range(groups):
        @pl.when(me_e != e)
        def _():
            pl.semaphore_signal(barrier, 1, device_id=(me_s, e), device_id_type=mesh_id)
    pl.semaphore_wait(barrier, groups - 1)

    def upd_copy(e, source_e):
        return pltpu.make_async_remote_copy(
            src_ref=column_ref.at[pl.ds(e * members, members)],
            dst_ref=update_out.at[:, pl.ds(source_e * rows, rows)],
            send_sem=upd_send.at[e],
            recv_sem=upd_recv.at[source_e],
            device_id=(me_s, e),
            device_id_type=mesh_id,
        )

    keep_upd = pltpu.make_async_copy(
        column_ref.at[pl.ds(me_e * members, members)],
        update_out.at[:, pl.ds(me_e * rows, rows)],
        local_sem,
    )
    for e in range(groups):
        @pl.when(me_e != e)
        def _():
            upd_copy(e, me_e).start()
    keep_upd.start()
    keep_upd.wait()
    for e in range(groups):
        @pl.when(me_e != e)
        def _():
            upd_copy(e, me_e).wait_send()
            upd_copy(e, e).wait_recv()


def send_back(column, slab_rows):
    total, rows, across = column.shape
    groups = slab_rows // rows
    members = total // groups
    anywhere = pl.BlockSpec(memory_space=pl.ANY)
    return pl.pallas_call(
        return_kernel,
        out_shape=jax.ShapeDtypeStruct((members, slab_rows, across), jnp.float32),
        in_specs=[anywhere],
        out_specs=anywhere,
        scratch_shapes=[
            pltpu.SemaphoreType.DMA((groups,)),
            pltpu.SemaphoreType.DMA((groups,)),
            pltpu.SemaphoreType.DMA,
        ],
        compiler_params=pltpu.CompilerParams(collective_id=2, has_side_effects=True),
    )(column)


def gather_grid(slab, n_space, n_ens):
    rows = n_space // 2
    me_s = lax.axis_index("space")
    z, half = me_s // 2, me_s % 2
    pieces = [(slab, me_s)]
    for flip in (0, 1):
        for dz in range(1 - flip, rows):
            pairs = []
            for s in range(n_space):
                zs, hs = s // 2, s % 2
                t = ((zs + dz) % rows) * 2 + (hs ^ flip)
                for e in range(n_ens):
                    pairs.append((s * n_ens + e, t * n_ens + (e ^ (2 * flip))))
            got = lax.ppermute(slab, ("space", "ens"), pairs)
            pieces.append((got, ((z - dz) % rows) * 2 + (half ^ flip)))
    thick = slab.shape[0]
    grid = jnp.zeros((n_space * thick,) + slab.shape[1:], slab.dtype)
    for got, source in pieces:
        grid = lax.dynamic_update_slice_in_dim(grid, got, source * thick, axis=0)
    return grid


def grid_kernel(slab_ref, mine_ref, other_ref, send_sems, recv_sems, local_sem, pair_sems):
    thick = slab_ref.shape[0]
    rows = mine_ref.shape[0] // thick // 2
    me_s = lax.axis_index("space")
    me_e = lax.axis_index("ens")
    z, half = me_s // 2, me_s % 2
    across_x = me_e + 2 - 4 * ((me_e // 2) % 2)
    partner = me_e + 1 - 2 * (me_e % 2)
    mesh_id = pl.DeviceIdType.MESH
    patterns = [(0, dz) for dz in range(1, rows)] + [(1, dz) for dz in range(rows)]

    def place(flip, dz, sign):
        s = ((z + sign * dz + rows) % rows) * 2 + (half + flip) % 2
        return s, (across_x if flip else me_e)

    barrier = pltpu.get_barrier_semaphore()
    friends = [place(0, dz, 1) for dz in range(1, rows)] + [place(1, dz, 1) for dz in range(rows)]
    for s, e in friends + [(me_s, partner)]:
        pl.semaphore_signal(barrier, 1, device_id=(s, e), device_id_type=mesh_id)
    pl.semaphore_wait(barrier, len(friends) + 1)

    def push(k, flip, dz, sign):
        s, e = place(flip, dz, sign)
        where = me_s if sign > 0 else s
        return pltpu.make_async_remote_copy(
            src_ref=slab_ref,
            dst_ref=mine_ref.at[pl.ds(where * thick, thick)],
            send_sem=send_sems.at[k],
            recv_sem=recv_sems.at[k],
            device_id=(s, e),
            device_id_type=mesh_id,
        )

    def hand(slab_index, source):
        return pltpu.make_async_remote_copy(
            src_ref=source,
            dst_ref=other_ref.at[pl.ds(slab_index * thick, thick)],
            send_sem=pair_sems.at[0, slab_index],
            recv_sem=pair_sems.at[1, slab_index],
            device_id=(me_s, partner),
            device_id_type=mesh_id,
        )

    keep = pltpu.make_async_copy(slab_ref, mine_ref.at[pl.ds(me_s * thick, thick)], local_sem)
    for k, (flip, dz) in enumerate(patterns):
        push(k, flip, dz, 1).start()
    keep.start()
    hand(me_s, slab_ref).start()
    keep.wait()
    for k, (flip, dz) in enumerate(patterns):
        push(k, flip, dz, 1).wait_send()
        push(k, flip, dz, -1).wait_recv()
        landed, _ = place(flip, dz, -1)
        hand(landed, mine_ref.at[pl.ds(landed * thick, thick)]).start()
    for slab_index in range(2 * rows):
        hand(slab_index, mine_ref.at[pl.ds(slab_index * thick, thick)]).wait_send()
        hand(slab_index, mine_ref.at[pl.ds(slab_index * thick, thick)]).wait_recv()


def gather_grids(slab, n_space):
    thick, depth, across = slab.shape
    anywhere = pl.BlockSpec(memory_space=pl.ANY)
    grid = jax.ShapeDtypeStruct((n_space * thick, depth, across), jnp.float32)
    return pl.pallas_call(
        grid_kernel,
        out_shape=(grid, grid),
        in_specs=[anywhere],
        out_specs=(anywhere, anywhere),
        scratch_shapes=[
            pltpu.SemaphoreType.DMA((n_space - 1,)),
            pltpu.SemaphoreType.DMA((n_space - 1,)),
            pltpu.SemaphoreType.DMA,
            pltpu.SemaphoreType.DMA((2, n_space)),
        ],
        compiler_params=pltpu.CompilerParams(collective_id=5, has_side_effects=True),
    )(slab)


def shards(
    log_perm,
    storage,
    head_init,
    well_cells,
    well_rates,
    obs_cells,
    obs_values,
    noise_var,
    step_size,
    perturb,
):
    members, planes, depth, across = log_perm.shape
    n_space = lax.axis_size("space")
    n_ens = lax.axis_size("ens")
    cell_count = planes * depth * across
    total_members = members * n_ens
    grid_planes = planes * n_space

    whole_log = lax.all_to_all(log_perm, "space", 0, 1, tiled=True)
    core = lax.axis_index("ens") % 2
    mine, other = gather_grids(jnp.where(core == 0, storage, head_init), n_space)
    whole_storage = jnp.where(core == 0, mine, other)
    whole_head = jnp.where(core == 0, other, mine)
    source = (
        jnp.zeros((grid_planes * depth * across,), jnp.float32)
        .at[well_cells]
        .add(well_rates)
        .reshape(grid_planes, depth, across)
    )
    forcing = whole_storage * whole_head + source
    slab_rows = planes * depth
    by_rows = log_perm.reshape(members, slab_rows, across)
    field, band = forward_pallas(
        whole_log[0], whole_storage, whole_head, forcing, by_rows, n_ens
    )
    picked = field.reshape(-1)[obs_cells]
    head_field = lax.all_to_all(field[None], "space", 1, 0, tiled=True)

    obs_count = picked.shape[0]
    own_perturb = lax.dynamic_index_in_dim(perturb, lax.axis_index("space"), 0, keepdims=False)
    row = jnp.zeros((1, 8, 128), jnp.float32)
    row = row.at[0, 0, :obs_count].set(picked).at[0, 0, obs_count : 2 * obs_count].set(own_perturb)
    rows = gather_rows(row, total_members)
    every_obs = rows[:, 0, :obs_count]
    every_perturb = rows[:, 0, obs_count : 2 * obs_count]
    mean_obs = jnp.mean(every_obs, axis=0)
    spread = every_obs - mean_obs
    covariance = jnp.dot(spread.T, spread, precision=HIGHEST) / (total_members - 1)
    system = covariance + jnp.diag(noise_var / step_size[0])
    factor_lower = jnp.linalg.cholesky(system)
    gain_rows = solve_pair(factor_lower, obs_values[None, :] + every_perturb - every_obs)
    mixing = jnp.dot(gain_rows, spread.T, precision=HIGHEST)

    change = jnp.einsum("jk,kry->jry", mixing, band, precision=HIGHEST)
    new_band = band + change / (total_members - 1)
    updated = send_back(new_band, slab_rows)
    updated = updated.reshape(log_perm.shape)
    return (head_field, updated)


def solution(mesh):
    return jax.shard_map(
        shards,
        mesh=mesh,
        in_specs=(
            P("ens", "space", None, None),
            P("space", None, None),
            P("space", None, None),
            P(),
            P(),
            P(),
            P(),
            P(),
            P(),
            P("ens", None),
        ),
        out_specs=(P("ens", "space", None, None), P("ens", "space", None, None)),
        check_vma=False,
    )
```

```python
import jax
from jax.experimental import pallas as pl
from jax.experimental.pallas import tpu as pltpu
import jax.numpy as jnp
from jax import lax
from jax.sharding import PartitionSpec as P

SWEEPS = 3


OMEGA = 0.8
HIGHEST = lax.Precision.HIGHEST
DIRECTIONS = [
    (a, b, c) for a in (-1, 0, 1) for b in (-1, 0, 1) for c in (-1, 0, 1) if (a, b, c) != (0, 0, 0)
]


def shifted(padded, a, b, c, planes, depth, across):
    return padded[..., 1 + a : 1 + a + planes, 1 + b : 1 + b + depth, 1 + c : 1 + c + across]


def solve_pair(factor, residual):
    first = lax.linalg.triangular_solve(factor, residual.T, left_side=True, lower=True)
    second = lax.linalg.triangular_solve(
        factor, first, left_side=True, lower=True, transpose_a=True
    )
    return second.T


HALF = [(a, b, c) for a, b, c in DIRECTIONS if (a, b, c) > (0, 0, 0)]


def shift_plane(x, b, c):
    depth, across = x.shape
    valid = None
    if b != 0:
        x = pltpu.roll(x, (-b) % depth, 0)
        rows = lax.broadcasted_iota(jnp.int32, x.shape, 0) + b
        valid = (rows >= 0) & (rows < depth)
    if c != 0:
        x = pltpu.roll(x, (-c) % across, 1)
        cols = lax.broadcasted_iota(jnp.int32, x.shape, 1) + c
        ok = (cols >= 0) & (cols < across)
        valid = ok if valid is None else valid & ok
    if valid is None:
        return x
    return jnp.where(valid, x, 0.0)


def roll_plane(x, b, c):
    depth, across = x.shape
    if b != 0:
        x = pltpu.roll(x, (-b) % depth, 0)
    if c != 0:
        x = pltpu.roll(x, (-c) % across, 1)
    return x


def forward_kernel(
    log_ref, sto_ref, init_ref, forc_ref, rows_ref, out_ref, band_ref,
    perm, trans, diag, head_a, head_b, band_send, band_recv, local_sem,
):
    planes, depth, across = log_ref.shape
    members, slab_rows, _ = rows_ref.shape
    groups = band_ref.shape[0] // members
    rows = slab_rows // groups
    me_s = lax.axis_index("space")
    me_e = lax.axis_index("ens")
    mesh_id = pl.DeviceIdType.MESH
    barrier = pltpu.get_barrier_semaphore()
    for e in range(groups):
        @pl.when(me_e != e)
        def _():
            pl.semaphore_signal(barrier, 1, device_id=(me_s, e), device_id_type=mesh_id)

    def band_copy(e, source_e):
        return pltpu.make_async_remote_copy(
            src_ref=rows_ref.at[:, pl.ds(e * rows, rows)],
            dst_ref=band_ref.at[pl.ds(source_e * members, members)],
            send_sem=band_send.at[e],
            recv_sem=band_recv.at[source_e],
            device_id=(me_s, e),
            device_id_type=mesh_id,
        )

    keep_band = pltpu.make_async_copy(
        rows_ref.at[:, pl.ds(me_e * rows, rows)],
        band_ref.at[pl.ds(me_e * members, members)],
        local_sem,
    )
    zero = jnp.zeros((depth, across), jnp.float32)
    for buf in (perm, head_a, head_b):
        buf[0] = zero
        buf[planes + 1] = zero

    def fill(p, carry):
        perm[p + 1] = jnp.exp(log_ref[p])
        head_a[p + 1] = init_ref[p]
        return carry

    lax.fori_loop(0, planes, fill, 0)

    def transmissibility(p, carry):
        own = perm[p + 1]
        for k, (a, b, c) in enumerate(HALF):
            factor = 2.0 ** (1 - abs(a) - abs(b) - abs(c))
            other = shift_plane(perm[p + 1 + a], b, c)
            trans[k, p] = factor * 2.0 * own * other / (own + other)
        return carry

    lax.fori_loop(0, planes, transmissibility, 0)

    pl.semaphore_wait(barrier, groups - 1)
    for e in range(groups):
        @pl.when(me_e != e)
        def _():
            band_copy(e, me_e).start()
    keep_band.start()

    def diagonal(p, carry):
        total = sto_ref[p]
        for k, (a, b, c) in enumerate(HALF):
            back = p - a
            inside = (back >= 0) & (back < planes)
            behind = roll_plane(trans[k, jnp.clip(back, 0, planes - 1)], -b, -c)
            total = total + trans[k, p] + jnp.where(inside, behind, 0.0)
        diag[p] = total
        return carry

    lax.fori_loop(0, planes, diagonal, 0)

    def sweep(source, target, padded_target):
        def body(p, carry):
            gathered = None
            for k, (a, b, c) in enumerate(HALF):
                ahead = trans[k, p] * roll_plane(source[p + 1 + a], b, c)
                back = jnp.clip(p - a, 0, planes - 1)
                flow = roll_plane(trans[k, back] * source[p + 1 - a], -b, -c)
                term = ahead + flow
                gathered = term if gathered is None else gathered + term
            value = (1.0 - OMEGA) * source[p + 1] + OMEGA * (forc_ref[p] + gathered) / diag[p]
            if padded_target:
                target[p + 1] = value
            else:
                target[p] = value
            return carry

        lax.fori_loop(0, planes, body, 0)

    sweep(head_a, head_b, True)
    sweep(head_b, head_a, True)
    sweep(head_a, out_ref, False)
    keep_band.wait()
    for e in range(groups):
        @pl.when(me_e != e)
        def _():
            band_copy(e, me_e).wait_send()
            band_copy(e, e).wait_recv()


def forward_pallas(log_row, storage, head_init, forcing, by_rows, groups):
    planes, depth, across = log_row.shape
    members, slab_rows, _ = by_rows.shape
    vmem = pl.BlockSpec(memory_space=pltpu.VMEM)
    anywhere = pl.BlockSpec(memory_space=pl.ANY)
    return pl.pallas_call(
        forward_kernel,
        out_shape=(
            jax.ShapeDtypeStruct((planes, depth, across), jnp.float32),
            jax.ShapeDtypeStruct((members * groups, slab_rows // groups, across), jnp.float32),
        ),
        in_specs=[vmem] * 4 + [anywhere],
        out_specs=(vmem, anywhere),
        scratch_shapes=[
            pltpu.VMEM((planes + 2, depth, across), jnp.float32),
            pltpu.VMEM((len(HALF), planes, depth, across), jnp.float32),
            pltpu.VMEM((planes, depth, across), jnp.float32),
            pltpu.VMEM((planes + 2, depth, across), jnp.float32),
            pltpu.VMEM((planes + 2, depth, across), jnp.float32),
            pltpu.SemaphoreType.DMA((groups,)),
            pltpu.SemaphoreType.DMA((groups,)),
            pltpu.SemaphoreType.DMA,
        ],
        compiler_params=pltpu.CompilerParams(
            vmem_limit_bytes=66 * 1024 * 1024, collective_id=3, has_side_effects=True
        ),
    )(log_row, storage, head_init, forcing, by_rows)


def gather_kernel(row_ref, out_ref, landing, send_sem, recv_sem):
    total = landing.shape[0]
    n_space = lax.axis_size("space")
    me_s = lax.axis_index("space")
    me_e = lax.axis_index("ens")
    mine = me_e * n_space + me_s
    mesh_id = pl.DeviceIdType.MESH

    barrier = pltpu.get_barrier_semaphore()

    def greet(i, carry):
        @pl.when(i != mine)
        def _():
            pl.semaphore_signal(
                barrier, 1, device_id=(i % n_space, i // n_space), device_id_type=mesh_id
            )

        return carry

    lax.fori_loop(0, total, greet, 0)
    pl.semaphore_wait(barrier, total - 1)

    def send(i, carry):
        @pl.when(i != mine)
        def _():
            pltpu.make_async_remote_copy(
                src_ref=row_ref,
                dst_ref=landing.at[pl.ds(mine, 1)],
                send_sem=send_sem,
                recv_sem=recv_sem,
                device_id=(i % n_space, i // n_space),
                device_id_type=mesh_id,
            ).start()

        return carry

    lax.fori_loop(0, total, send, 0)
    landing[pl.ds(mine, 1)] = row_ref[...]
    partner = (mine + 1) % total
    everything = pltpu.make_async_remote_copy(
        src_ref=landing.at[pl.ds(0, total - 1)],
        dst_ref=landing.at[pl.ds(1, total - 1)],
        send_sem=send_sem,
        recv_sem=recv_sem,
        device_id=(partner % n_space, partner // n_space),
        device_id_type=mesh_id,
    )
    everything.wait_send()
    everything.wait_recv()
    out_ref[...] = landing[...]


def gather_rows(row, total):
    vmem = pl.BlockSpec(memory_space=pltpu.VMEM)
    return pl.pallas_call(
        gather_kernel,
        out_shape=jax.ShapeDtypeStruct((total,) + row.shape[1:], jnp.float32),
        in_specs=[vmem],
        out_specs=vmem,
        scratch_shapes=[
            pltpu.VMEM((total,) + row.shape[1:], jnp.float32),
            pltpu.SemaphoreType.DMA,
            pltpu.SemaphoreType.DMA,
        ],
        compiler_params=pltpu.CompilerParams(collective_id=1, has_side_effects=True),
    )(row)


def return_kernel(column_ref, update_out, upd_send, upd_recv, local_sem):
    groups = update_out.shape[1] // column_ref.shape[1]
    rows = column_ref.shape[1]
    members = update_out.shape[0]
    me_s = lax.axis_index("space")
    me_e = lax.axis_index("ens")
    mesh_id = pl.DeviceIdType.MESH

    barrier = pltpu.get_barrier_semaphore()
    for e in range(groups):
        @pl.when(me_e != e)
        def _():
            pl.semaphore_signal(barrier, 1, device_id=(me_s, e), device_id_type=mesh_id)
    pl.semaphore_wait(barrier, groups - 1)

    def upd_copy(e, source_e):
        return pltpu.make_async_remote_copy(
            src_ref=column_ref.at[pl.ds(e * members, members)],
            dst_ref=update_out.at[:, pl.ds(source_e * rows, rows)],
            send_sem=upd_send.at[e],
            recv_sem=upd_recv.at[source_e],
            device_id=(me_s, e),
            device_id_type=mesh_id,
        )

    keep_upd = pltpu.make_async_copy(
        column_ref.at[pl.ds(me_e * members, members)],
        update_out.at[:, pl.ds(me_e * rows, rows)],
        local_sem,
    )
    for e in range(groups):
        @pl.when(me_e != e)
        def _():
            upd_copy(e, me_e).start()
    keep_upd.start()
    keep_upd.wait()
    for e in range(groups):
        @pl.when(me_e != e)
        def _():
            upd_copy(e, me_e).wait_send()
            upd_copy(e, e).wait_recv()


def send_back(column, slab_rows):
    total, rows, across = column.shape
    groups = slab_rows // rows
    members = total // groups
    anywhere = pl.BlockSpec(memory_space=pl.ANY)
    return pl.pallas_call(
        return_kernel,
        out_shape=jax.ShapeDtypeStruct((members, slab_rows, across), jnp.float32),
        in_specs=[anywhere],
        out_specs=anywhere,
        scratch_shapes=[
            pltpu.SemaphoreType.DMA((groups,)),
            pltpu.SemaphoreType.DMA((groups,)),
            pltpu.SemaphoreType.DMA,
        ],
        compiler_params=pltpu.CompilerParams(collective_id=2, has_side_effects=True),
    )(column)


def gather_grid(slab, n_space, n_ens):
    rows = n_space // 2
    me_s = lax.axis_index("space")
    z, half = me_s // 2, me_s % 2
    pieces = [(slab, me_s)]
    for flip in (0, 1):
        for dz in range(1 - flip, rows):
            pairs = []
            for s in range(n_space):
                zs, hs = s // 2, s % 2
                t = ((zs + dz) % rows) * 2 + (hs ^ flip)
                for e in range(n_ens):
                    pairs.append((s * n_ens + e, t * n_ens + (e ^ (2 * flip))))
            got = lax.ppermute(slab, ("space", "ens"), pairs)
            pieces.append((got, ((z - dz) % rows) * 2 + (half ^ flip)))
    thick = slab.shape[0]
    grid = jnp.zeros((n_space * thick,) + slab.shape[1:], slab.dtype)
    for got, source in pieces:
        grid = lax.dynamic_update_slice_in_dim(grid, got, source * thick, axis=0)
    return grid


def grid_kernel(
    slab_ref, log_ref, mine_ref, other_ref, whole_ref,
    send_sems, recv_sems, local_sem, pair_sems, part_sems, part_local,
):
    thick = slab_ref.shape[0]
    rows = mine_ref.shape[0] // thick // 2
    me_s = lax.axis_index("space")
    me_e = lax.axis_index("ens")
    z, half = me_s // 2, me_s % 2
    across_x = me_e + 2 - 4 * ((me_e // 2) % 2)
    partner = me_e + 1 - 2 * (me_e % 2)
    mesh_id = pl.DeviceIdType.MESH
    patterns = [(0, dz) for dz in range(1, rows)] + [(1, dz) for dz in range(rows)]

    def place(flip, dz, sign):
        s = ((z + sign * dz + rows) % rows) * 2 + (half + flip) % 2
        return s, (across_x if flip else me_e)

    barrier = pltpu.get_barrier_semaphore()
    friends = [place(0, dz, 1) for dz in range(1, rows)] + [place(1, dz, 1) for dz in range(rows)]
    crosswise = [(zz * 2 + 1 - half, me_e) for zz in range(rows)]
    for s, e in friends + crosswise + [(me_s, partner)]:
        pl.semaphore_signal(barrier, 1, device_id=(s, e), device_id_type=mesh_id)
    pl.semaphore_wait(barrier, len(friends) + len(crosswise) + 1)

    def particle(t, landing):
        return pltpu.make_async_remote_copy(
            src_ref=log_ref.at[t],
            dst_ref=whole_ref.at[pl.ds(landing * thick, thick)],
            send_sem=part_sems.at[0, t],
            recv_sem=part_sems.at[1, landing],
            device_id=(t, me_e),
            device_id_type=mesh_id,
        )

    own_part = pltpu.make_async_copy(
        log_ref.at[me_s], whole_ref.at[pl.ds(me_s * thick, thick)], part_local
    )
    for t in range(2 * rows):
        @pl.when(me_s != t)
        def _():
            particle(t, me_s).start()
    own_part.start()

    def push(k, flip, dz, sign):
        s, e = place(flip, dz, sign)
        where = me_s if sign > 0 else s
        return pltpu.make_async_remote_copy(
            src_ref=slab_ref,
            dst_ref=mine_ref.at[pl.ds(where * thick, thick)],
            send_sem=send_sems.at[k],
            recv_sem=recv_sems.at[k],
            device_id=(s, e),
            device_id_type=mesh_id,
        )

    def hand(slab_index, source):
        return pltpu.make_async_remote_copy(
            src_ref=source,
            dst_ref=other_ref.at[pl.ds(slab_index * thick, thick)],
            send_sem=pair_sems.at[0, slab_index],
            recv_sem=pair_sems.at[1, slab_index],
            device_id=(me_s, partner),
            device_id_type=mesh_id,
        )

    keep = pltpu.make_async_copy(slab_ref, mine_ref.at[pl.ds(me_s * thick, thick)], local_sem)
    for k, (flip, dz) in enumerate(patterns):
        push(k, flip, dz, 1).start()
    keep.start()
    hand(me_s, slab_ref).start()
    keep.wait()
    for k, (flip, dz) in enumerate(patterns):
        push(k, flip, dz, 1).wait_send()
        push(k, flip, dz, -1).wait_recv()
        landed, _ = place(flip, dz, -1)
        hand(landed, mine_ref.at[pl.ds(landed * thick, thick)]).start()
    for slab_index in range(2 * rows):
        hand(slab_index, mine_ref.at[pl.ds(slab_index * thick, thick)]).wait_send()
        hand(slab_index, mine_ref.at[pl.ds(slab_index * thick, thick)]).wait_recv()
    own_part.wait()
    for t in range(2 * rows):
        @pl.when(me_s != t)
        def _():
            particle(t, me_s).wait_send()
            particle(t, t).wait_recv()


def gather_grids(slab, log_perm, n_space):
    thick, depth, across = slab.shape
    anywhere = pl.BlockSpec(memory_space=pl.ANY)
    grid = jax.ShapeDtypeStruct((n_space * thick, depth, across), jnp.float32)
    return pl.pallas_call(
        grid_kernel,
        out_shape=(grid, grid, grid),
        in_specs=[anywhere, anywhere],
        out_specs=(anywhere, anywhere, anywhere),
        scratch_shapes=[
            pltpu.SemaphoreType.DMA((n_space - 1,)),
            pltpu.SemaphoreType.DMA((n_space - 1,)),
            pltpu.SemaphoreType.DMA,
            pltpu.SemaphoreType.DMA((2, n_space)),
            pltpu.SemaphoreType.DMA((2, n_space)),
            pltpu.SemaphoreType.DMA,
        ],
        compiler_params=pltpu.CompilerParams(collective_id=5, has_side_effects=True),
    )(slab, log_perm)


def shards(
    log_perm,
    storage,
    head_init,
    well_cells,
    well_rates,
    obs_cells,
    obs_values,
    noise_var,
    step_size,
    perturb,
):
    members, planes, depth, across = log_perm.shape
    n_space = lax.axis_size("space")
    n_ens = lax.axis_size("ens")
    cell_count = planes * depth * across
    total_members = members * n_ens
    grid_planes = planes * n_space

    core = lax.axis_index("ens") % 2
    mine, other, whole_log = gather_grids(
        jnp.where(core == 0, storage, head_init), log_perm, n_space
    )
    whole_storage = jnp.where(core == 0, mine, other)
    whole_head = jnp.where(core == 0, other, mine)
    source = (
        jnp.zeros((grid_planes * depth * across,), jnp.float32)
        .at[well_cells]
        .add(well_rates)
        .reshape(grid_planes, depth, across)
    )
    forcing = whole_storage * whole_head + source
    slab_rows = planes * depth
    by_rows = log_perm.reshape(members, slab_rows, across)
    field, band = forward_pallas(
        whole_log, whole_storage, whole_head, forcing, by_rows, n_ens
    )
    picked = field.reshape(-1)[obs_cells]
    head_field = lax.all_to_all(field[None], "space", 1, 0, tiled=True)

    obs_count = picked.shape[0]
    own_perturb = lax.dynamic_index_in_dim(perturb, lax.axis_index("space"), 0, keepdims=False)
    row = jnp.zeros((1, 8, 128), jnp.float32)
    row = row.at[0, 0, :obs_count].set(picked).at[0, 0, obs_count : 2 * obs_count].set(own_perturb)
    rows = gather_rows(row, total_members)
    every_obs = rows[:, 0, :obs_count]
    every_perturb = rows[:, 0, obs_count : 2 * obs_count]
    mean_obs = jnp.mean(every_obs, axis=0)
    spread = every_obs - mean_obs
    covariance = jnp.dot(spread.T, spread, precision=HIGHEST) / (total_members - 1)
    system = covariance + jnp.diag(noise_var / step_size[0])
    factor_lower = jnp.linalg.cholesky(system)
    gain_rows = solve_pair(factor_lower, obs_values[None, :] + every_perturb - every_obs)
    mixing = jnp.dot(gain_rows, spread.T, precision=HIGHEST)

    change = jnp.einsum("jk,kry->jry", mixing, band, precision=HIGHEST)
    new_band = band + change / (total_members - 1)
    updated = send_back(new_band, slab_rows)
    updated = updated.reshape(log_perm.shape)
    return (head_field, updated)


def solution(mesh):
    return jax.shard_map(
        shards,
        mesh=mesh,
        in_specs=(
            P("ens", "space", None, None),
            P("space", None, None),
            P("space", None, None),
            P(),
            P(),
            P(),
            P(),
            P(),
            P(),
            P("ens", None),
        ),
        out_specs=(P("ens", "space", None, None), P("ens", "space", None, None)),
        check_vma=False,
    )
```

```python
import jax
from jax.experimental import pallas as pl
from jax.experimental.pallas import tpu as pltpu
import jax.numpy as jnp
from jax import lax
from jax.sharding import PartitionSpec as P

SWEEPS = 3


OMEGA = 0.8
HIGHEST = lax.Precision.HIGHEST
DIRECTIONS = [
    (a, b, c) for a in (-1, 0, 1) for b in (-1, 0, 1) for c in (-1, 0, 1) if (a, b, c) != (0, 0, 0)
]


def shifted(padded, a, b, c, planes, depth, across):
    return padded[..., 1 + a : 1 + a + planes, 1 + b : 1 + b + depth, 1 + c : 1 + c + across]


def solve_pair(factor, residual):
    first = lax.linalg.triangular_solve(factor, residual.T, left_side=True, lower=True)
    second = lax.linalg.triangular_solve(
        factor, first, left_side=True, lower=True, transpose_a=True
    )
    return second.T


HALF = [(a, b, c) for a, b, c in DIRECTIONS if (a, b, c) > (0, 0, 0)]


def shift_plane(x, b, c):
    depth, across = x.shape
    valid = None
    if b != 0:
        x = pltpu.roll(x, (-b) % depth, 0)
        rows = lax.broadcasted_iota(jnp.int32, x.shape, 0) + b
        valid = (rows >= 0) & (rows < depth)
    if c != 0:
        x = pltpu.roll(x, (-c) % across, 1)
        cols = lax.broadcasted_iota(jnp.int32, x.shape, 1) + c
        ok = (cols >= 0) & (cols < across)
        valid = ok if valid is None else valid & ok
    if valid is None:
        return x
    return jnp.where(valid, x, 0.0)


def roll_plane(x, b, c):
    depth, across = x.shape
    if b != 0:
        x = pltpu.roll(x, (-b) % depth, 0)
    if c != 0:
        x = pltpu.roll(x, (-c) % across, 1)
    return x


def forward_kernel(
    log_ref, sto_ref, init_ref, forc_ref, rows_ref, out_ref, band_ref,
    perm, trans, diag, head_a, head_b, band_send, band_recv, local_sem,
):
    planes, depth, across = log_ref.shape
    members, slab_rows, _ = rows_ref.shape
    groups = band_ref.shape[0] // members
    rows = slab_rows // groups
    me_s = lax.axis_index("space")
    me_e = lax.axis_index("ens")
    mesh_id = pl.DeviceIdType.MESH
    barrier = pltpu.get_barrier_semaphore()
    for e in range(groups):
        @pl.when(me_e != e)
        def _():
            pl.semaphore_signal(barrier, 1, device_id=(me_s, e), device_id_type=mesh_id)

    def band_copy(e, source_e):
        return pltpu.make_async_remote_copy(
            src_ref=rows_ref.at[:, pl.ds(e * rows, rows)],
            dst_ref=band_ref.at[pl.ds(source_e * members, members)],
            send_sem=band_send.at[e],
            recv_sem=band_recv.at[source_e],
            device_id=(me_s, e),
            device_id_type=mesh_id,
        )

    keep_band = pltpu.make_async_copy(
        rows_ref.at[:, pl.ds(me_e * rows, rows)],
        band_ref.at[pl.ds(me_e * members, members)],
        local_sem,
    )
    zero = jnp.zeros((depth, across), jnp.float32)
    for buf in (perm, head_a, head_b):
        buf[0] = zero
        buf[planes + 1] = zero

    def fill(p, carry):
        perm[p + 1] = jnp.exp(log_ref[p])
        head_a[p + 1] = init_ref[p]
        return carry

    lax.fori_loop(0, planes, fill, 0)

    def transmissibility(p, carry):
        own = perm[p + 1]
        for k, (a, b, c) in enumerate(HALF):
            factor = 2.0 ** (1 - abs(a) - abs(b) - abs(c))
            other = shift_plane(perm[p + 1 + a], b, c)
            trans[k, p] = factor * 2.0 * own * other / (own + other)
        return carry

    lax.fori_loop(0, planes, transmissibility, 0)

    pl.semaphore_wait(barrier, groups - 1)
    for e in range(groups):
        @pl.when(me_e != e)
        def _():
            band_copy(e, me_e).start()
    keep_band.start()

    def diagonal(p, carry):
        total = sto_ref[p]
        for k, (a, b, c) in enumerate(HALF):
            back = p - a
            inside = (back >= 0) & (back < planes)
            behind = roll_plane(trans[k, jnp.clip(back, 0, planes - 1)], -b, -c)
            total = total + trans[k, p] + jnp.where(inside, behind, 0.0)
        diag[p] = total
        return carry

    lax.fori_loop(0, planes, diagonal, 0)

    def sweep(source, target, padded_target):
        def body(p, carry):
            gathered = None
            for k, (a, b, c) in enumerate(HALF):
                ahead = trans[k, p] * roll_plane(source[p + 1 + a], b, c)
                back = jnp.clip(p - a, 0, planes - 1)
                flow = roll_plane(trans[k, back] * source[p + 1 - a], -b, -c)
                term = ahead + flow
                gathered = term if gathered is None else gathered + term
            value = (1.0 - OMEGA) * source[p + 1] + OMEGA * (forc_ref[p] + gathered) / diag[p]
            if padded_target:
                target[p + 1] = value
            else:
                target[p] = value
            return carry

        lax.fori_loop(0, planes, body, 0)

    sweep(head_a, head_b, True)
    sweep(head_b, head_a, True)
    sweep(head_a, out_ref, False)
    keep_band.wait()
    for e in range(groups):
        @pl.when(me_e != e)
        def _():
            band_copy(e, me_e).wait_send()
            band_copy(e, e).wait_recv()


def forward_pallas(log_row, storage, head_init, forcing, by_rows, groups):
    planes, depth, across = log_row.shape
    members, slab_rows, _ = by_rows.shape
    vmem = pl.BlockSpec(memory_space=pltpu.VMEM)
    anywhere = pl.BlockSpec(memory_space=pl.ANY)
    return pl.pallas_call(
        forward_kernel,
        out_shape=(
            jax.ShapeDtypeStruct((planes, depth, across), jnp.float32),
            jax.ShapeDtypeStruct((members * groups, slab_rows // groups, across), jnp.float32),
        ),
        in_specs=[vmem] * 4 + [anywhere],
        out_specs=(vmem, anywhere),
        scratch_shapes=[
            pltpu.VMEM((planes + 2, depth, across), jnp.float32),
            pltpu.VMEM((len(HALF), planes, depth, across), jnp.float32),
            pltpu.VMEM((planes, depth, across), jnp.float32),
            pltpu.VMEM((planes + 2, depth, across), jnp.float32),
            pltpu.VMEM((planes + 2, depth, across), jnp.float32),
            pltpu.SemaphoreType.DMA((groups,)),
            pltpu.SemaphoreType.DMA((groups,)),
            pltpu.SemaphoreType.DMA,
        ],
        compiler_params=pltpu.CompilerParams(
            vmem_limit_bytes=66 * 1024 * 1024, collective_id=3, has_side_effects=True
        ),
    )(log_row, storage, head_init, forcing, by_rows)


def gather_kernel(row_ref, out_ref, landing, send_sem, recv_sem):
    total = landing.shape[0]
    n_space = lax.axis_size("space")
    me_s = lax.axis_index("space")
    me_e = lax.axis_index("ens")
    mine = me_e * n_space + me_s
    mesh_id = pl.DeviceIdType.MESH

    barrier = pltpu.get_barrier_semaphore()

    def greet(i, carry):
        @pl.when(i != mine)
        def _():
            pl.semaphore_signal(
                barrier, 1, device_id=(i % n_space, i // n_space), device_id_type=mesh_id
            )

        return carry

    lax.fori_loop(0, total, greet, 0)
    pl.semaphore_wait(barrier, total - 1)

    def send(i, carry):
        @pl.when(i != mine)
        def _():
            pltpu.make_async_remote_copy(
                src_ref=row_ref,
                dst_ref=landing.at[pl.ds(mine, 1)],
                send_sem=send_sem,
                recv_sem=recv_sem,
                device_id=(i % n_space, i // n_space),
                device_id_type=mesh_id,
            ).start()

        return carry

    lax.fori_loop(0, total, send, 0)
    landing[pl.ds(mine, 1)] = row_ref[...]
    partner = (mine + 1) % total
    everything = pltpu.make_async_remote_copy(
        src_ref=landing.at[pl.ds(0, total - 1)],
        dst_ref=landing.at[pl.ds(1, total - 1)],
        send_sem=send_sem,
        recv_sem=recv_sem,
        device_id=(partner % n_space, partner // n_space),
        device_id_type=mesh_id,
    )
    everything.wait_send()
    everything.wait_recv()
    out_ref[...] = landing[...]


def gather_rows(row, total):
    vmem = pl.BlockSpec(memory_space=pltpu.VMEM)
    return pl.pallas_call(
        gather_kernel,
        out_shape=jax.ShapeDtypeStruct((total,) + row.shape[1:], jnp.float32),
        in_specs=[vmem],
        out_specs=vmem,
        scratch_shapes=[
            pltpu.VMEM((total,) + row.shape[1:], jnp.float32),
            pltpu.SemaphoreType.DMA,
            pltpu.SemaphoreType.DMA,
        ],
        compiler_params=pltpu.CompilerParams(collective_id=1, has_side_effects=True),
    )(row)


def return_kernel(column_ref, update_out, upd_send, upd_recv, local_sem):
    groups = update_out.shape[1] // column_ref.shape[1]
    rows = column_ref.shape[1]
    members = update_out.shape[0]
    me_s = lax.axis_index("space")
    me_e = lax.axis_index("ens")
    mesh_id = pl.DeviceIdType.MESH

    barrier = pltpu.get_barrier_semaphore()
    for e in range(groups):
        @pl.when(me_e != e)
        def _():
            pl.semaphore_signal(barrier, 1, device_id=(me_s, e), device_id_type=mesh_id)
    pl.semaphore_wait(barrier, groups - 1)

    def upd_copy(e, source_e):
        return pltpu.make_async_remote_copy(
            src_ref=column_ref.at[pl.ds(e * members, members)],
            dst_ref=update_out.at[:, pl.ds(source_e * rows, rows)],
            send_sem=upd_send.at[e],
            recv_sem=upd_recv.at[source_e],
            device_id=(me_s, e),
            device_id_type=mesh_id,
        )

    keep_upd = pltpu.make_async_copy(
        column_ref.at[pl.ds(me_e * members, members)],
        update_out.at[:, pl.ds(me_e * rows, rows)],
        local_sem,
    )
    for e in range(groups):
        @pl.when(me_e != e)
        def _():
            upd_copy(e, me_e).start()
    keep_upd.start()
    keep_upd.wait()
    for e in range(groups):
        @pl.when(me_e != e)
        def _():
            upd_copy(e, me_e).wait_send()
            upd_copy(e, e).wait_recv()


def send_back(column, slab_rows):
    total, rows, across = column.shape
    groups = slab_rows // rows
    members = total // groups
    anywhere = pl.BlockSpec(memory_space=pl.ANY)
    return pl.pallas_call(
        return_kernel,
        out_shape=jax.ShapeDtypeStruct((members, slab_rows, across), jnp.float32),
        in_specs=[anywhere],
        out_specs=anywhere,
        scratch_shapes=[
            pltpu.SemaphoreType.DMA((groups,)),
            pltpu.SemaphoreType.DMA((groups,)),
            pltpu.SemaphoreType.DMA,
        ],
        compiler_params=pltpu.CompilerParams(collective_id=2, has_side_effects=True),
    )(column)


def gather_grid(slab, n_space, n_ens):
    rows = n_space // 2
    me_s = lax.axis_index("space")
    z, half = me_s // 2, me_s % 2
    pieces = [(slab, me_s)]
    for flip in (0, 1):
        for dz in range(1 - flip, rows):
            pairs = []
            for s in range(n_space):
                zs, hs = s // 2, s % 2
                t = ((zs + dz) % rows) * 2 + (hs ^ flip)
                for e in range(n_ens):
                    pairs.append((s * n_ens + e, t * n_ens + (e ^ (2 * flip))))
            got = lax.ppermute(slab, ("space", "ens"), pairs)
            pieces.append((got, ((z - dz) % rows) * 2 + (half ^ flip)))
    thick = slab.shape[0]
    grid = jnp.zeros((n_space * thick,) + slab.shape[1:], slab.dtype)
    for got, source in pieces:
        grid = lax.dynamic_update_slice_in_dim(grid, got, source * thick, axis=0)
    return grid


def grid_kernel(slab_ref, mine_ref, other_ref, send_sems, recv_sems, local_sem, pair_sems):
    thick = slab_ref.shape[0]
    rows = mine_ref.shape[0] // thick // 2
    me_s = lax.axis_index("space")
    me_e = lax.axis_index("ens")
    z, half = me_s // 2, me_s % 2
    across_x = me_e + 2 - 4 * ((me_e // 2) % 2)
    partner = me_e + 1 - 2 * (me_e % 2)
    mesh_id = pl.DeviceIdType.MESH
    patterns = [(0, dz) for dz in range(1, rows)] + [(1, dz) for dz in range(rows)]

    def place(flip, dz, sign):
        s = ((z + sign * dz + rows) % rows) * 2 + (half + flip) % 2
        return s, (across_x if flip else me_e)

    barrier = pltpu.get_barrier_semaphore()
    friends = [place(0, dz, 1) for dz in range(1, rows)] + [place(1, dz, 1) for dz in range(rows)]
    for s, e in friends + [(me_s, partner)]:
        pl.semaphore_signal(barrier, 1, device_id=(s, e), device_id_type=mesh_id)
    pl.semaphore_wait(barrier, len(friends) + 1)

    def push(k, flip, dz, sign):
        s, e = place(flip, dz, sign)
        where = me_s if sign > 0 else s
        return pltpu.make_async_remote_copy(
            src_ref=slab_ref,
            dst_ref=mine_ref.at[pl.ds(where * thick, thick)],
            send_sem=send_sems.at[k],
            recv_sem=recv_sems.at[k],
            device_id=(s, e),
            device_id_type=mesh_id,
        )

    def hand(slab_index, source):
        return pltpu.make_async_remote_copy(
            src_ref=source,
            dst_ref=other_ref.at[pl.ds(slab_index * thick, thick)],
            send_sem=pair_sems.at[0, slab_index],
            recv_sem=pair_sems.at[1, slab_index],
            device_id=(me_s, partner),
            device_id_type=mesh_id,
        )

    keep = pltpu.make_async_copy(slab_ref, mine_ref.at[pl.ds(me_s * thick, thick)], local_sem)
    for k, (flip, dz) in enumerate(patterns):
        push(k, flip, dz, 1).start()
    keep.start()
    hand(me_s, slab_ref).start()
    keep.wait()
    for k, (flip, dz) in enumerate(patterns):
        push(k, flip, dz, 1).wait_send()
        push(k, flip, dz, -1).wait_recv()
        landed, _ = place(flip, dz, -1)
        hand(landed, mine_ref.at[pl.ds(landed * thick, thick)]).start()
    for slab_index in range(2 * rows):
        hand(slab_index, mine_ref.at[pl.ds(slab_index * thick, thick)]).wait_send()
        hand(slab_index, mine_ref.at[pl.ds(slab_index * thick, thick)]).wait_recv()


def gather_grids(slab, n_space):
    thick, depth, across = slab.shape
    anywhere = pl.BlockSpec(memory_space=pl.ANY)
    grid = jax.ShapeDtypeStruct((n_space * thick, depth, across), jnp.float32)
    return pl.pallas_call(
        grid_kernel,
        out_shape=(grid, grid),
        in_specs=[anywhere],
        out_specs=(anywhere, anywhere),
        scratch_shapes=[
            pltpu.SemaphoreType.DMA((n_space - 1,)),
            pltpu.SemaphoreType.DMA((n_space - 1,)),
            pltpu.SemaphoreType.DMA,
            pltpu.SemaphoreType.DMA((2, n_space)),
        ],
        compiler_params=pltpu.CompilerParams(collective_id=5, has_side_effects=True),
    )(slab)


def shards(
    log_perm,
    storage,
    head_init,
    well_cells,
    well_rates,
    obs_cells,
    obs_values,
    noise_var,
    step_size,
    perturb,
):
    members, planes, depth, across = log_perm.shape
    n_space = lax.axis_size("space")
    n_ens = lax.axis_size("ens")
    cell_count = planes * depth * across
    total_members = members * n_ens
    grid_planes = planes * n_space

    whole_log = lax.all_to_all(log_perm, "space", 0, 1, tiled=True)
    core = lax.axis_index("ens") % 2
    mine, other = gather_grids(jnp.where(core == 0, storage, head_init), n_space)
    whole_storage = jnp.where(core == 0, mine, other)
    whole_head = jnp.where(core == 0, other, mine)
    source = (
        jnp.zeros((grid_planes * depth * across,), jnp.float32)
        .at[well_cells]
        .add(well_rates)
        .reshape(grid_planes, depth, across)
    )
    forcing = whole_storage * whole_head + source
    slab_rows = planes * depth
    by_rows = log_perm.reshape(members, slab_rows, across)
    field, band = forward_pallas(
        whole_log[0], whole_storage, whole_head, forcing, by_rows, n_ens
    )
    picked = field.reshape(-1)[obs_cells]
    head_field = lax.all_to_all(field[None], "space", 1, 0, tiled=True)

    obs_count = picked.shape[0]
    own_perturb = lax.dynamic_index_in_dim(perturb, lax.axis_index("space"), 0, keepdims=False)
    row = jnp.zeros((1, 8, 128), jnp.float32)
    row = row.at[0, 0, :obs_count].set(picked).at[0, 0, obs_count : 2 * obs_count].set(own_perturb)
    rows = gather_rows(row, total_members)
    every_obs = rows[:, 0, :obs_count]
    every_perturb = rows[:, 0, obs_count : 2 * obs_count]
    mean_obs = jnp.mean(every_obs, axis=0)
    spread = every_obs - mean_obs
    covariance = jnp.dot(spread.T, spread, precision=HIGHEST) / (total_members - 1)
    system = covariance + jnp.diag(noise_var / step_size[0])
    factor_lower = jnp.linalg.cholesky(system)
    gain_rows = solve_pair(factor_lower, obs_values[None, :] + every_perturb - every_obs)
    mixing = jnp.dot(gain_rows, spread.T, precision=HIGHEST)

    step = jnp.eye(total_members, dtype=jnp.float32) + mixing / (total_members - 1)
    new_band = jnp.einsum("jk,kry->jry", step, band, precision=HIGHEST)
    updated = send_back(new_band, slab_rows)
    updated = updated.reshape(log_perm.shape)
    return (head_field, updated)


def solution(mesh):
    return jax.shard_map(
        shards,
        mesh=mesh,
        in_specs=(
            P("ens", "space", None, None),
            P("space", None, None),
            P("space", None, None),
            P(),
            P(),
            P(),
            P(),
            P(),
            P(),
            P("ens", None),
        ),
        out_specs=(P("ens", "space", None, None), P("ens", "space", None, None)),
        check_vma=False,
    )
```

```python
import jax
from jax.experimental import pallas as pl
from jax.experimental.pallas import tpu as pltpu
import jax.numpy as jnp
from jax import lax
from jax.sharding import PartitionSpec as P

SWEEPS = 3


OMEGA = 0.8
HIGHEST = lax.Precision.HIGHEST
DIRECTIONS = [
    (a, b, c) for a in (-1, 0, 1) for b in (-1, 0, 1) for c in (-1, 0, 1) if (a, b, c) != (0, 0, 0)
]


def shifted(padded, a, b, c, planes, depth, across):
    return padded[..., 1 + a : 1 + a + planes, 1 + b : 1 + b + depth, 1 + c : 1 + c + across]


def solve_pair(factor, residual):
    first = lax.linalg.triangular_solve(factor, residual.T, left_side=True, lower=True)
    second = lax.linalg.triangular_solve(
        factor, first, left_side=True, lower=True, transpose_a=True
    )
    return second.T


HALF = [(a, b, c) for a, b, c in DIRECTIONS if (a, b, c) > (0, 0, 0)]


def shift_plane(x, b, c):
    depth, across = x.shape
    valid = None
    if b != 0:
        x = pltpu.roll(x, (-b) % depth, 0)
        rows = lax.broadcasted_iota(jnp.int32, x.shape, 0) + b
        valid = (rows >= 0) & (rows < depth)
    if c != 0:
        x = pltpu.roll(x, (-c) % across, 1)
        cols = lax.broadcasted_iota(jnp.int32, x.shape, 1) + c
        ok = (cols >= 0) & (cols < across)
        valid = ok if valid is None else valid & ok
    if valid is None:
        return x
    return jnp.where(valid, x, 0.0)


def roll_plane(x, b, c):
    depth, across = x.shape
    if b != 0:
        x = pltpu.roll(x, (-b) % depth, 0)
    if c != 0:
        x = pltpu.roll(x, (-c) % across, 1)
    return x


def forward_kernel(
    log_ref, mine_ref, other_ref, src_ref, rows_ref, out_ref, band_ref,
    perm, trans, diag, head_a, head_b, band_send, band_recv, local_sem, forc_ref,
):
    planes, depth, across = log_ref.shape
    members, slab_rows, _ = rows_ref.shape
    groups = band_ref.shape[0] // members
    rows = slab_rows // groups
    me_s = lax.axis_index("space")
    me_e = lax.axis_index("ens")
    mesh_id = pl.DeviceIdType.MESH
    barrier = pltpu.get_barrier_semaphore()
    for e in range(groups):
        @pl.when(me_e != e)
        def _():
            pl.semaphore_signal(barrier, 1, device_id=(me_s, e), device_id_type=mesh_id)

    def band_copy(e, source_e):
        return pltpu.make_async_remote_copy(
            src_ref=rows_ref.at[:, pl.ds(e * rows, rows)],
            dst_ref=band_ref.at[pl.ds(source_e * members, members)],
            send_sem=band_send.at[e],
            recv_sem=band_recv.at[source_e],
            device_id=(me_s, e),
            device_id_type=mesh_id,
        )

    keep_band = pltpu.make_async_copy(
        rows_ref.at[:, pl.ds(me_e * rows, rows)],
        band_ref.at[pl.ds(me_e * members, members)],
        local_sem,
    )
    zero = jnp.zeros((depth, across), jnp.float32)
    for buf in (perm, head_a, head_b):
        buf[0] = zero
        buf[planes + 1] = zero

    first_core = lax.axis_index("ens") % 2 == 0

    def fill(p, carry):
        perm[p + 1] = jnp.exp(log_ref[p])
        storage = jnp.where(first_core, mine_ref[p], other_ref[p])
        start = jnp.where(first_core, other_ref[p], mine_ref[p])
        head_a[p + 1] = start
        forc_ref[p] = storage * start + src_ref[p]
        return carry

    lax.fori_loop(0, planes, fill, 0)

    def transmissibility(p, carry):
        own = perm[p + 1]
        for k, (a, b, c) in enumerate(HALF):
            factor = 2.0 ** (1 - abs(a) - abs(b) - abs(c))
            other = shift_plane(perm[p + 1 + a], b, c)
            trans[k, p] = factor * 2.0 * own * other / (own + other)
        return carry

    lax.fori_loop(0, planes, transmissibility, 0)

    pl.semaphore_wait(barrier, groups - 1)
    for e in range(groups):
        @pl.when(me_e != e)
        def _():
            band_copy(e, me_e).start()
    keep_band.start()

    def diagonal(p, carry):
        total = jnp.where(first_core, mine_ref[p], other_ref[p])
        for k, (a, b, c) in enumerate(HALF):
            back = p - a
            inside = (back >= 0) & (back < planes)
            behind = roll_plane(trans[k, jnp.clip(back, 0, planes - 1)], -b, -c)
            total = total + trans[k, p] + jnp.where(inside, behind, 0.0)
        diag[p] = total
        return carry

    lax.fori_loop(0, planes, diagonal, 0)

    def sweep(source, target, padded_target):
        def body(p, carry):
            gathered = None
            for k, (a, b, c) in enumerate(HALF):
                ahead = trans[k, p] * roll_plane(source[p + 1 + a], b, c)
                back = jnp.clip(p - a, 0, planes - 1)
                flow = roll_plane(trans[k, back] * source[p + 1 - a], -b, -c)
                term = ahead + flow
                gathered = term if gathered is None else gathered + term
            value = (1.0 - OMEGA) * source[p + 1] + OMEGA * (forc_ref[p] + gathered) / diag[p]
            if padded_target:
                target[p + 1] = value
            else:
                target[p] = value
            return carry

        lax.fori_loop(0, planes, body, 0)

    sweep(head_a, head_b, True)
    sweep(head_b, head_a, True)
    sweep(head_a, out_ref, False)
    keep_band.wait()
    for e in range(groups):
        @pl.when(me_e != e)
        def _():
            band_copy(e, me_e).wait_send()
            band_copy(e, e).wait_recv()


def forward_pallas(log_row, mine, other, source, by_rows, groups):
    planes, depth, across = log_row.shape
    members, slab_rows, _ = by_rows.shape
    vmem = pl.BlockSpec(memory_space=pltpu.VMEM)
    anywhere = pl.BlockSpec(memory_space=pl.ANY)
    return pl.pallas_call(
        forward_kernel,
        out_shape=(
            jax.ShapeDtypeStruct((planes, depth, across), jnp.float32),
            jax.ShapeDtypeStruct((members * groups, slab_rows // groups, across), jnp.float32),
        ),
        in_specs=[vmem] * 4 + [anywhere],
        out_specs=(vmem, anywhere),
        scratch_shapes=[
            pltpu.VMEM((planes + 2, depth, across), jnp.float32),
            pltpu.VMEM((len(HALF), planes, depth, across), jnp.float32),
            pltpu.VMEM((planes, depth, across), jnp.float32),
            pltpu.VMEM((planes + 2, depth, across), jnp.float32),
            pltpu.VMEM((planes + 2, depth, across), jnp.float32),
            pltpu.SemaphoreType.DMA((groups,)),
            pltpu.SemaphoreType.DMA((groups,)),
            pltpu.SemaphoreType.DMA,
            pltpu.VMEM((planes, depth, across), jnp.float32),
        ],
        compiler_params=pltpu.CompilerParams(
            vmem_limit_bytes=66 * 1024 * 1024, collective_id=3, has_side_effects=True
        ),
    )(log_row, mine, other, source, by_rows)


def gather_kernel(row_ref, out_ref, landing, send_sem, recv_sem):
    total = landing.shape[0]
    n_space = lax.axis_size("space")
    me_s = lax.axis_index("space")
    me_e = lax.axis_index("ens")
    mine = me_e * n_space + me_s
    mesh_id = pl.DeviceIdType.MESH

    barrier = pltpu.get_barrier_semaphore()

    def greet(i, carry):
        @pl.when(i != mine)
        def _():
            pl.semaphore_signal(
                barrier, 1, device_id=(i % n_space, i // n_space), device_id_type=mesh_id
            )

        return carry

    lax.fori_loop(0, total, greet, 0)
    pl.semaphore_wait(barrier, total - 1)

    def send(i, carry):
        @pl.when(i != mine)
        def _():
            pltpu.make_async_remote_copy(
                src_ref=row_ref,
                dst_ref=landing.at[pl.ds(mine, 1)],
                send_sem=send_sem,
                recv_sem=recv_sem,
                device_id=(i % n_space, i // n_space),
                device_id_type=mesh_id,
            ).start()

        return carry

    lax.fori_loop(0, total, send, 0)
    landing[pl.ds(mine, 1)] = row_ref[...]
    partner = (mine + 1) % total
    everything = pltpu.make_async_remote_copy(
        src_ref=landing.at[pl.ds(0, total - 1)],
        dst_ref=landing.at[pl.ds(1, total - 1)],
        send_sem=send_sem,
        recv_sem=recv_sem,
        device_id=(partner % n_space, partner // n_space),
        device_id_type=mesh_id,
    )
    everything.wait_send()
    everything.wait_recv()
    out_ref[...] = landing[...]


def gather_rows(row, total):
    vmem = pl.BlockSpec(memory_space=pltpu.VMEM)
    return pl.pallas_call(
        gather_kernel,
        out_shape=jax.ShapeDtypeStruct((total,) + row.shape[1:], jnp.float32),
        in_specs=[vmem],
        out_specs=vmem,
        scratch_shapes=[
            pltpu.VMEM((total,) + row.shape[1:], jnp.float32),
            pltpu.SemaphoreType.DMA,
            pltpu.SemaphoreType.DMA,
        ],
        compiler_params=pltpu.CompilerParams(collective_id=1, has_side_effects=True),
    )(row)


def return_kernel(column_ref, update_out, upd_send, upd_recv, local_sem):
    groups = update_out.shape[1] // column_ref.shape[1]
    rows = column_ref.shape[1]
    members = update_out.shape[0]
    me_s = lax.axis_index("space")
    me_e = lax.axis_index("ens")
    mesh_id = pl.DeviceIdType.MESH

    barrier = pltpu.get_barrier_semaphore()
    for e in range(groups):
        @pl.when(me_e != e)
        def _():
            pl.semaphore_signal(barrier, 1, device_id=(me_s, e), device_id_type=mesh_id)
    pl.semaphore_wait(barrier, groups - 1)

    def upd_copy(e, source_e):
        return pltpu.make_async_remote_copy(
            src_ref=column_ref.at[pl.ds(e * members, members)],
            dst_ref=update_out.at[:, pl.ds(source_e * rows, rows)],
            send_sem=upd_send.at[e],
            recv_sem=upd_recv.at[source_e],
            device_id=(me_s, e),
            device_id_type=mesh_id,
        )

    keep_upd = pltpu.make_async_copy(
        column_ref.at[pl.ds(me_e * members, members)],
        update_out.at[:, pl.ds(me_e * rows, rows)],
        local_sem,
    )
    for e in range(groups):
        @pl.when(me_e != e)
        def _():
            upd_copy(e, me_e).start()
    keep_upd.start()
    keep_upd.wait()
    for e in range(groups):
        @pl.when(me_e != e)
        def _():
            upd_copy(e, me_e).wait_send()
            upd_copy(e, e).wait_recv()


def send_back(column, slab_rows):
    total, rows, across = column.shape
    groups = slab_rows // rows
    members = total // groups
    anywhere = pl.BlockSpec(memory_space=pl.ANY)
    return pl.pallas_call(
        return_kernel,
        out_shape=jax.ShapeDtypeStruct((members, slab_rows, across), jnp.float32),
        in_specs=[anywhere],
        out_specs=anywhere,
        scratch_shapes=[
            pltpu.SemaphoreType.DMA((groups,)),
            pltpu.SemaphoreType.DMA((groups,)),
            pltpu.SemaphoreType.DMA,
        ],
        compiler_params=pltpu.CompilerParams(collective_id=2, has_side_effects=True),
    )(column)


def gather_grid(slab, n_space, n_ens):
    rows = n_space // 2
    me_s = lax.axis_index("space")
    z, half = me_s // 2, me_s % 2
    pieces = [(slab, me_s)]
    for flip in (0, 1):
        for dz in range(1 - flip, rows):
            pairs = []
            for s in range(n_space):
                zs, hs = s // 2, s % 2
                t = ((zs + dz) % rows) * 2 + (hs ^ flip)
                for e in range(n_ens):
                    pairs.append((s * n_ens + e, t * n_ens + (e ^ (2 * flip))))
            got = lax.ppermute(slab, ("space", "ens"), pairs)
            pieces.append((got, ((z - dz) % rows) * 2 + (half ^ flip)))
    thick = slab.shape[0]
    grid = jnp.zeros((n_space * thick,) + slab.shape[1:], slab.dtype)
    for got, source in pieces:
        grid = lax.dynamic_update_slice_in_dim(grid, got, source * thick, axis=0)
    return grid


def grid_kernel(slab_ref, mine_ref, other_ref, send_sems, recv_sems, local_sem, pair_sems):
    thick = slab_ref.shape[0]
    rows = mine_ref.shape[0] // thick // 2
    me_s = lax.axis_index("space")
    me_e = lax.axis_index("ens")
    z, half = me_s // 2, me_s % 2
    across_x = me_e + 2 - 4 * ((me_e // 2) % 2)
    partner = me_e + 1 - 2 * (me_e % 2)
    mesh_id = pl.DeviceIdType.MESH
    patterns = [(0, dz) for dz in range(1, rows)] + [(1, dz) for dz in range(rows)]

    def place(flip, dz, sign):
        s = ((z + sign * dz + rows) % rows) * 2 + (half + flip) % 2
        return s, (across_x if flip else me_e)

    barrier = pltpu.get_barrier_semaphore()
    friends = [place(0, dz, 1) for dz in range(1, rows)] + [place(1, dz, 1) for dz in range(rows)]
    for s, e in friends + [(me_s, partner)]:
        pl.semaphore_signal(barrier, 1, device_id=(s, e), device_id_type=mesh_id)
    pl.semaphore_wait(barrier, len(friends) + 1)

    def push(k, flip, dz, sign):
        s, e = place(flip, dz, sign)
        where = me_s if sign > 0 else s
        return pltpu.make_async_remote_copy(
            src_ref=slab_ref,
            dst_ref=mine_ref.at[pl.ds(where * thick, thick)],
            send_sem=send_sems.at[k],
            recv_sem=recv_sems.at[k],
            device_id=(s, e),
            device_id_type=mesh_id,
        )

    def hand(slab_index, source):
        return pltpu.make_async_remote_copy(
            src_ref=source,
            dst_ref=other_ref.at[pl.ds(slab_index * thick, thick)],
            send_sem=pair_sems.at[0, slab_index],
            recv_sem=pair_sems.at[1, slab_index],
            device_id=(me_s, partner),
            device_id_type=mesh_id,
        )

    keep = pltpu.make_async_copy(slab_ref, mine_ref.at[pl.ds(me_s * thick, thick)], local_sem)
    for k, (flip, dz) in enumerate(patterns):
        push(k, flip, dz, 1).start()
    keep.start()
    hand(me_s, slab_ref).start()
    keep.wait()
    for k, (flip, dz) in enumerate(patterns):
        push(k, flip, dz, 1).wait_send()
        push(k, flip, dz, -1).wait_recv()
        landed, _ = place(flip, dz, -1)
        hand(landed, mine_ref.at[pl.ds(landed * thick, thick)]).start()
    for slab_index in range(2 * rows):
        hand(slab_index, mine_ref.at[pl.ds(slab_index * thick, thick)]).wait_send()
        hand(slab_index, mine_ref.at[pl.ds(slab_index * thick, thick)]).wait_recv()


def gather_grids(slab, n_space):
    thick, depth, across = slab.shape
    anywhere = pl.BlockSpec(memory_space=pl.ANY)
    grid = jax.ShapeDtypeStruct((n_space * thick, depth, across), jnp.float32)
    return pl.pallas_call(
        grid_kernel,
        out_shape=(grid, grid),
        in_specs=[anywhere],
        out_specs=(anywhere, anywhere),
        scratch_shapes=[
            pltpu.SemaphoreType.DMA((n_space - 1,)),
            pltpu.SemaphoreType.DMA((n_space - 1,)),
            pltpu.SemaphoreType.DMA,
            pltpu.SemaphoreType.DMA((2, n_space)),
        ],
        compiler_params=pltpu.CompilerParams(collective_id=5, has_side_effects=True),
    )(slab)


def shards(
    log_perm,
    storage,
    head_init,
    well_cells,
    well_rates,
    obs_cells,
    obs_values,
    noise_var,
    step_size,
    perturb,
):
    members, planes, depth, across = log_perm.shape
    n_space = lax.axis_size("space")
    n_ens = lax.axis_size("ens")
    cell_count = planes * depth * across
    total_members = members * n_ens
    grid_planes = planes * n_space

    whole_log = lax.all_to_all(log_perm, "space", 0, 1, tiled=True)
    core = lax.axis_index("ens") % 2
    mine, other = gather_grids(jnp.where(core == 0, storage, head_init), n_space)
    source = (
        jnp.zeros((grid_planes * depth * across,), jnp.float32)
        .at[well_cells]
        .add(well_rates)
        .reshape(grid_planes, depth, across)
    )
    slab_rows = planes * depth
    by_rows = log_perm.reshape(members, slab_rows, across)
    field, band = forward_pallas(
        whole_log[0], mine, other, source, by_rows, n_ens
    )
    picked = field.reshape(-1)[obs_cells]
    head_field = lax.all_to_all(field[None], "space", 1, 0, tiled=True)

    obs_count = picked.shape[0]
    own_perturb = lax.dynamic_index_in_dim(perturb, lax.axis_index("space"), 0, keepdims=False)
    row = jnp.zeros((1, 8, 128), jnp.float32)
    row = row.at[0, 0, :obs_count].set(picked).at[0, 0, obs_count : 2 * obs_count].set(own_perturb)
    rows = gather_rows(row, total_members)
    every_obs = rows[:, 0, :obs_count]
    every_perturb = rows[:, 0, obs_count : 2 * obs_count]
    mean_obs = jnp.mean(every_obs, axis=0)
    spread = every_obs - mean_obs
    covariance = jnp.dot(spread.T, spread, precision=HIGHEST) / (total_members - 1)
    system = covariance + jnp.diag(noise_var / step_size[0])
    factor_lower = jnp.linalg.cholesky(system)
    gain_rows = solve_pair(factor_lower, obs_values[None, :] + every_perturb - every_obs)
    mixing = jnp.dot(gain_rows, spread.T, precision=HIGHEST)

    step = jnp.eye(total_members, dtype=jnp.float32) + mixing / (total_members - 1)
    new_band = jnp.einsum("jk,kry->jry", step, band, precision=HIGHEST)
    updated = send_back(new_band, slab_rows)
    updated = updated.reshape(log_perm.shape)
    return (head_field, updated)


def solution(mesh):
    return jax.shard_map(
        shards,
        mesh=mesh,
        in_specs=(
            P("ens", "space", None, None),
            P("space", None, None),
            P("space", None, None),
            P(),
            P(),
            P(),
            P(),
            P(),
            P(),
            P("ens", None),
        ),
        out_specs=(P("ens", "space", None, None), P("ens", "space", None, None)),
        check_vma=False,
    )
```

```python
import jax
from jax.experimental import pallas as pl
from jax.experimental.pallas import tpu as pltpu
import jax.numpy as jnp
from jax import lax
from jax.sharding import PartitionSpec as P

SWEEPS = 3


OMEGA = 0.8
HIGHEST = lax.Precision.HIGHEST
DIRECTIONS = [
    (a, b, c) for a in (-1, 0, 1) for b in (-1, 0, 1) for c in (-1, 0, 1) if (a, b, c) != (0, 0, 0)
]


def shifted(padded, a, b, c, planes, depth, across):
    return padded[..., 1 + a : 1 + a + planes, 1 + b : 1 + b + depth, 1 + c : 1 + c + across]


def solve_pair(factor, residual):
    first = lax.linalg.triangular_solve(factor, residual.T, left_side=True, lower=True)
    second = lax.linalg.triangular_solve(
        factor, first, left_side=True, lower=True, transpose_a=True
    )
    return second.T


HALF = [(a, b, c) for a, b, c in DIRECTIONS if (a, b, c) > (0, 0, 0)]


def shift_plane(x, b, c):
    depth, across = x.shape
    valid = None
    if b != 0:
        x = pltpu.roll(x, (-b) % depth, 0)
        rows = lax.broadcasted_iota(jnp.int32, x.shape, 0) + b
        valid = (rows >= 0) & (rows < depth)
    if c != 0:
        x = pltpu.roll(x, (-c) % across, 1)
        cols = lax.broadcasted_iota(jnp.int32, x.shape, 1) + c
        ok = (cols >= 0) & (cols < across)
        valid = ok if valid is None else valid & ok
    if valid is None:
        return x
    return jnp.where(valid, x, 0.0)


def roll_plane(x, b, c):
    depth, across = x.shape
    if b != 0:
        x = pltpu.roll(x, (-b) % depth, 0)
    if c != 0:
        x = pltpu.roll(x, (-c) % across, 1)
    return x


def forward_kernel(
    log_ref, mine_ref, other_ref, src_ref, rows_ref, out_ref, band_ref,
    perm, trans, diag, head_a, head_b, band_send, band_recv, local_sem, forc_ref,
):
    planes, depth, across = log_ref.shape
    members, slab_rows, _ = rows_ref.shape
    groups = band_ref.shape[0] // members
    rows = slab_rows // groups
    me_s = lax.axis_index("space")
    me_e = lax.axis_index("ens")
    mesh_id = pl.DeviceIdType.MESH
    barrier = pltpu.get_barrier_semaphore()
    for e in range(groups):
        @pl.when(me_e != e)
        def _():
            pl.semaphore_signal(barrier, 1, device_id=(me_s, e), device_id_type=mesh_id)

    def band_copy(e, source_e):
        return pltpu.make_async_remote_copy(
            src_ref=rows_ref.at[:, pl.ds(e * rows, rows)],
            dst_ref=band_ref.at[pl.ds(source_e * members, members)],
            send_sem=band_send.at[e],
            recv_sem=band_recv.at[source_e],
            device_id=(me_s, e),
            device_id_type=mesh_id,
        )

    keep_band = pltpu.make_async_copy(
        rows_ref.at[:, pl.ds(me_e * rows, rows)],
        band_ref.at[pl.ds(me_e * members, members)],
        local_sem,
    )
    zero = jnp.zeros((depth, across), jnp.float32)
    for buf in (perm, head_a, head_b):
        buf[0] = zero
        buf[planes + 1] = zero

    first_core = lax.axis_index("ens") % 2 == 0

    def fill(p, carry):
        perm[p + 1] = jnp.exp(log_ref[p])
        storage = jnp.where(first_core, mine_ref[p], other_ref[p])
        start = jnp.where(first_core, other_ref[p], mine_ref[p])
        head_a[p + 1] = start
        forc_ref[p] = storage * start + src_ref[p]
        return carry

    lax.fori_loop(0, planes, fill, 0)

    def transmissibility(p, carry):
        own = perm[p + 1]
        for k, (a, b, c) in enumerate(HALF):
            factor = 2.0 ** (1 - abs(a) - abs(b) - abs(c))
            other = shift_plane(perm[p + 1 + a], b, c)
            trans[k, p] = factor * 2.0 * own * other / (own + other)
        return carry

    lax.fori_loop(0, planes, transmissibility, 0)

    pl.semaphore_wait(barrier, groups - 1)
    for e in range(groups):
        @pl.when(me_e != e)
        def _():
            band_copy(e, me_e).start()
    keep_band.start()

    def diagonal(p, carry):
        total = jnp.where(first_core, mine_ref[p], other_ref[p])
        for k, (a, b, c) in enumerate(HALF):
            back = p - a
            inside = (back >= 0) & (back < planes)
            behind = roll_plane(trans[k, jnp.clip(back, 0, planes - 1)], -b, -c)
            total = total + trans[k, p] + jnp.where(inside, behind, 0.0)
        diag[p] = total
        return carry

    lax.fori_loop(0, planes, diagonal, 0)

    def sweep(source, target, padded_target):
        def body(p, carry):
            gathered = None
            for k, (a, b, c) in enumerate(HALF):
                ahead = trans[k, p] * roll_plane(source[p + 1 + a], b, c)
                back = jnp.clip(p - a, 0, planes - 1)
                flow = roll_plane(trans[k, back] * source[p + 1 - a], -b, -c)
                term = ahead + flow
                gathered = term if gathered is None else gathered + term
            value = (1.0 - OMEGA) * source[p + 1] + OMEGA * (forc_ref[p] + gathered) / diag[p]
            if padded_target:
                target[p + 1] = value
            else:
                target[p] = value
            return carry

        lax.fori_loop(0, planes, body, 0)

    sweep(head_a, head_b, True)
    sweep(head_b, head_a, True)
    sweep(head_a, out_ref, False)
    keep_band.wait()
    for e in range(groups):
        @pl.when(me_e != e)
        def _():
            band_copy(e, me_e).wait_send()
            band_copy(e, e).wait_recv()


def forward_pallas(log_row, mine, other, source, by_rows, groups):
    planes, depth, across = log_row.shape
    members, slab_rows, _ = by_rows.shape
    vmem = pl.BlockSpec(memory_space=pltpu.VMEM)
    anywhere = pl.BlockSpec(memory_space=pl.ANY)
    return pl.pallas_call(
        forward_kernel,
        out_shape=(
            jax.ShapeDtypeStruct((planes, depth, across), jnp.float32),
            jax.ShapeDtypeStruct((members * groups, slab_rows // groups, across), jnp.float32),
        ),
        in_specs=[vmem] * 4 + [anywhere],
        out_specs=(vmem, anywhere),
        scratch_shapes=[
            pltpu.VMEM((planes + 2, depth, across), jnp.float32),
            pltpu.VMEM((len(HALF), planes, depth, across), jnp.float32),
            pltpu.VMEM((planes, depth, across), jnp.float32),
            pltpu.VMEM((planes + 2, depth, across), jnp.float32),
            pltpu.VMEM((planes + 2, depth, across), jnp.float32),
            pltpu.SemaphoreType.DMA((groups,)),
            pltpu.SemaphoreType.DMA((groups,)),
            pltpu.SemaphoreType.DMA,
            pltpu.VMEM((planes, depth, across), jnp.float32),
        ],
        compiler_params=pltpu.CompilerParams(
            vmem_limit_bytes=66 * 1024 * 1024, collective_id=3, has_side_effects=True
        ),
    )(log_row, mine, other, source, by_rows)


def gather_kernel(row_ref, out_ref, landing, send_sem, recv_sem):
    total = landing.shape[0]
    n_space = lax.axis_size("space")
    me_s = lax.axis_index("space")
    me_e = lax.axis_index("ens")
    mine = me_e * n_space + me_s
    mesh_id = pl.DeviceIdType.MESH

    barrier = pltpu.get_barrier_semaphore()

    def greet(i, carry):
        @pl.when(i != mine)
        def _():
            pl.semaphore_signal(
                barrier, 1, device_id=(i % n_space, i // n_space), device_id_type=mesh_id
            )

        return carry

    lax.fori_loop(0, total, greet, 0)
    pl.semaphore_wait(barrier, total - 1)

    def send(i, carry):
        @pl.when(i != mine)
        def _():
            pltpu.make_async_remote_copy(
                src_ref=row_ref,
                dst_ref=landing.at[pl.ds(mine, 1)],
                send_sem=send_sem,
                recv_sem=recv_sem,
                device_id=(i % n_space, i // n_space),
                device_id_type=mesh_id,
            ).start()

        return carry

    lax.fori_loop(0, total, send, 0)
    landing[pl.ds(mine, 1)] = row_ref[...]
    partner = (mine + 1) % total
    everything = pltpu.make_async_remote_copy(
        src_ref=landing.at[pl.ds(0, total - 1)],
        dst_ref=landing.at[pl.ds(1, total - 1)],
        send_sem=send_sem,
        recv_sem=recv_sem,
        device_id=(partner % n_space, partner // n_space),
        device_id_type=mesh_id,
    )
    everything.wait_send()
    everything.wait_recv()
    out_ref[...] = landing[...]


def gather_rows(row, total):
    vmem = pl.BlockSpec(memory_space=pltpu.VMEM)
    return pl.pallas_call(
        gather_kernel,
        out_shape=jax.ShapeDtypeStruct((total,) + row.shape[1:], jnp.float32),
        in_specs=[vmem],
        out_specs=vmem,
        scratch_shapes=[
            pltpu.VMEM((total,) + row.shape[1:], jnp.float32),
            pltpu.SemaphoreType.DMA,
            pltpu.SemaphoreType.DMA,
        ],
        compiler_params=pltpu.CompilerParams(collective_id=1, has_side_effects=True),
    )(row)


def return_kernel(column_ref, update_out, upd_send, upd_recv, local_sem):
    groups = update_out.shape[1] // column_ref.shape[1]
    rows = column_ref.shape[1]
    members = update_out.shape[0]
    me_s = lax.axis_index("space")
    me_e = lax.axis_index("ens")
    mesh_id = pl.DeviceIdType.MESH

    barrier = pltpu.get_barrier_semaphore()
    for e in range(groups):
        @pl.when(me_e != e)
        def _():
            pl.semaphore_signal(barrier, 1, device_id=(me_s, e), device_id_type=mesh_id)
    pl.semaphore_wait(barrier, groups - 1)

    def upd_copy(e, source_e):
        return pltpu.make_async_remote_copy(
            src_ref=column_ref.at[pl.ds(e * members, members)],
            dst_ref=update_out.at[:, pl.ds(source_e * rows, rows)],
            send_sem=upd_send.at[e],
            recv_sem=upd_recv.at[source_e],
            device_id=(me_s, e),
            device_id_type=mesh_id,
        )

    keep_upd = pltpu.make_async_copy(
        column_ref.at[pl.ds(me_e * members, members)],
        update_out.at[:, pl.ds(me_e * rows, rows)],
        local_sem,
    )
    for e in range(groups):
        @pl.when(me_e != e)
        def _():
            upd_copy(e, me_e).start()
    keep_upd.start()
    keep_upd.wait()
    for e in range(groups):
        @pl.when(me_e != e)
        def _():
            upd_copy(e, me_e).wait_send()
            upd_copy(e, e).wait_recv()


def send_back(column, slab_rows):
    total, rows, across = column.shape
    groups = slab_rows // rows
    members = total // groups
    anywhere = pl.BlockSpec(memory_space=pl.ANY)
    return pl.pallas_call(
        return_kernel,
        out_shape=jax.ShapeDtypeStruct((members, slab_rows, across), jnp.float32),
        in_specs=[anywhere],
        out_specs=anywhere,
        scratch_shapes=[
            pltpu.SemaphoreType.DMA((groups,)),
            pltpu.SemaphoreType.DMA((groups,)),
            pltpu.SemaphoreType.DMA,
        ],
        compiler_params=pltpu.CompilerParams(collective_id=2, has_side_effects=True),
    )(column)


def gather_grid(slab, n_space, n_ens):
    rows = n_space // 2
    me_s = lax.axis_index("space")
    z, half = me_s // 2, me_s % 2
    pieces = [(slab, me_s)]
    for flip in (0, 1):
        for dz in range(1 - flip, rows):
            pairs = []
            for s in range(n_space):
                zs, hs = s // 2, s % 2
                t = ((zs + dz) % rows) * 2 + (hs ^ flip)
                for e in range(n_ens):
                    pairs.append((s * n_ens + e, t * n_ens + (e ^ (2 * flip))))
            got = lax.ppermute(slab, ("space", "ens"), pairs)
            pieces.append((got, ((z - dz) % rows) * 2 + (half ^ flip)))
    thick = slab.shape[0]
    grid = jnp.zeros((n_space * thick,) + slab.shape[1:], slab.dtype)
    for got, source in pieces:
        grid = lax.dynamic_update_slice_in_dim(grid, got, source * thick, axis=0)
    return grid


def grid_kernel(slab_ref, mine_ref, other_ref, send_sems, recv_sems, local_sem, pair_sems):
    thick = slab_ref.shape[0]
    rows = mine_ref.shape[0] // thick // 2
    me_s = lax.axis_index("space")
    me_e = lax.axis_index("ens")
    z, half = me_s // 2, me_s % 2
    across_x = me_e + 2 - 4 * ((me_e // 2) % 2)
    partner = me_e + 1 - 2 * (me_e % 2)
    mesh_id = pl.DeviceIdType.MESH
    patterns = [(0, dz) for dz in range(1, rows)] + [(1, dz) for dz in range(rows)]

    def place(flip, dz, sign):
        s = ((z + sign * dz + rows) % rows) * 2 + (half + flip) % 2
        return s, (across_x if flip else me_e)

    barrier = pltpu.get_barrier_semaphore()
    friends = [place(0, dz, 1) for dz in range(1, rows)] + [place(1, dz, 1) for dz in range(rows)]
    for s, e in friends + [(me_s, partner)]:
        pl.semaphore_signal(barrier, 1, device_id=(s, e), device_id_type=mesh_id)
    pl.semaphore_wait(barrier, len(friends) + 1)

    def push(k, flip, dz, sign):
        s, e = place(flip, dz, sign)
        where = me_s if sign > 0 else s
        return pltpu.make_async_remote_copy(
            src_ref=slab_ref,
            dst_ref=mine_ref.at[pl.ds(where * thick, thick)],
            send_sem=send_sems.at[k],
            recv_sem=recv_sems.at[k],
            device_id=(s, e),
            device_id_type=mesh_id,
        )

    def hand(slab_index, source):
        return pltpu.make_async_remote_copy(
            src_ref=source,
            dst_ref=other_ref.at[pl.ds(slab_index * thick, thick)],
            send_sem=pair_sems.at[0, slab_index],
            recv_sem=pair_sems.at[1, slab_index],
            device_id=(me_s, partner),
            device_id_type=mesh_id,
        )

    keep = pltpu.make_async_copy(slab_ref, mine_ref.at[pl.ds(me_s * thick, thick)], local_sem)
    for k, (flip, dz) in enumerate(patterns):
        push(k, flip, dz, 1).start()
    keep.start()
    hand(me_s, slab_ref).start()
    keep.wait()
    for k, (flip, dz) in enumerate(patterns):
        push(k, flip, dz, 1).wait_send()
        push(k, flip, dz, -1).wait_recv()
        landed, _ = place(flip, dz, -1)
        hand(landed, mine_ref.at[pl.ds(landed * thick, thick)]).start()
    for slab_index in range(2 * rows):
        hand(slab_index, mine_ref.at[pl.ds(slab_index * thick, thick)]).wait_send()
        hand(slab_index, mine_ref.at[pl.ds(slab_index * thick, thick)]).wait_recv()


def gather_grids(slab, n_space):
    thick, depth, across = slab.shape
    anywhere = pl.BlockSpec(memory_space=pl.ANY)
    grid = jax.ShapeDtypeStruct((n_space * thick, depth, across), jnp.float32)
    return pl.pallas_call(
        grid_kernel,
        out_shape=(grid, grid),
        in_specs=[anywhere],
        out_specs=(anywhere, anywhere),
        scratch_shapes=[
            pltpu.SemaphoreType.DMA((n_space - 1,)),
            pltpu.SemaphoreType.DMA((n_space - 1,)),
            pltpu.SemaphoreType.DMA,
            pltpu.SemaphoreType.DMA((2, n_space)),
        ],
        compiler_params=pltpu.CompilerParams(collective_id=5, has_side_effects=True),
    )(slab)


def shards(
    log_perm,
    storage,
    head_init,
    well_cells,
    well_rates,
    obs_cells,
    obs_values,
    noise_var,
    step_size,
    perturb,
):
    members, planes, depth, across = log_perm.shape
    n_space = lax.axis_size("space")
    n_ens = lax.axis_size("ens")
    cell_count = planes * depth * across
    total_members = members * n_ens
    grid_planes = planes * n_space

    whole_log = lax.all_to_all(log_perm, "space", 0, 1, tiled=True)
    core = lax.axis_index("ens") % 2
    mine, other = gather_grids(jnp.where(core == 0, storage, head_init), n_space)
    plane_cells = depth * across
    source = (
        jnp.zeros((grid_planes, depth, across), jnp.float32)
        .at[well_cells // plane_cells, (well_cells % plane_cells) // across, well_cells % across]
        .add(well_rates)
    )
    slab_rows = planes * depth
    by_rows = log_perm.reshape(members, slab_rows, across)
    field, band = forward_pallas(
        whole_log[0], mine, other, source, by_rows, n_ens
    )
    picked = field.reshape(-1)[obs_cells]
    head_field = lax.all_to_all(field[None], "space", 1, 0, tiled=True)

    obs_count = picked.shape[0]
    own_perturb = lax.dynamic_index_in_dim(perturb, lax.axis_index("space"), 0, keepdims=False)
    row = jnp.zeros((1, 8, 128), jnp.float32)
    row = row.at[0, 0, :obs_count].set(picked).at[0, 0, obs_count : 2 * obs_count].set(own_perturb)
    rows = gather_rows(row, total_members)
    every_obs = rows[:, 0, :obs_count]
    every_perturb = rows[:, 0, obs_count : 2 * obs_count]
    mean_obs = jnp.mean(every_obs, axis=0)
    spread = every_obs - mean_obs
    covariance = jnp.dot(spread.T, spread, precision=HIGHEST) / (total_members - 1)
    system = covariance + jnp.diag(noise_var / step_size[0])
    factor_lower = jnp.linalg.cholesky(system)
    gain_rows = solve_pair(factor_lower, obs_values[None, :] + every_perturb - every_obs)
    mixing = jnp.dot(gain_rows, spread.T, precision=HIGHEST)

    step = jnp.eye(total_members, dtype=jnp.float32) + mixing / (total_members - 1)
    new_band = jnp.einsum("jk,kry->jry", step, band, precision=HIGHEST)
    updated = send_back(new_band, slab_rows)
    updated = updated.reshape(log_perm.shape)
    return (head_field, updated)


def solution(mesh):
    return jax.shard_map(
        shards,
        mesh=mesh,
        in_specs=(
            P("ens", "space", None, None),
            P("space", None, None),
            P("space", None, None),
            P(),
            P(),
            P(),
            P(),
            P(),
            P(),
            P("ens", None),
        ),
        out_specs=(P("ens", "space", None, None), P("ens", "space", None, None)),
        check_vma=False,
    )
```
